32 devices in a mesh: fsdp: 2 (over x), ctx: 16 (over z, y, core).
Axes of the slice: x: 2, y: 2, z: 4, core: 2. Of those that a mesh axis runs over, the one named last changes fastest.
Arguments:
- inputs: bfloat16 [2, 2048, 960], P('fsdp', 'ctx'), may hold values from -6 to 6
- grad_output: bfloat16 [2, 2048, 960], P('fsdp', 'ctx'), may hold values from -6 to 6
- w_query: bfloat16 [960, 960], P('fsdp', 'ctx'), may hold values from -50 to 50
- w_key: bfloat16 [960, 320], P('fsdp', 'ctx'), may hold values from -50 to 50
- w_value: bfloat16 [960, 320], P('fsdp', 'ctx'), may hold values from -0.1875 to 0.1875
- w_out: bfloat16 [960, 960], P('fsdp', 'ctx'), may hold values from -0.75 to 0.75
- w_gate: bfloat16 [960, 2560], P('fsdp', 'ctx'), may hold values from -0.1875 to 0.1875
- w_up: bfloat16 [960, 2560], P('fsdp', 'ctx'), may hold values from -0.1875 to 0.1875
- w_down: bfloat16 [2560, 960], P('fsdp', 'ctx'), may hold values from -0.125 to 0.125
- gain_attn: bfloat16 [960], P('ctx'), may hold values from 0.5 to 1.5
- gain_mlp: bfloat16 [960], P('ctx'), may hold values from 0.5 to 1.5
Outputs:
- output: bfloat16 [2, 2048, 960], P('fsdp', 'ctx')
- grad_input: bfloat16 [2, 2048, 960], P('fsdp', 'ctx')
- grad_w_query: float32 [960, 960], P('fsdp', 'ctx')
- grad_w_key: float32 [960, 320], P('fsdp', 'ctx')
- grad_w_value: float32 [960, 320], P('fsdp', 'ctx')
- grad_w_out: float32 [960, 960], P('fsdp', 'ctx')
- grad_w_gate: float32 [960, 2560], P('fsdp', 'ctx')
- grad_w_up: float32 [960, 2560], P('fsdp', 'ctx')
- grad_w_down: float32 [2560, 960], P('fsdp', 'ctx')
- grad_gain_attn: float32 [960], P('ctx')
- grad_gain_mlp: float32 [960], P('ctx')
The draws below stay inside these ranges and needn't reach their ends.
All inputs are finite; a program needn't handle non-finite values.
Results may differ from the reference program's by a relative error of at most 0.018.
Values may be sent and summed in bfloat16 or wider, within the bound.
A program may use at most 256 MiB of HBM per device.

```python
import math
import jax
import jax.numpy as jnp
from jax import lax

D = 960
FF = 2560
HEADS = 15
KV_HEADS = 5
HEAD = 64
SEQS = 2
LENGTH = 2048
KEY_BLOCK = 512


def paired_weights(key):
    base_key = jax.random.fold_in(key, 71)
    subkeys = jax.random.split(base_key, 3)
    key_matrix = jax.random.normal(subkeys[0], (D, KV_HEADS * HEAD), jnp.float32) / math.sqrt(D)
    query_matrix = jax.random.normal(subkeys[2], (D, HEADS * HEAD), jnp.float32) / math.sqrt(D)
    return (query_matrix, key_matrix)


def draw_w_query(key, part):
    query_matrix, key_matrix = paired_weights(key)
    return query_matrix.astype(jnp.bfloat16)


def draw_w_key(key, part):
    query_matrix, key_matrix = paired_weights(key)
    return key_matrix.astype(jnp.bfloat16)


def level_of(own_key, dims, cuts, low, top_value):
    loudness, own = 1.0, jax.random.fold_in(own_key, 6)
    for dim, shards_of in cuts:
        steps = jnp.exp(jax.random.uniform(jax.random.fold_in(own, dim), (shards_of,), jnp.float32, low / len(cuts), top_value / len(cuts)))
        loudness = loudness * jnp.repeat(steps, dims[dim] // shards_of).reshape([-1 if axis == dim else 1 for axis in range(len(dims))])
    return loudness


def bell_draw(rng, shape, width, bound, cuts=(), held_as=jnp.bfloat16):
    result = width * jax.random.normal(rng, shape, jnp.float32)
    if cuts:
        result = result * level_of(rng, shape, cuts, -0.22, 0.18)
    return jnp.clip(result, -bound, bound).astype(held_as)


def setup_inputs(seed: int = 0) -> dict:
    splits = jax.random.split(jax.random.key(seed), 12)
    return {
        "inputs": bell_draw(splits[0], (SEQS, LENGTH, D), 1.0, 6.0, ((0, 2), (1, 16))),
        "grad_output": bell_draw(splits[1], (SEQS, LENGTH, D), 1.0, 6.0, ((0, 2), (1, 16))),
        "w_query": draw_w_query(jax.random.fold_in(splits[11], 71), 0),
        "w_key": draw_w_key(jax.random.fold_in(splits[11], 71), 0),
        "w_value": bell_draw(splits[4], (D, KV_HEADS * HEAD), D ** -0.5, 0.1875, ((0, 2), (1, 16))),
        "w_out": bell_draw(splits[5], (HEADS * HEAD, D), 64 ** -0.5, 0.75, ((0, 2), (1, 16))),
        "w_gate": bell_draw(splits[6], (D, FF), D ** -0.5, 0.1875, ((0, 2), (1, 16))),
        "w_up": bell_draw(splits[7], (D, FF), D ** -0.5, 0.1875, ((0, 2), (1, 16))),
        "w_down": bell_draw(splits[8], (FF, D), FF ** -0.5, 0.125, ((0, 2), (1, 16))),
        "gain_attn": jnp.clip(1.0 + 0.1 * jax.random.normal(splits[9], (D,), jnp.float32), 0.5, 1.5).astype(jnp.bfloat16),
        "gain_mlp": jnp.clip(1.0 + 0.1 * jax.random.normal(splits[10], (D,), jnp.float32), 0.5, 1.5).astype(jnp.bfloat16),
    }


EPSILON = 1e-05
ROPE_THETA = 100000.0

def lowered(tensor):
    return lax.optimization_barrier(tensor.astype(jnp.bfloat16)).astype(jnp.float32)

def tables(positions, head_size):
    half_size = head_size // 2
    frequency = ROPE_THETA ** (-jnp.arange(half_size, dtype=jnp.float32) * 2.0 / head_size)
    angles = positions.astype(jnp.float32)[:, None] * frequency[None, :]
    return (jnp.cos(angles), jnp.sin(angles))

def rotate(values, cosine, sine_table):
    half_size = values.shape[-1] // 2
    first_half = values[..., :half_size]
    second = values[..., half_size:]
    cosine = cosine[:, None, :]
    sine_table = sine_table[:, None, :]
    return jnp.concatenate([first_half * cosine - second * sine_table, second * cosine + first_half * sine_table], axis=-1)

def unrotate(values, cosine, sine_table):
    half_size = values.shape[-1] // 2
    first_half = values[..., :half_size]
    second = values[..., half_size:]
    cosine = cosine[:, None, :]
    sine_table = sine_table[:, None, :]
    return jnp.concatenate([first_half * cosine + second * sine_table, second * cosine - first_half * sine_table], axis=-1)

def normed(row_values, gain_vec):
    scale_rows = lax.rsqrt(lax.optimization_barrier(jnp.mean(row_values * row_values, axis=-1, keepdims=True)) + EPSILON)
    return row_values * scale_rows * gain_vec

def attention_forward(query_rot, key_rows, value_rows):
    block_total = LENGTH // KEY_BLOCK
    key_pos = jnp.arange(LENGTH, dtype=jnp.int32)

    def query_block(block_index):
        row_start = block_index * KEY_BLOCK
        query_rows = lax.dynamic_slice_in_dim(query_rot, row_start, KEY_BLOCK, 0)
        scores = jnp.einsum('qgrd,kgd->grqk', query_rows.astype(jnp.float32), key_rows.astype(jnp.float32)) * 0.125
        allowed = key_pos[None, :] <= (row_start + jnp.arange(KEY_BLOCK, dtype=jnp.int32))[:, None]
        scores = jnp.where(allowed, scores, -jnp.inf)
        new_peak = lax.optimization_barrier(jnp.max(scores, axis=-1))
        logsum = new_peak + jnp.log(lax.optimization_barrier(jnp.sum(jnp.exp(scores - new_peak[..., None]), axis=-1)))
        prob_low = lowered(jnp.exp(scores - logsum[..., None]))
        attended = jnp.einsum('grqk,kgd->qgrd', prob_low, value_rows.astype(jnp.float32)).astype(jnp.bfloat16)
        return (attended, logsum)
    attended, logsum = lax.map(query_block, jnp.arange(block_total, dtype=jnp.int32))
    return (attended.reshape(LENGTH, KV_HEADS, HEADS // KV_HEADS, HEAD), logsum)

def attention_backward(query_rot, key_rows, value_rows, attended, logsum, grad_attended):
    block_total = LENGTH // KEY_BLOCK
    key_pos = jnp.arange(LENGTH, dtype=jnp.int32)

    def query_block(loop_state, block_index):
        grad_keys, grad_values = loop_state
        row_start = block_index * KEY_BLOCK
        query_rows = lax.dynamic_slice_in_dim(query_rot, row_start, KEY_BLOCK, 0).astype(jnp.float32)
        grad_rows = lax.dynamic_slice_in_dim(grad_attended, row_start, KEY_BLOCK, 0).astype(jnp.float32)
        scores = jnp.einsum('qgrd,kgd->grqk', query_rows, key_rows.astype(jnp.float32)) * 0.125
        allowed = key_pos[None, :] <= (row_start + jnp.arange(KEY_BLOCK, dtype=jnp.int32))[:, None]
        scores = jnp.where(allowed, scores, -jnp.inf)
        prob_full = jnp.where(allowed, jnp.exp(scores - logsum[block_index][..., None]), 0.0)
        grad_probs = jnp.einsum('qgrd,kgd->grqk', grad_rows, value_rows.astype(jnp.float32))
        row_delta = lax.optimization_barrier(jnp.sum(prob_full * grad_probs, axis=-1))
        grad_scores = lowered(prob_full * (grad_probs - row_delta[..., None]) * 0.125)
        grad_values = grad_values + jnp.einsum('grqk,qgrd->kgd', lowered(prob_full), grad_rows)
        grad_keys = grad_keys + jnp.einsum('grqk,qgrd->kgd', grad_scores, query_rows)
        grad_query = jnp.einsum('grqk,kgd->qgrd', grad_scores, key_rows.astype(jnp.float32))
        return ((grad_keys, grad_values), grad_query)
    zero_sums = (jnp.zeros((LENGTH, KV_HEADS, HEAD), jnp.float32), jnp.zeros((LENGTH, KV_HEADS, HEAD), jnp.float32))
    (grad_keys, grad_values), grad_query = lax.scan(query_block, zero_sums, jnp.arange(block_total, dtype=jnp.int32))
    return (grad_query.reshape(LENGTH, HEADS, HEAD), grad_keys, grad_values)

def one_sequence(rows_in, grad_rows, weights, gains):
    full_query, full_key, full_value, full_out, full_gate, full_up, full_down = weights
    gain_first, gain_second = gains
    repeat_count = HEADS // KV_HEADS
    cosine, sine_table = tables(jnp.arange(LENGTH, dtype=jnp.int32), HEAD)
    resid1 = rows_in.astype(jnp.float32)
    normal1 = normed(resid1, gain_first).astype(jnp.bfloat16)
    query_raw = jnp.dot(normal1, full_query, preferred_element_type=jnp.float32).reshape(LENGTH, HEADS, HEAD)
    query_rot = rotate(query_raw, cosine, sine_table).astype(jnp.bfloat16)
    key_raw = jnp.dot(normal1, full_key, preferred_element_type=jnp.float32).reshape(LENGTH, KV_HEADS, HEAD)
    key_rows = rotate(key_raw, cosine, sine_table).astype(jnp.bfloat16)
    value_rows = jnp.dot(normal1, full_value, preferred_element_type=jnp.float32).astype(jnp.bfloat16).reshape(LENGTH, KV_HEADS, HEAD)
    query_grouped = query_rot.reshape(LENGTH, KV_HEADS, repeat_count, HEAD)
    attended, logsum = attention_forward(query_grouped, key_rows, value_rows)
    attended_rows = attended.reshape(LENGTH, HEADS * HEAD)
    resid2 = resid1 + jnp.dot(attended_rows, full_out, preferred_element_type=jnp.float32)
    normal2 = normed(resid2, gain_second).astype(jnp.bfloat16)
    gate_act = jnp.dot(normal2, full_gate, preferred_element_type=jnp.float32)
    up_act = jnp.dot(normal2, full_up, preferred_element_type=jnp.float32)
    hidden = (jax.nn.silu(gate_act) * up_act).astype(jnp.bfloat16)
    output = (resid2 + jnp.dot(hidden, full_down, preferred_element_type=jnp.float32)).astype(jnp.bfloat16)
    grad_hidden = jnp.dot(grad_rows, full_down.T, preferred_element_type=jnp.float32)
    term_down = jnp.dot(hidden.T, grad_rows, preferred_element_type=jnp.float32)
    gate_sigma = jax.nn.sigmoid(gate_act)
    grad_up = (grad_hidden * gate_act * gate_sigma).astype(jnp.bfloat16)
    grad_gate = (grad_hidden * up_act * gate_sigma * (1.0 + gate_act * (1.0 - gate_sigma))).astype(jnp.bfloat16)
    term_gate = jnp.dot(normal2.T, grad_gate, preferred_element_type=jnp.float32)
    term_up = jnp.dot(normal2.T, grad_up, preferred_element_type=jnp.float32)
    grad_norm2 = jnp.dot(grad_gate, full_gate.T, preferred_element_type=jnp.float32) + jnp.dot(grad_up, full_up.T, preferred_element_type=jnp.float32)
    normed_out, pull_second = jax.vjp(normed, resid2, gain_second)
    grad_part2, term_gain2 = pull_second(grad_norm2)
    grad_resid2 = grad_rows.astype(jnp.float32) + grad_part2
    grad_branch = grad_resid2.astype(jnp.bfloat16)
    term_out = jnp.dot(attended_rows.T, grad_branch, preferred_element_type=jnp.float32)
    grad_attended = jnp.dot(grad_branch, full_out.T, preferred_element_type=jnp.float32).astype(jnp.bfloat16)
    grad_grouped = grad_attended.reshape(LENGTH, KV_HEADS, repeat_count, HEAD)
    grad_query_acc, grad_keys_acc, grad_values_acc = attention_backward(query_grouped, key_rows, value_rows, attended, logsum, grad_grouped)
    grad_query = unrotate(grad_query_acc, cosine, sine_table).reshape(LENGTH, HEADS * HEAD).astype(jnp.bfloat16)
    grad_keys = unrotate(grad_keys_acc, cosine, sine_table).reshape(LENGTH, KV_HEADS * HEAD).astype(jnp.bfloat16)
    grad_values = grad_values_acc.reshape(LENGTH, KV_HEADS * HEAD).astype(jnp.bfloat16)
    term_query = jnp.dot(normal1.T, grad_query, preferred_element_type=jnp.float32)
    term_key = jnp.dot(normal1.T, grad_keys, preferred_element_type=jnp.float32)
    term_value = jnp.dot(normal1.T, grad_values, preferred_element_type=jnp.float32)
    grad_norm1 = jnp.dot(grad_query, full_query.T, preferred_element_type=jnp.float32)
    grad_norm1 = grad_norm1 + jnp.dot(grad_keys, full_key.T, preferred_element_type=jnp.float32)
    grad_norm1 = grad_norm1 + jnp.dot(grad_values, full_value.T, preferred_element_type=jnp.float32)
    normed_first, pull_first = jax.vjp(normed, resid1, gain_first)
    grad_part1, term_gain1 = pull_first(grad_norm1)
    grad_input = (grad_resid2 + grad_part1).astype(jnp.bfloat16)
    terms = (term_query, term_key, term_value, term_out, term_gate, term_up, term_down, term_gain1, term_gain2)
    return (output, grad_input, terms)

def reference(inputs, grad_output, w_query, w_key, w_value, w_out, w_gate, w_up, w_down, gain_attn, gain_mlp):
    weights = (w_query, w_key, w_value, w_out, w_gate, w_up, w_down)
    gains = (gain_attn.astype(jnp.float32), gain_mlp.astype(jnp.float32))
    zero_sums = tuple((jnp.zeros(matrix.shape, jnp.float32) for matrix in weights))
    zero_sums = zero_sums + (jnp.zeros((D,), jnp.float32), jnp.zeros((D,), jnp.float32))

    def seq_step(running, seq_pair):
        output, grad_input, terms = one_sequence(seq_pair[0], seq_pair[1], weights, gains)
        return (tuple((left + right for left, right in zip(running, terms))), (output, grad_input))
    totals, (outputs, grads) = lax.scan(seq_step, zero_sums, (inputs, grad_output))
    return (outputs, grads, totals[0], totals[1], totals[2], totals[3], totals[4], totals[5], totals[6], totals[7], totals[8])
```

```python
import functools

import jax
import jax.numpy as jnp
from jax import lax
from jax.experimental import pallas as pl
from jax.experimental.pallas import tpu as pltpu
from jax.sharding import PartitionSpec as P

HEADS = 15
KV_HEADS = 5
HEAD = 64

EPSILON = 1e-05
ROPE_THETA = 100000.0
MESH = pl.DeviceIdType.MESH
VMEM_LIMIT = 60 * 1024 * 1024


def tables(positions, head_size):
    half_size = head_size // 2
    frequency = ROPE_THETA ** (-jnp.arange(half_size, dtype=jnp.float32) * 2.0 / head_size)
    angles = positions.astype(jnp.float32)[:, None] * frequency[None, :]
    return (jnp.cos(angles), jnp.sin(angles))


def rotate(values, cosine, sine_table):
    half_size = values.shape[-1] // 2
    first_half = values[..., :half_size]
    second = values[..., half_size:]
    cosine = cosine[:, None, :]
    sine_table = sine_table[:, None, :]
    return jnp.concatenate(
        [first_half * cosine - second * sine_table, second * cosine + first_half * sine_table],
        axis=-1,
    )


def unrotate(values, cosine, sine_table):
    return rotate(values, cosine, -sine_table)


def normed(row_values, gain_vec):
    scale_rows = lax.rsqrt(jnp.mean(row_values * row_values, axis=-1, keepdims=True) + EPSILON)
    return row_values * scale_rows * gain_vec


class Place:
    def __init__(self, depth, use_x):
        self.depth = depth
        self.use_x = use_x
        self.f = lax.axis_index("fsdp")
        self.ctx = lax.axis_index("ctx")
        self.c = self.ctx % 2
        self.y = (self.ctx // 2) % 2
        self.z = self.ctx // 4
        self.has_up = self.z < depth - 1
        self.has_down = self.z > 0

    def device(self, way):
        if way == "c":
            return (self.f, self.ctx + 1 - 2 * self.c)
        if way == "y":
            return (self.f, self.ctx + 2 - 4 * self.y)
        if way == "x":
            return (1 - self.f, self.ctx)
        return (self.f, self.ctx + (4 if way == "up" else -4))

    def piece(self, route, rel_p, rel_q, z):
        rel = {route[1]: rel_q}
        if route[0] is not None:
            rel[route[0]] = rel_p
        y0 = 1 - self.y if rel.get("y", 0) else self.y
        pid = z * 2 + y0
        if self.use_x:
            x0 = 1 - self.f if rel.get("x", 0) else self.f
            pid = pid + x0 * 2 * self.depth
        return pid

    def barrier(self):
        sem = pltpu.get_barrier_semaphore()
        ways = ["c", "y"] + (["x"] if self.use_x else [])
        for way in ways:
            pl.semaphore_signal(sem, inc=1, device_id=self.device(way), device_id_type=MESH)

        @pl.when(self.has_up)
        def _():
            pl.semaphore_signal(sem, inc=1, device_id=self.device("up"), device_id_type=MESH)

        @pl.when(self.has_down)
        def _():
            pl.semaphore_signal(sem, inc=1, device_id=self.device("down"), device_id_type=MESH)

        peers = len(ways) + self.has_up.astype(jnp.int32) + self.has_down.astype(jnp.int32)
        pl.semaphore_wait(sem, peers)


def both_sides(place, distance, body):
    high = place.z + distance
    low = place.z - distance

    @pl.when((distance >= 0) & (high < place.depth))
    def _():
        body(high, True)

    @pl.when((distance >= 1) & (low >= 0))
    def _():
        body(low, False)


def gather_kernel(depth, use_x, routes, *refs):
    count = len(routes)
    ins, outs = refs[:count], refs[count : 2 * count]
    recv, send_z, send_p, send_q, send_c, local_sem = refs[2 * count :]
    place = Place(depth, use_x)
    place.barrier()

    def copy(k, pid, send_sem, way, src=None):
        slot = pid * 2 + place.c
        return pltpu.make_async_remote_copy(
            src_ref=outs[k].at[slot] if src is None else src,
            dst_ref=outs[k].at[slot],
            send_sem=send_sem,
            recv_sem=recv.at[k, slot],
            device_id=place.device(way),
            device_id_type=MESH,
        )

    def forward_z(k, z0, up, src=None):
        pid = place.piece(routes[k], 0, 0, z0)
        return copy(k, pid, send_z.at[k, 0 if up else 1, z0], "up" if up else "down", src)

    def forward_p(k, z0, src=None):
        return copy(k, place.piece(routes[k], 0, 0, z0), send_p.at[k, z0], routes[k][0], src)

    def forward_q(k, rel_p, z0, src=None):
        pid = place.piece(routes[k], rel_p, 0, z0)
        return copy(k, pid, send_q.at[k, rel_p, z0], routes[k][1], src)

    def forward_c(k, pid, src=None):
        return copy(k, pid, send_c.at[k, pid], "c", src)

    def arrived(k, pid):
        copy(k, pid, send_c.at[k, pid], "c").wait_recv()

    own = []
    for k in range(count):
        pid = place.piece(routes[k], 0, 0, place.z)
        src = ins[k]

        @pl.when(place.has_up)
        def _():
            forward_z(k, place.z, True, src).start()

        @pl.when(place.has_down)
        def _():
            forward_z(k, place.z, False, src).start()

        if routes[k][0] is not None:
            forward_p(k, place.z, src).start()
        forward_q(k, 0, place.z, src).start()
        forward_c(k, pid, src).start()
        mine = pltpu.make_async_copy(src, outs[k].at[pid * 2 + place.c], local_sem.at[k])
        mine.start()
        own.append(mine)

    def step(d, carry):
        def from_z(z0, above):
            for k in range(count):
                pid = place.piece(routes[k], 0, 0, z0)
                arrived(k, pid)
                if above:

                    @pl.when(place.has_down)
                    def _():
                        forward_z(k, z0, False).start()

                else:

                    @pl.when(place.has_up)
                    def _():
                        forward_z(k, z0, True).start()

                if routes[k][0] is not None:
                    forward_p(k, z0).start()
                forward_q(k, 0, z0).start()
                forward_c(k, pid).start()

        def from_p(z0, above):
            for k in range(count):
                if routes[k][0] is not None:
                    pid = place.piece(routes[k], 1, 0, z0)
                    arrived(k, pid)
                    forward_q(k, 1, z0).start()
                    forward_c(k, pid).start()

        def from_q(rel_p, z0, above):
            for k in range(count):
                if routes[k][0] is not None or not rel_p:
                    pid = place.piece(routes[k], rel_p, 1, z0)
                    arrived(k, pid)
                    forward_c(k, pid).start()

        @pl.when((d >= 1) & (d < depth))
        def _():
            both_sides(place, d, from_z)

        both_sides(place, d - 1, from_p)
        both_sides(place, d - 1, functools.partial(from_q, 0))
        both_sides(place, d - 2, functools.partial(from_q, 1))
        return carry

    lax.fori_loop(1, depth + 2, step, 0)

    def finish(z0, carry):
        for k in range(count):

            @pl.when(place.has_up & (z0 <= place.z))
            def _():
                forward_z(k, z0, True).wait_send()

            @pl.when(place.has_down & (z0 >= place.z))
            def _():
                forward_z(k, z0, False).wait_send()

            if routes[k][0] is not None:
                forward_p(k, z0).wait_send()
                forward_q(k, 1, z0).wait_send()
            forward_q(k, 0, z0).wait_send()
        return carry

    lax.fori_loop(0, depth, finish, 0)

    def finish_partner(pid, carry):
        for k in range(count):
            forward_c(k, pid).wait_send()
            slot = pid * 2 + 1 - place.c
            pltpu.make_async_remote_copy(
                src_ref=outs[k].at[slot],
                dst_ref=outs[k].at[slot],
                send_sem=send_c.at[k, pid],
                recv_sem=recv.at[k, slot],
                device_id=place.device("c"),
                device_id_type=MESH,
            ).wait_recv()
        return carry

    lax.fori_loop(0, (4 if use_x else 2) * depth, finish_partner, 0)
    for mine in own:
        mine.wait()


def gather(arrays, routes, use_x, collective_id, name):
    depth = lax.axis_size("ctx") // 4
    pieces = (4 if use_x else 2) * depth
    count = len(arrays)
    dma = pltpu.SemaphoreType.DMA
    return pl.pallas_call(
        functools.partial(gather_kernel, depth, use_x, routes),
        out_shape=[jax.ShapeDtypeStruct((2 * pieces, *a.shape), a.dtype) for a in arrays],
        in_specs=[pl.BlockSpec(memory_space=pltpu.VMEM)] * count,
        out_specs=[pl.BlockSpec(memory_space=pl.ANY)] * count,
        scratch_shapes=[
            dma((count, 2 * pieces)),
            dma((count, 2, depth)),
            dma((count, depth)),
            dma((count, 2, depth)),
            dma((count, pieces)),
            dma((count,)),
        ],
        compiler_params=pltpu.CompilerParams(
            collective_id=collective_id, has_side_effects=True, vmem_limit_bytes=VMEM_LIMIT
        ),
        name=name,
    )(*arrays)


def add_up(dst, sources, rows):
    block = 32 if rows % 32 == 0 else 16

    def body(i, carry):
        span = pl.ds(pl.multiple_of(i * block, block), block)
        total = sources[0][span, :].astype(jnp.float32)
        for source in sources[1:]:
            total = total + source[span, :].astype(jnp.float32)
        dst[span, :] = total.astype(dst.dtype)
        return carry

    lax.fori_loop(0, rows // block, body, 0)


def scatter_kernel(depth, use_x, routes, *refs):
    count = len(routes)
    ins, outs = refs[:count], refs[count : 2 * count]
    own, part, land_q, land_p, land_z = (
        refs[(2 + i) * count : (3 + i) * count] for i in range(5)
    )
    load_sem, c_send, c_recv, q_send, q_recv, p_send, p_recv, z_send, z_recv = refs[7 * count :]
    place = Place(depth, use_x)
    pieces = (4 if use_x else 2) * depth
    rows = [out.shape[0] for out in outs]

    def load(k):
        return pltpu.make_async_copy(ins[k].at[:, place.c], own[k], load_sem.at[k])

    for k in range(count):
        load(k).start()
    place.barrier()

    def remote(src, dst, send_sem, recv_sem, way):
        return pltpu.make_async_remote_copy(
            src_ref=src,
            dst_ref=dst,
            send_sem=send_sem,
            recv_sem=recv_sem,
            device_id=place.device(way),
            device_id_type=MESH,
        )

    def send_c(k, pid):
        return remote(
            ins[k].at[pid, 1 - place.c], part[k].at[pid], c_send.at[k, pid], c_recv.at[k, pid], "c"
        )

    def send_q(k, rel_p, z0):
        pid = place.piece(routes[k], rel_p, 1, z0)
        return remote(
            own[k].at[pid],
            land_q[k].at[rel_p, z0],
            q_send.at[k, rel_p, z0],
            q_recv.at[k, rel_p, z0],
            routes[k][1],
        )

    def send_p(k, z0):
        pid = place.piece(routes[k], 1, 0, z0)
        return remote(
            own[k].at[pid], land_p[k].at[z0], p_send.at[k, z0], p_recv.at[k, z0], routes[k][0]
        )

    def send_z(k, z0, up):
        pid = place.piece(routes[k], 0, 0, z0)
        if up:
            target = z0
        else:
            target = jnp.where(z0 == place.z - 1, depth, z0)
        return remote(
            own[k].at[pid],
            land_z[k].at[target],
            z_send.at[k, z0],
            z_recv.at[k, target],
            "up" if up else "down",
        )

    def wait_z(k, index):
        pltpu.make_async_copy(land_z[k].at[index], land_z[k].at[index], z_recv.at[k, index]).wait()

    def first(s, carry):
        def body(z0, above):
            for k in range(count):
                for rel_q in (1, 0):
                    for rel_p in (1, 0) if routes[k][0] is not None else (0,):
                        send_c(k, place.piece(routes[k], rel_p, rel_q, z0)).start()

        both_sides(place, depth - 1 - s, body)
        return carry

    lax.fori_loop(0, depth, first, 0)
    for k in range(count):
        load(k).wait()

    def step(s, carry):
        def leaf(z0, above):
            for k in range(count):
                for rel_p in (1, 0) if routes[k][0] is not None else (0,):
                    pid = place.piece(routes[k], rel_p, 1, z0)
                    send_c(k, pid).wait_recv()
                    add_up(own[k].at[pid], [own[k].at[pid], part[k].at[pid]], rows[k])
                    send_q(k, rel_p, z0).start()

        def middle(z0, above):
            for k in range(count):
                if routes[k][0] is not None:
                    pid = place.piece(routes[k], 1, 0, z0)
                    send_c(k, pid).wait_recv()
                    send_q(k, 1, z0).wait_recv()
                    add_up(
                        own[k].at[pid],
                        [own[k].at[pid], part[k].at[pid], land_q[k].at[1, z0]],
                        rows[k],
                    )
                    send_p(k, z0).start()

        def sources_of(k, z0):
            pid = place.piece(routes[k], 0, 0, z0)
            send_c(k, pid).wait_recv()
            send_q(k, 0, z0).wait_recv()
            sources = [own[k].at[pid], part[k].at[pid], land_q[k].at[0, z0]]
            if routes[k][0] is not None:
                send_p(k, z0).wait_recv()
                sources.append(land_p[k].at[z0])
            return pid, sources

        def along(z0, above):
            for k in range(count):
                pid, sources = sources_of(k, z0)
                child = place.has_down if above else place.has_up

                @pl.when(child)
                def _():
                    wait_z(k, z0)
                    add_up(own[k].at[pid], sources + [land_z[k].at[z0]], rows[k])

                @pl.when(jnp.logical_not(child))
                def _():
                    add_up(own[k].at[pid], sources, rows[k])

                send_z(k, z0, above).start()

        both_sides(place, depth - 1 - s, leaf)

        @pl.when(s < depth + 1)
        def _():
            both_sides(place, depth - s, middle)

        @pl.when(depth + 1 - s >= 1)
        def _():
            both_sides(place, depth + 1 - s, along)

        @pl.when(s == depth + 1)
        def _():
            for k in range(count):
                _, sources = sources_of(k, place.z)
                add_up(outs[k], sources, rows[k])

                @pl.when(place.has_down)
                def _():
                    wait_z(k, place.z)
                    add_up(outs[k], [outs[k], land_z[k].at[place.z]], rows[k])

                @pl.when(place.has_up)
                def _():
                    wait_z(k, depth)
                    add_up(outs[k], [outs[k], land_z[k].at[depth]], rows[k])

        return carry

    lax.fori_loop(0, depth + 2, step, 0)

    def finish(z0, carry):
        for k in range(count):
            send_q(k, 0, z0).wait_send()
            if routes[k][0] is not None:
                send_q(k, 1, z0).wait_send()
                send_p(k, z0).wait_send()

            @pl.when(z0 > place.z)
            def _():
                send_z(k, z0, True).wait_send()

            @pl.when(z0 < place.z)
            def _():
                send_z(k, z0, False).wait_send()

        return carry

    lax.fori_loop(0, depth, finish, 0)

    def finish_partner(pid, carry):
        for k in range(count):
            send_c(k, pid).wait_send()
        return carry

    lax.fori_loop(0, pieces, finish_partner, 0)


def scatter(arrays, routes, use_x, collective_id, name):
    depth = lax.axis_size("ctx") // 4
    pieces = (4 if use_x else 2) * depth
    count = len(arrays)
    dma = pltpu.SemaphoreType.DMA
    shapes = [a.shape[1:] for a in arrays]
    pairs = [a.reshape(pieces, 2, *s) for a, s in zip(arrays, shapes)]
    bf16 = jnp.bfloat16
    return pl.pallas_call(
        functools.partial(scatter_kernel, depth, use_x, routes),
        out_shape=[jax.ShapeDtypeStruct(s, jnp.float32) for s in shapes],
        in_specs=[pl.BlockSpec(memory_space=pl.ANY)] * count,
        out_specs=[pl.BlockSpec(memory_space=pltpu.VMEM)] * count,
        scratch_shapes=[pltpu.VMEM((pieces, *s), bf16) for s in shapes]
        + [pltpu.VMEM((pieces, *s), bf16) for s in shapes]
        + [pltpu.VMEM((2, depth, *s), bf16) for s in shapes]
        + [pltpu.VMEM((depth, *s), bf16) for s in shapes]
        + [pltpu.VMEM((depth + 1, *s), bf16) for s in shapes]
        + [
            dma((count,)),
            dma((count, pieces)),
            dma((count, pieces)),
            dma((count, 2, depth)),
            dma((count, 2, depth)),
            dma((count, depth)),
            dma((count, depth)),
            dma((count, depth)),
            dma((count, depth + 1)),
        ],
        compiler_params=pltpu.CompilerParams(
            collective_id=collective_id, has_side_effects=True, vmem_limit_bytes=VMEM_LIMIT
        ),
        name=name,
    )(*pairs)


def padded(rows, multiple=16):
    return -(-rows // multiple) * multiple


def pad_rows(rows, total):
    return jnp.pad(rows, ((0, total - rows.shape[0]), (0, 0)))


XY, YX, ONLY_Y = ("x", "y"), ("y", "x"), (None, "y")
WEIGHT_ROUTES = (YX, YX, XY, XY, YX)


def halves(values, split_count):
    return values.reshape(values.shape[0], split_count, values.shape[1] // split_count)


def forward_dot(values, weights):
    split_count = weights.shape[0]
    part = values.shape[1] // split_count
    total = None
    for i in range(split_count):
        term = lax.dot_general(
            values[:, i * part : (i + 1) * part],
            weights[i],
            (((1,), (1,)), ((), ())),
            preferred_element_type=jnp.float32,
        )
        total = term if total is None else total + term
    return total


def backward_dot(grads, weights):
    return jnp.concatenate(
        [
            jnp.dot(grads, weights[i], preferred_element_type=jnp.float32)
            for i in range(weights.shape[0])
        ],
        axis=-1,
    )


def weight_terms(grads, values, split_count):
    part = values.shape[1] // split_count
    return jnp.stack(
        [
            lax.dot_general(
                grads,
                values[:, i * part : (i + 1) * part],
                (((0,), (0,)), ((), ())),
                preferred_element_type=jnp.float32,
            ).astype(jnp.bfloat16)
            for i in range(split_count)
        ]
    )


def local(
    inputs, grad_output, w_query, w_key, w_value, w_out, w_gate, w_up, w_down, gain_attn, gain_mlp
):
    seq_count, block_len, model_width = inputs.shape
    row_count = seq_count * block_len
    split_count = lax.axis_size("fsdp")
    cycle_size = lax.axis_size("ctx")
    cycle_index = lax.axis_index("ctx")
    length = block_len * cycle_size
    key_block = min(512, length)
    groups = KV_HEADS
    head_size = HEAD
    repeat_count = HEADS // KV_HEADS
    kv_width = groups * head_size
    positions = cycle_index * block_len + jnp.arange(block_len, dtype=jnp.int32)
    cosine, sine_table = tables(positions, head_size)
    cosine = jnp.tile(cosine, (seq_count, 1))
    sine_table = jnp.tile(sine_table, (seq_count, 1))
    needed = (cycle_index * block_len + block_len + key_block - 1) // key_block
    wide_q, wide_k, wide_v = w_query.shape[1], w_key.shape[1], w_value.shape[1]
    wide_o, wide_g, wide_u = w_out.shape[1], w_gate.shape[1], w_up.shape[1]
    wide_d = w_down.shape[1]
    pad_q, pad_k, pad_v = padded(wide_q), padded(wide_k + 1), padded(wide_v)
    pad_o, pad_g, pad_u, pad_d = padded(wide_o), padded(wide_g), padded(wide_u), padded(wide_d)
    part_width = w_query.shape[0]
    gain_size = gain_attn.shape[0]

    def open_up(values, wide, start, pad):
        pieces = values.reshape(values.shape[0], cycle_size, -1)
        return pieces[:, :, start : start + wide].reshape(values.shape[0], cycle_size * wide)

    def close_up(values, wide, pad):
        pieces = values.reshape(values.shape[0], cycle_size, wide)
        return jnp.pad(pieces, ((0, 0), (0, 0), (0, pad - wide))).reshape(values.shape[0], -1)

    gain_row = jnp.pad(
        jnp.concatenate([gain_attn, gain_mlp]), (0, part_width - 2 * gain_size)
    )[None, :]
    first_piece = jnp.concatenate(
        [
            pad_rows(w_query.T, pad_q),
            pad_rows(jnp.concatenate([w_key.T, gain_row], axis=0), pad_k),
            pad_rows(w_value.T, pad_v),
        ],
        axis=0,
    )
    first, out_w, gate_w, up_w, down_w = gather(
        [
            first_piece,
            pad_rows(w_out.T, pad_o),
            pad_rows(w_gate.T, pad_g),
            pad_rows(w_up.T, pad_u),
            pad_rows(w_down.T, pad_d),
        ],
        WEIGHT_ROUTES,
        True,
        0,
        "gather_weights",
    )
    gain_rows = first[:cycle_size, pad_q + wide_k, : 2 * gain_size]
    gain_first = gain_rows[:, :gain_size].reshape(-1).astype(jnp.float32)
    gain_second = gain_rows[:, gain_size:].reshape(-1).astype(jnp.float32)
    first, out_w, gate_w, up_w, down_w = (
        w.reshape(split_count, -1, w.shape[-1]) for w in (first, out_w, gate_w, up_w, down_w)
    )

    resid1 = inputs.reshape(row_count, model_width).astype(jnp.float32)
    normal1 = normed(resid1, gain_first).astype(jnp.bfloat16)
    raw = forward_dot(normal1, first)
    query_raw = open_up(raw, wide_q, 0, pad_q).reshape(row_count, HEADS, head_size)
    query_rot = rotate(query_raw, cosine, sine_table).astype(jnp.bfloat16)
    key_raw = open_up(raw, wide_k, pad_q, pad_k).reshape(row_count, groups, head_size)
    key_rows = (
        rotate(key_raw, cosine, sine_table)
        .astype(jnp.bfloat16)
        .reshape(seq_count, block_len, kv_width)
    )
    value_rows = (
        open_up(raw, wide_v, pad_q + pad_k, pad_v)
        .astype(jnp.bfloat16)
        .reshape(seq_count, block_len, kv_width)
    )
    query_grouped = query_rot.reshape(seq_count, block_len, groups, repeat_count, head_size)
    (pair_all,) = gather(
        [jnp.concatenate([key_rows, value_rows], axis=-1).reshape(row_count, 2 * kv_width)],
        (ONLY_Y,),
        False,
        1,
        "gather_pairs",
    )
    pair_all = pair_all.reshape(cycle_size, seq_count, block_len, 2 * kv_width)
    pair_all = jnp.transpose(pair_all, (1, 0, 2, 3)).reshape(seq_count, length, 2 * kv_width)
    keys_all = pair_all[..., :kv_width]
    values_all = pair_all[..., kv_width:]
    key_heads = keys_all.reshape(seq_count, length, groups, head_size)
    value_heads = values_all.reshape(seq_count, length, groups, head_size)
    scores = (
        jnp.einsum(
            "sqgrd,skgd->sgrqk", query_grouped, key_heads, preferred_element_type=jnp.float32
        )
        * 0.125
    )
    allowed = jnp.arange(length, dtype=jnp.int32)[None, :] <= positions[:, None]
    scores = jnp.where(allowed, scores, -jnp.inf)
    new_peak = jnp.max(scores, axis=-1)
    exp_terms = jnp.exp(scores - new_peak[..., None])
    denom_run = jnp.sum(exp_terms, axis=-1)
    running = jnp.einsum(
        "sgrqk,skgd->sgrqd",
        exp_terms.astype(jnp.bfloat16),
        value_heads,
        preferred_element_type=jnp.float32,
    )
    attended_wide = running / denom_run[..., None]
    attended = jnp.transpose(attended_wide, (0, 3, 1, 2, 4)).astype(jnp.bfloat16)
    logsum = new_peak + jnp.log(denom_run)
    attended_rows = attended.reshape(row_count, HEADS * head_size)
    resid2 = resid1 + open_up(forward_dot(attended_rows, out_w), wide_o, 0, pad_o)
    normal2 = normed(resid2, gain_second).astype(jnp.bfloat16)
    gate_act = forward_dot(normal2, gate_w)
    up_act = forward_dot(normal2, up_w)
    gate_sigma = jax.nn.sigmoid(gate_act)
    hidden = (gate_act * gate_sigma * up_act).astype(jnp.bfloat16)
    hidden_flat = open_up(hidden, wide_g, 0, pad_g)
    output = (
        resid2 + open_up(forward_dot(hidden_flat, down_w), wide_d, 0, pad_d)
    ).astype(jnp.bfloat16)

    grad_rows = grad_output.reshape(row_count, model_width)
    grad_rows_padded = close_up(grad_rows, wide_d, pad_d)
    terms_down = weight_terms(grad_rows_padded, hidden_flat, split_count)
    grad_hidden = close_up(backward_dot(grad_rows_padded, down_w), wide_g, pad_g)
    grad_up = (grad_hidden * gate_act * gate_sigma).astype(jnp.bfloat16)
    grad_gate = (grad_hidden * up_act * gate_sigma * (1.0 + gate_act * (1.0 - gate_sigma))).astype(
        jnp.bfloat16
    )
    grad_norm2 = backward_dot(grad_gate, gate_w) + backward_dot(grad_up, up_w)
    normed_out, pull_second = jax.vjp(normed, resid2, gain_second)
    grad_part2, term_gain2 = pull_second(grad_norm2)
    grad_resid2 = grad_rows.astype(jnp.float32) + grad_part2
    grad_branch = close_up(grad_resid2.astype(jnp.bfloat16), wide_o, pad_o)
    terms_out = weight_terms(grad_branch, attended_rows, split_count)
    terms_gate = weight_terms(grad_gate, normal2, split_count)
    terms_up = weight_terms(grad_up, normal2, split_count)
    grad_attended = backward_dot(grad_branch, out_w).astype(jnp.bfloat16)
    grad_grouped = grad_attended.reshape(seq_count, block_len, groups, repeat_count, head_size)
    row_delta = jnp.sum(
        jnp.transpose(grad_grouped, (0, 2, 3, 1, 4)).astype(jnp.float32) * attended_wide, axis=-1
    )

    def retrace(step_index, loop_state):
        grad_query_acc, grad_pair_all = loop_state
        key_start = step_index * key_block
        pair = lax.dynamic_slice_in_dim(pair_all, key_start, key_block, 1)
        key_heads = pair[..., :kv_width].reshape(seq_count, key_block, groups, head_size)
        value_heads = pair[..., kv_width:].reshape(seq_count, key_block, groups, head_size)
        scores = (
            jnp.einsum(
                "sqgrd,skgd->sgrqk", query_grouped, key_heads, preferred_element_type=jnp.float32
            )
            * 0.125
        )
        allowed = (key_start + jnp.arange(key_block, dtype=jnp.int32))[None, :] <= positions[
            :, None
        ]
        prob_full = jnp.where(
            allowed, jnp.exp(jnp.where(allowed, scores, -jnp.inf) - logsum[..., None]), 0.0
        )
        grad_probs = jnp.einsum(
            "sqgrd,skgd->sgrqk", grad_grouped, value_heads, preferred_element_type=jnp.float32
        )
        grad_scores = (prob_full * (grad_probs - row_delta[..., None]) * 0.125).astype(jnp.bfloat16)
        prob_low = prob_full.astype(jnp.bfloat16)
        value_term = jnp.einsum(
            "sgrqk,sqgrd->skgd", prob_low, grad_grouped, preferred_element_type=jnp.float32
        ).reshape(seq_count, key_block, kv_width)
        key_term = jnp.einsum(
            "sgrqk,sqgrd->skgd", grad_scores, query_grouped, preferred_element_type=jnp.float32
        ).reshape(seq_count, key_block, kv_width)
        grad_query_acc = grad_query_acc + jnp.einsum(
            "sgrqk,skgd->sgrqd", grad_scores, key_heads, preferred_element_type=jnp.float32
        )
        pair_term = jnp.concatenate([key_term, value_term], axis=-1).astype(jnp.bfloat16)
        grad_pair_all = lax.dynamic_update_slice_in_dim(grad_pair_all, pair_term, key_start, 1)
        return (grad_query_acc, grad_pair_all)

    back_state = (
        jnp.zeros((seq_count, groups, repeat_count, block_len, head_size), jnp.float32),
        jnp.zeros((seq_count, length, 2 * kv_width), jnp.bfloat16),
    )
    grad_query_acc, grad_pair_all = lax.fori_loop(0, needed, retrace, back_state)
    grad_pair_all = grad_pair_all.reshape(seq_count, cycle_size, block_len, 2 * kv_width)
    grad_pair_all = jnp.transpose(grad_pair_all, (1, 0, 2, 3)).reshape(
        cycle_size, row_count, 2 * kv_width
    )
    (grad_pair_own,) = scatter([grad_pair_all], (ONLY_Y,), False, 2, "scatter_pairs")
    grad_query_rows = jnp.transpose(grad_query_acc, (0, 3, 1, 2, 4)).reshape(
        row_count, HEADS, head_size
    )
    grad_query = (
        unrotate(grad_query_rows, cosine, sine_table)
        .reshape(row_count, HEADS * head_size)
        .astype(jnp.bfloat16)
    )
    grad_keys = (
        unrotate(grad_pair_own[..., :kv_width].reshape(row_count, groups, head_size), cosine, sine_table)
        .reshape(row_count, kv_width)
        .astype(jnp.bfloat16)
    )
    grad_values = grad_pair_own[..., kv_width:].astype(jnp.bfloat16)

    def shaped(values, wide, pad):
        pieces = values.reshape(row_count, cycle_size, wide)
        return jnp.pad(pieces, ((0, 0), (0, 0), (0, pad - wide)))

    grad_raw = jnp.concatenate(
        [
            shaped(grad_query, wide_q, pad_q),
            shaped(grad_keys, wide_k, pad_k),
            shaped(grad_values, wide_v, pad_v),
        ],
        axis=-1,
    ).reshape(row_count, -1)
    grad_norm1 = backward_dot(grad_raw, first)
    normed_first, pull_first = jax.vjp(normed, resid1, gain_first)
    grad_part1, term_gain1 = pull_first(grad_norm1)
    grad_input = (
        (grad_resid2 + grad_part1).astype(jnp.bfloat16).reshape(seq_count, block_len, model_width)
    )
    gain_terms = jnp.concatenate(
        [term_gain1.reshape(cycle_size, -1), term_gain2.reshape(cycle_size, -1)], axis=-1
    ).astype(jnp.bfloat16)
    terms_first = weight_terms(grad_raw, normal1, split_count)
    terms_first = terms_first.reshape(split_count, cycle_size, -1, part_width)
    terms_first = terms_first.at[:, :, pad_q + wide_k, : 2 * gain_size].set(gain_terms[None])

    def pieces_of(terms):
        return terms.reshape(split_count * cycle_size, -1, terms.shape[-1])

    sum_first, sum_out, sum_gate, sum_up, sum_down = scatter(
        [pieces_of(t) for t in (terms_first, terms_out, terms_gate, terms_up, terms_down)],
        WEIGHT_ROUTES,
        True,
        3,
        "scatter_weights",
    )
    start_k, start_v = pad_q, pad_q + pad_k
    gain_sums = sum_first[pad_q + wide_k]
    return (
        output.reshape(seq_count, block_len, model_width),
        grad_input,
        sum_first[:wide_q].T,
        sum_first[start_k : start_k + wide_k].T,
        sum_first[start_v : start_v + wide_v].T,
        sum_out[:wide_o].T,
        sum_gate[:wide_g].T,
        sum_up[:wide_u].T,
        sum_down[:wide_d].T,
        gain_sums[:gain_size],
        gain_sums[gain_size : 2 * gain_size],
    )


def solution(mesh):
    rows, weight, gain = P("fsdp", "ctx", None), P("fsdp", "ctx"), P("ctx")
    return jax.shard_map(
        local,
        mesh=mesh,
        in_specs=(rows, rows) + (weight,) * 7 + (gain, gain),
        out_specs=(rows, rows) + (weight,) * 7 + (gain, gain),
        check_vma=False,
    )
```

```python
import functools

import jax
import jax.numpy as jnp
from jax import lax
from jax.experimental import pallas as pl
from jax.experimental.pallas import tpu as pltpu
from jax.sharding import PartitionSpec as P

HEADS = 15
KV_HEADS = 5
HEAD = 64

EPSILON = 1e-05
ROPE_THETA = 100000.0
MESH = pl.DeviceIdType.MESH
VMEM_LIMIT = 67_000_000


def tables(positions, head_size):
    half_size = head_size // 2
    frequency = ROPE_THETA ** (-jnp.arange(half_size, dtype=jnp.float32) * 2.0 / head_size)
    angles = positions.astype(jnp.float32)[:, None] * frequency[None, :]
    return (jnp.cos(angles), jnp.sin(angles))


def rotate(values, cosine, sine_table):
    half_size = values.shape[-1] // 2
    first_half = values[..., :half_size]
    second = values[..., half_size:]
    cosine = cosine[:, None, :]
    sine_table = sine_table[:, None, :]
    return jnp.concatenate(
        [first_half * cosine - second * sine_table, second * cosine + first_half * sine_table],
        axis=-1,
    )


def unrotate(values, cosine, sine_table):
    return rotate(values, cosine, -sine_table)


def normed(row_values, gain_vec):
    scale_rows = lax.rsqrt(jnp.mean(row_values * row_values, axis=-1, keepdims=True) + EPSILON)
    return row_values * scale_rows * gain_vec


class Place:
    def __init__(self, depth, use_x):
        self.depth = depth
        self.use_x = use_x
        self.f = lax.axis_index("fsdp")
        self.ctx = lax.axis_index("ctx")
        self.c = self.ctx % 2
        self.y = (self.ctx // 2) % 2
        self.z = self.ctx // 4
        self.has_up = self.z < depth - 1
        self.has_down = self.z > 0

    def device(self, way):
        if way == "c":
            return (self.f, self.ctx + 1 - 2 * self.c)
        if way == "y":
            return (self.f, self.ctx + 2 - 4 * self.y)
        if way == "x":
            return (1 - self.f, self.ctx)
        return (self.f, self.ctx + (4 if way == "up" else -4))

    def piece(self, route, rel_p, rel_q, z):
        rel = {route[1]: rel_q}
        if route[0] is not None:
            rel[route[0]] = rel_p
        y0 = 1 - self.y if rel.get("y", 0) else self.y
        pid = z * 2 + y0
        if self.use_x:
            x0 = 1 - self.f if rel.get("x", 0) else self.f
            pid = pid + x0 * 2 * self.depth
        return pid

    def barrier(self):
        sem = pltpu.get_barrier_semaphore()
        ways = ["c", "y"] + (["x"] if self.use_x else [])
        for way in ways:
            pl.semaphore_signal(sem, inc=1, device_id=self.device(way), device_id_type=MESH)

        @pl.when(self.has_up)
        def _():
            pl.semaphore_signal(sem, inc=1, device_id=self.device("up"), device_id_type=MESH)

        @pl.when(self.has_down)
        def _():
            pl.semaphore_signal(sem, inc=1, device_id=self.device("down"), device_id_type=MESH)

        peers = len(ways) + self.has_up.astype(jnp.int32) + self.has_down.astype(jnp.int32)
        pl.semaphore_wait(sem, peers)


def both_sides(place, distance, body):
    high = place.z + distance
    low = place.z - distance

    @pl.when((distance >= 0) & (high < place.depth))
    def _():
        body(high, True)

    @pl.when((distance >= 1) & (low >= 0))
    def _():
        body(low, False)


def gather_kernel(depth, use_x, routes, work, *refs):
    count = len(routes)
    ins, work_ins, refs = refs[:count], refs[count : count + work.ins], refs[count + work.ins :]
    outs, work_outs, refs = refs[:count], refs[count : count + work.outs], refs[count + work.outs :]
    recv, send_z, send_p, send_q, send_c, local_sem = refs
    place = Place(depth, use_x)
    place.barrier()

    def copy(k, pid, send_sem, way, src=None):
        slot = pid * 2 + place.c
        return pltpu.make_async_remote_copy(
            src_ref=outs[k].at[slot] if src is None else src,
            dst_ref=outs[k].at[slot],
            send_sem=send_sem,
            recv_sem=recv.at[k, slot],
            device_id=place.device(way),
            device_id_type=MESH,
        )

    def forward_z(k, z0, up, src=None):
        pid = place.piece(routes[k], 0, 0, z0)
        return copy(k, pid, send_z.at[k, 0 if up else 1, z0], "up" if up else "down", src)

    def forward_p(k, z0, src=None):
        return copy(k, place.piece(routes[k], 0, 0, z0), send_p.at[k, z0], routes[k][0], src)

    def forward_q(k, rel_p, z0, src=None):
        pid = place.piece(routes[k], rel_p, 0, z0)
        return copy(k, pid, send_q.at[k, rel_p, z0], routes[k][1], src)

    def forward_c(k, pid, src=None):
        return copy(k, pid, send_c.at[k, pid], "c", src)

    def arrived(k, pid):
        copy(k, pid, send_c.at[k, pid], "c").wait_recv()

    own = []
    for k in range(count):
        pid = place.piece(routes[k], 0, 0, place.z)
        src = ins[k]

        @pl.when(place.has_up)
        def _():
            forward_z(k, place.z, True, src).start()

        @pl.when(place.has_down)
        def _():
            forward_z(k, place.z, False, src).start()

        if routes[k][0] is not None:
            forward_p(k, place.z, src).start()
        forward_q(k, 0, place.z, src).start()
        forward_c(k, pid, src).start()
        mine = pltpu.make_async_copy(src, outs[k].at[pid * 2 + place.c], local_sem.at[k])
        mine.start()
        own.append(mine)

    def step(d, carry):
        def from_z(z0, above):
            for k in range(count):
                pid = place.piece(routes[k], 0, 0, z0)
                arrived(k, pid)
                if above:

                    @pl.when(place.has_down)
                    def _():
                        forward_z(k, z0, False).start()

                else:

                    @pl.when(place.has_up)
                    def _():
                        forward_z(k, z0, True).start()

                if routes[k][0] is not None:
                    forward_p(k, z0).start()
                forward_q(k, 0, z0).start()
                forward_c(k, pid).start()

        def from_p(z0, above):
            for k in range(count):
                if routes[k][0] is not None:
                    pid = place.piece(routes[k], 1, 0, z0)
                    arrived(k, pid)
                    forward_q(k, 1, z0).start()
                    forward_c(k, pid).start()

        def from_q(rel_p, z0, above):
            for k in range(count):
                if routes[k][0] is not None or not rel_p:
                    pid = place.piece(routes[k], rel_p, 1, z0)
                    arrived(k, pid)
                    forward_c(k, pid).start()

        @pl.when((d >= 1) & (d < depth))
        def _():
            both_sides(place, d, from_z)

        both_sides(place, d - 1, from_p)
        both_sides(place, d - 1, functools.partial(from_q, 0))
        both_sides(place, d - 2, functools.partial(from_q, 1))

        if work.count:

            @pl.when(d - 1 < work.count)
            def _():
                work.body(d - 1, place.ctx, *work_ins, *work_outs)

        return carry

    lax.fori_loop(1, depth + 2, step, 0)
    for item in range(depth + 1, work.count):
        work.body(item, place.ctx, *work_ins, *work_outs)

    def finish(z0, carry):
        for k in range(count):

            @pl.when(place.has_up & (z0 <= place.z))
            def _():
                forward_z(k, z0, True).wait_send()

            @pl.when(place.has_down & (z0 >= place.z))
            def _():
                forward_z(k, z0, False).wait_send()

            if routes[k][0] is not None:
                forward_p(k, z0).wait_send()
                forward_q(k, 1, z0).wait_send()
            forward_q(k, 0, z0).wait_send()
        return carry

    lax.fori_loop(0, depth, finish, 0)

    def finish_partner(pid, carry):
        for k in range(count):
            forward_c(k, pid).wait_send()
            slot = pid * 2 + 1 - place.c
            pltpu.make_async_remote_copy(
                src_ref=outs[k].at[slot],
                dst_ref=outs[k].at[slot],
                send_sem=send_c.at[k, pid],
                recv_sem=recv.at[k, slot],
                device_id=place.device("c"),
                device_id_type=MESH,
            ).wait_recv()
        return carry

    lax.fori_loop(0, (4 if use_x else 2) * depth, finish_partner, 0)
    for mine in own:
        mine.wait()


class Work:
    def __init__(self, count=0, body=None, arrays=(), shapes=()):
        self.count, self.body, self.arrays, self.shapes = count, body, arrays, list(shapes)
        self.ins, self.outs = len(arrays), len(self.shapes)


def gather(arrays, routes, use_x, collective_id, name, work=Work()):
    depth = lax.axis_size("ctx") // 4
    pieces = (4 if use_x else 2) * depth
    count = len(arrays)
    dma = pltpu.SemaphoreType.DMA
    return pl.pallas_call(
        functools.partial(gather_kernel, depth, use_x, routes, work),
        out_shape=[jax.ShapeDtypeStruct((2 * pieces, *a.shape), a.dtype) for a in arrays]
        + work.shapes,
        in_specs=[pl.BlockSpec(memory_space=pltpu.VMEM)] * (count + work.ins),
        out_specs=[pl.BlockSpec(memory_space=pl.ANY)] * count
        + [pl.BlockSpec(memory_space=pltpu.VMEM)] * work.outs,
        scratch_shapes=[
            dma((count, 2 * pieces)),
            dma((count, 2, depth)),
            dma((count, depth)),
            dma((count, 2, depth)),
            dma((count, pieces)),
            dma((count,)),
        ],
        compiler_params=pltpu.CompilerParams(
            collective_id=collective_id, has_side_effects=True, vmem_limit_bytes=VMEM_LIMIT
        ),
        name=name,
    )(*arrays, *work.arrays)


def add_up(dst, sources, rows):
    block = 32 if rows % 32 == 0 else 16

    def body(i, carry):
        span = pl.ds(pl.multiple_of(i * block, block), block)
        total = sources[0][span, :].astype(jnp.float32)
        for source in sources[1:]:
            total = total + source[span, :].astype(jnp.float32)
        dst[span, :] = total.astype(dst.dtype)
        return carry

    lax.fori_loop(0, rows // block, body, 0)


def scatter_kernel(depth, use_x, routes, work, *refs):
    count = len(routes)
    ins, work_ins, refs = refs[:count], refs[count : count + work.ins], refs[count + work.ins :]
    outs, work_outs, refs = refs[:count], refs[count : count + work.outs], refs[count + work.outs :]
    own, part, land_q, land_p, land_z = (refs[i * count : (1 + i) * count] for i in range(5))
    load_sem, c_send, c_recv, q_send, q_recv, p_send, p_recv, z_send, z_recv = refs[5 * count :]
    place = Place(depth, use_x)
    pieces = (4 if use_x else 2) * depth
    rows = [out.shape[0] for out in outs]

    def load(k):
        return pltpu.make_async_copy(ins[k].at[:, place.c], own[k], load_sem.at[k])

    for k in range(count):
        load(k).start()
    place.barrier()

    def remote(src, dst, send_sem, recv_sem, way):
        return pltpu.make_async_remote_copy(
            src_ref=src,
            dst_ref=dst,
            send_sem=send_sem,
            recv_sem=recv_sem,
            device_id=place.device(way),
            device_id_type=MESH,
        )

    def send_c(k, pid):
        return remote(
            ins[k].at[pid, 1 - place.c], part[k].at[pid], c_send.at[k, pid], c_recv.at[k, pid], "c"
        )

    def send_q(k, rel_p, z0):
        pid = place.piece(routes[k], rel_p, 1, z0)
        return remote(
            own[k].at[pid],
            land_q[k].at[rel_p, z0],
            q_send.at[k, rel_p, z0],
            q_recv.at[k, rel_p, z0],
            routes[k][1],
        )

    def send_p(k, z0):
        pid = place.piece(routes[k], 1, 0, z0)
        return remote(
            own[k].at[pid], land_p[k].at[z0], p_send.at[k, z0], p_recv.at[k, z0], routes[k][0]
        )

    def send_z(k, z0, up):
        pid = place.piece(routes[k], 0, 0, z0)
        if up:
            target = z0
        else:
            target = jnp.where(z0 == place.z - 1, depth, z0)
        return remote(
            own[k].at[pid],
            land_z[k].at[target],
            z_send.at[k, z0],
            z_recv.at[k, target],
            "up" if up else "down",
        )

    def wait_z(k, index):
        pltpu.make_async_copy(land_z[k].at[index], land_z[k].at[index], z_recv.at[k, index]).wait()

    def first(s, carry):
        def body(z0, above):
            for k in range(count):
                for rel_q in (1, 0):
                    for rel_p in (1, 0) if routes[k][0] is not None else (0,):
                        send_c(k, place.piece(routes[k], rel_p, rel_q, z0)).start()

        both_sides(place, depth - 1 - s, body)
        return carry

    lax.fori_loop(0, depth, first, 0)
    for k in range(count):
        load(k).wait()

    def step(s, carry):
        def leaf(z0, above):
            for k in range(count):
                for rel_p in (1, 0) if routes[k][0] is not None else (0,):
                    pid = place.piece(routes[k], rel_p, 1, z0)
                    send_c(k, pid).wait_recv()
                    add_up(own[k].at[pid], [own[k].at[pid], part[k].at[pid]], rows[k])
                    send_q(k, rel_p, z0).start()

        def middle(z0, above):
            for k in range(count):
                if routes[k][0] is not None:
                    pid = place.piece(routes[k], 1, 0, z0)
                    send_c(k, pid).wait_recv()
                    send_q(k, 1, z0).wait_recv()
                    add_up(
                        own[k].at[pid],
                        [own[k].at[pid], part[k].at[pid], land_q[k].at[1, z0]],
                        rows[k],
                    )
                    send_p(k, z0).start()

        def sources_of(k, z0):
            pid = place.piece(routes[k], 0, 0, z0)
            send_c(k, pid).wait_recv()
            send_q(k, 0, z0).wait_recv()
            sources = [own[k].at[pid], part[k].at[pid], land_q[k].at[0, z0]]
            if routes[k][0] is not None:
                send_p(k, z0).wait_recv()
                sources.append(land_p[k].at[z0])
            return pid, sources

        def along(z0, above):
            for k in range(count):
                pid, sources = sources_of(k, z0)
                child = place.has_down if above else place.has_up

                @pl.when(child)
                def _():
                    wait_z(k, z0)
                    add_up(own[k].at[pid], sources + [land_z[k].at[z0]], rows[k])

                @pl.when(jnp.logical_not(child))
                def _():
                    add_up(own[k].at[pid], sources, rows[k])

                send_z(k, z0, above).start()

        both_sides(place, depth - 1 - s, leaf)

        if work.count:

            @pl.when(s < work.count)
            def _():
                work.body(s, place.ctx, *work_ins, *work_outs)

        @pl.when(s < depth + 1)
        def _():
            both_sides(place, depth - s, middle)

        @pl.when(depth + 1 - s >= 1)
        def _():
            both_sides(place, depth + 1 - s, along)

        @pl.when(s == depth + 1)
        def _():
            for k in range(count):
                _, sources = sources_of(k, place.z)
                add_up(outs[k], sources, rows[k])

                @pl.when(place.has_down)
                def _():
                    wait_z(k, place.z)
                    add_up(outs[k], [outs[k], land_z[k].at[place.z]], rows[k])

                @pl.when(place.has_up)
                def _():
                    wait_z(k, depth)
                    add_up(outs[k], [outs[k], land_z[k].at[depth]], rows[k])

        return carry

    lax.fori_loop(0, depth + 2, step, 0)
    for item in range(depth + 2, work.count):
        work.body(item, place.ctx, *work_ins, *work_outs)

    def finish(z0, carry):
        for k in range(count):
            send_q(k, 0, z0).wait_send()
            if routes[k][0] is not None:
                send_q(k, 1, z0).wait_send()
                send_p(k, z0).wait_send()

            @pl.when(z0 > place.z)
            def _():
                send_z(k, z0, True).wait_send()

            @pl.when(z0 < place.z)
            def _():
                send_z(k, z0, False).wait_send()

        return carry

    lax.fori_loop(0, depth, finish, 0)

    def finish_partner(pid, carry):
        for k in range(count):
            send_c(k, pid).wait_send()
        return carry

    lax.fori_loop(0, pieces, finish_partner, 0)


def scatter(arrays, routes, use_x, collective_id, name, work=Work()):
    depth = lax.axis_size("ctx") // 4
    pieces = (4 if use_x else 2) * depth
    count = len(arrays)
    dma = pltpu.SemaphoreType.DMA
    shapes = [a.shape[1:] for a in arrays]
    pairs = [a.reshape(pieces, 2, *s) for a, s in zip(arrays, shapes)]
    bf16 = jnp.bfloat16
    return pl.pallas_call(
        functools.partial(scatter_kernel, depth, use_x, routes, work),
        out_shape=[jax.ShapeDtypeStruct(s, jnp.float32) for s in shapes] + work.shapes,
        in_specs=[pl.BlockSpec(memory_space=pl.ANY)] * count
        + [pl.BlockSpec(memory_space=pltpu.VMEM)] * work.ins,
        out_specs=[pl.BlockSpec(memory_space=pltpu.VMEM)] * (count + work.outs),
        scratch_shapes=[pltpu.VMEM((pieces, *s), bf16) for s in shapes]
        + [pltpu.VMEM((pieces, *s), bf16) for s in shapes]
        + [pltpu.VMEM((2, depth, *s), bf16) for s in shapes]
        + [pltpu.VMEM((depth, *s), bf16) for s in shapes]
        + [pltpu.VMEM((depth + 1, *s), bf16) for s in shapes]
        + [
            dma((count,)),
            dma((count, pieces)),
            dma((count, pieces)),
            dma((count, 2, depth)),
            dma((count, 2, depth)),
            dma((count, depth)),
            dma((count, depth)),
            dma((count, depth)),
            dma((count, depth + 1)),
        ],
        compiler_params=pltpu.CompilerParams(
            collective_id=collective_id, has_side_effects=True, vmem_limit_bytes=VMEM_LIMIT
        ),
        name=name,
    )(*pairs, *work.arrays)


def padded(rows, multiple=16):
    return -(-rows // multiple) * multiple


def pad_rows(rows, total):
    return jnp.pad(rows, ((0, total - rows.shape[0]), (0, 0)))


XY, YX, ONLY_Y = ("x", "y"), ("y", "x"), (None, "y")
REST_ROUTES = (YX, XY, XY, YX)


def halves(values, split_count):
    return values.reshape(values.shape[0], split_count, values.shape[1] // split_count)


def forward_dot(values, weights):
    split_count = weights.shape[0]
    part = values.shape[1] // split_count
    total = None
    for i in range(split_count):
        term = lax.dot_general(
            values[:, i * part : (i + 1) * part],
            weights[i],
            (((1,), (1,)), ((), ())),
            preferred_element_type=jnp.float32,
        )
        total = term if total is None else total + term
    return total


def backward_dot(grads, weights):
    return jnp.concatenate(
        [
            jnp.dot(grads, weights[i], preferred_element_type=jnp.float32)
            for i in range(weights.shape[0])
        ],
        axis=-1,
    )


def terms_kernel(grads, values, out):
    for i in range(values.shape[0]):
        out[i] = lax.dot_general(
            grads[...], values[i], (((0,), (0,)), ((), ())), preferred_element_type=jnp.float32
        ).astype(out.dtype)


def weight_terms(grads, values, split_count):
    rows, width = grads.shape
    values = jnp.transpose(halves(values, split_count), (1, 0, 2))
    block = next((b for b in (512, 256, 128) if width % b == 0), width)
    part = values.shape[2]
    return pl.pallas_call(
        terms_kernel,
        out_shape=jax.ShapeDtypeStruct((split_count, width, part), jnp.bfloat16),
        grid=(width // block,),
        in_specs=[
            pl.BlockSpec((rows, block), lambda i: (0, i)),
            pl.BlockSpec(values.shape, lambda i: (0, 0, 0)),
        ],
        out_specs=pl.BlockSpec((split_count, block, part), lambda i: (0, i, 0)),
        compiler_params=pltpu.CompilerParams(vmem_limit_bytes=VMEM_LIMIT),
        cost_estimate=pl.CostEstimate(
            flops=2 * rows * width * part * split_count,
            bytes_accessed=2 * width * part * split_count,
            transcendentals=0,
        ),
        name="weight_terms",
    )(grads, values)


PIECES_PER_BLOCK = 4


def block_scores(step, ctx, kv_ref, group, query):
    _, _, block_len, width = kv_ref.shape
    span = pl.ds(step * PIECES_PER_BLOCK, PIECES_PER_BLOCK)
    kv = kv_ref[span, group].reshape(PIECES_PER_BLOCK * block_len, width)
    scores = (
        lax.dot_general(kv, query, (((1,), (1,)), ((), ())), preferred_element_type=jnp.float32)
        * 0.125
    )
    key_pos = step * kv.shape[0] + lax.broadcasted_iota(jnp.int32, scores.shape, 0)
    query_pos = ctx * block_len + lax.rem(
        lax.broadcasted_iota(jnp.int32, scores.shape, 1), block_len
    )
    return kv, scores, key_pos <= query_pos


def attend_body(group, ctx, kv_ref, query_ref, out_ref, logsum_ref):
    query = query_ref[group]
    rows, width = query.shape

    def body(step, carry):
        peak, total, acc = carry
        kv, scores, allowed = block_scores(step, ctx, kv_ref, group, query)
        scores = jnp.where(allowed, scores, -jnp.inf)
        new_peak = jnp.maximum(peak, jnp.max(scores, axis=0, keepdims=True))
        terms = jnp.exp(scores - new_peak)
        shrink = jnp.exp(peak - new_peak)
        total = total * shrink + jnp.sum(terms, axis=0, keepdims=True)
        acc = acc * shrink + lax.dot_general(
            kv,
            terms.astype(jnp.bfloat16),
            (((0,), (0,)), ((), ())),
            preferred_element_type=jnp.float32,
        )
        return new_peak, total, acc

    peak, total, acc = lax.fori_loop(
        0,
        ctx // PIECES_PER_BLOCK + 1,
        body,
        (
            jnp.full((1, rows), -jnp.inf, jnp.float32),
            jnp.zeros((1, rows), jnp.float32),
            jnp.zeros((width, rows), jnp.float32),
        ),
    )
    out_ref[group] = acc / total
    logsum_ref[group] = peak + jnp.log(total)


def retrace_body(group, ctx, kv_ref, query_ref, grad_ref, logsum_ref, delta_ref, dq_ref, dkv_ref):
    query, grad = query_ref[group], grad_ref[group]
    logsum, delta = logsum_ref[group], delta_ref[group]
    blocks, _, block_len, width = kv_ref.shape
    needed = ctx // PIECES_PER_BLOCK + 1

    def body(step, dq):
        kv, scores, allowed = block_scores(step, ctx, kv_ref, group, query)
        probs = jnp.where(allowed, jnp.exp(scores - logsum), 0.0)
        grad_probs = lax.dot_general(
            kv, grad, (((1,), (1,)), ((), ())), preferred_element_type=jnp.float32
        )
        grad_scores = (probs * (grad_probs - delta) * 0.125).astype(jnp.bfloat16)
        dkv = jnp.dot(
            probs.astype(jnp.bfloat16), grad, preferred_element_type=jnp.float32
        ) + jnp.dot(grad_scores, query, preferred_element_type=jnp.float32)
        span = pl.ds(step * PIECES_PER_BLOCK, PIECES_PER_BLOCK)
        dkv_ref[span, group] = dkv.astype(jnp.bfloat16).reshape(PIECES_PER_BLOCK, block_len, width)
        return dq + lax.dot_general(
            grad_scores, kv, (((0,), (0,)), ((), ())), preferred_element_type=jnp.float32
        )

    dq_ref[group] = lax.fori_loop(0, needed, body, jnp.zeros(query.shape, jnp.float32))

    def clear(step, carry):
        span = pl.ds(step * PIECES_PER_BLOCK, PIECES_PER_BLOCK)
        dkv_ref[span, group] = jnp.zeros((PIECES_PER_BLOCK, block_len, width), jnp.bfloat16)
        return carry

    lax.fori_loop(needed, blocks // PIECES_PER_BLOCK, clear, 0)


def local(
    inputs, grad_output, w_query, w_key, w_value, w_out, w_gate, w_up, w_down, gain_attn, gain_mlp
):
    seq_count, block_len, model_width = inputs.shape
    row_count = seq_count * block_len
    split_count = lax.axis_size("fsdp")
    cycle_size = lax.axis_size("ctx")
    cycle_index = lax.axis_index("ctx")
    groups = KV_HEADS
    head_size = HEAD
    repeat_count = HEADS // KV_HEADS
    kv_width = groups * head_size
    positions = cycle_index * block_len + jnp.arange(block_len, dtype=jnp.int32)
    cosine, sine_table = tables(positions, head_size)
    cosine = jnp.tile(cosine, (seq_count, 1))
    sine_table = jnp.tile(sine_table, (seq_count, 1))
    wide_q, wide_k, wide_v = w_query.shape[1], w_key.shape[1], w_value.shape[1]
    wide_o, wide_g, wide_u = w_out.shape[1], w_gate.shape[1], w_up.shape[1]
    wide_d = w_down.shape[1]
    pad_q, pad_k, pad_v = padded(wide_q), padded(wide_k + 1), padded(wide_v)
    pad_o, pad_g, pad_u, pad_d = padded(wide_o), padded(wide_g), padded(wide_u), padded(wide_d)
    part_width = w_query.shape[0]
    gain_size = gain_attn.shape[0]

    def open_up(values, wide, start, pad):
        pieces = values.reshape(values.shape[0], cycle_size, -1)
        return pieces[:, :, start : start + wide].reshape(values.shape[0], cycle_size * wide)

    def close_up(values, wide, pad):
        pieces = values.reshape(values.shape[0], cycle_size, wide)
        return jnp.pad(pieces, ((0, 0), (0, 0), (0, pad - wide))).reshape(values.shape[0], -1)

    gain_row = jnp.pad(
        jnp.concatenate([gain_attn, gain_mlp]), (0, part_width - 2 * gain_size)
    )[None, :]
    first_piece = jnp.concatenate(
        [
            pad_rows(w_query.T, pad_q),
            pad_rows(jnp.concatenate([w_key.T, gain_row], axis=0), pad_k),
            pad_rows(w_value.T, pad_v),
        ],
        axis=0,
    )
    half = padded(first_piece.shape[0] // 2)
    first_a, first_b = gather(
        [first_piece[:half], first_piece[half:]], (YX, XY), True, 0, "gather_first"
    )
    first = jnp.concatenate([first_a, first_b], axis=1)
    gain_rows = first[:cycle_size, pad_q + wide_k, : 2 * gain_size]
    gain_first = gain_rows[:, :gain_size].reshape(-1).astype(jnp.float32)
    gain_second = gain_rows[:, gain_size:].reshape(-1).astype(jnp.float32)
    first = first.reshape(split_count, -1, part_width)

    resid1 = inputs.reshape(row_count, model_width).astype(jnp.float32)
    normal1 = normed(resid1, gain_first).astype(jnp.bfloat16)
    raw = forward_dot(normal1, first)
    query_raw = open_up(raw, wide_q, 0, pad_q).reshape(row_count, HEADS, head_size)
    query_rot = rotate(query_raw, cosine, sine_table).astype(jnp.bfloat16)
    key_raw = open_up(raw, wide_k, pad_q, pad_k).reshape(row_count, groups, head_size)
    key_rows = rotate(key_raw, cosine, sine_table).astype(jnp.bfloat16)
    value_rows = open_up(raw, wide_v, pad_q + pad_k, pad_v).astype(jnp.bfloat16)
    value_rows = value_rows.reshape(row_count, groups, head_size)
    pair_rows = jnp.transpose(jnp.concatenate([key_rows, value_rows], axis=-1), (1, 0, 2))
    (pair_all,) = gather(
        [pair_rows.reshape(groups * row_count, 2 * head_size)],
        (ONLY_Y,),
        False,
        1,
        "gather_pairs",
    )
    pair_all = pair_all.reshape(cycle_size, groups, row_count, 2 * head_size)

    def by_group(values):
        values = values.reshape(row_count, groups, repeat_count, head_size)
        return jnp.transpose(values, (1, 2, 0, 3)).reshape(groups, repeat_count * row_count, head_size)

    query_grouped = jnp.pad(by_group(query_rot), ((0, 0), (0, 0), (0, head_size)))
    width = repeat_count * row_count
    out_w, gate_w, up_w, down_w, attended_turned, logsum = gather(
        [
            pad_rows(w_out.T, pad_o),
            pad_rows(w_gate.T, pad_g),
            pad_rows(w_up.T, pad_u),
            pad_rows(w_down.T, pad_d),
        ],
        REST_ROUTES,
        True,
        4,
        "gather_rest_attend",
        Work(
            groups,
            attend_body,
            [pair_all, query_grouped],
            [
                jax.ShapeDtypeStruct((groups, 2 * head_size, width), jnp.float32),
                jax.ShapeDtypeStruct((groups, 1, width), jnp.float32),
            ],
        ),
    )
    out_w, gate_w, up_w, down_w = (
        w.reshape(split_count, -1, w.shape[-1]) for w in (out_w, gate_w, up_w, down_w)
    )
    attended_wide = jnp.transpose(
        attended_turned[:, head_size:].reshape(groups, head_size, repeat_count, row_count),
        (3, 0, 2, 1),
    )
    attended_rows = attended_wide.astype(jnp.bfloat16).reshape(row_count, HEADS * head_size)
    resid2 = resid1 + open_up(forward_dot(attended_rows, out_w), wide_o, 0, pad_o)
    normal2 = normed(resid2, gain_second).astype(jnp.bfloat16)
    gate_act = forward_dot(normal2, gate_w)
    up_act = forward_dot(normal2, up_w)
    gate_sigma = jax.nn.sigmoid(gate_act)
    hidden = (gate_act * gate_sigma * up_act).astype(jnp.bfloat16)
    hidden_flat = open_up(hidden, wide_g, 0, pad_g)
    output = (
        resid2 + open_up(forward_dot(hidden_flat, down_w), wide_d, 0, pad_d)
    ).astype(jnp.bfloat16)

    grad_rows = grad_output.reshape(row_count, model_width)
    grad_rows_padded = close_up(grad_rows, wide_d, pad_d)
    terms_down = weight_terms(grad_rows_padded, hidden_flat, split_count)
    grad_hidden = close_up(backward_dot(grad_rows_padded, down_w), wide_g, pad_g)
    grad_up = (grad_hidden * gate_act * gate_sigma).astype(jnp.bfloat16)
    grad_gate = (grad_hidden * up_act * gate_sigma * (1.0 + gate_act * (1.0 - gate_sigma))).astype(
        jnp.bfloat16
    )
    grad_norm2 = backward_dot(grad_gate, gate_w) + backward_dot(grad_up, up_w)
    normed_out, pull_second = jax.vjp(normed, resid2, gain_second)
    grad_part2, term_gain2 = pull_second(grad_norm2)
    grad_resid2 = grad_rows.astype(jnp.float32) + grad_part2
    grad_branch = close_up(grad_resid2.astype(jnp.bfloat16), wide_o, pad_o)
    terms_out = weight_terms(grad_branch, attended_rows, split_count)
    terms_gate = weight_terms(grad_gate, normal2, split_count)
    terms_up = weight_terms(grad_up, normal2, split_count)
    grad_attended = backward_dot(grad_branch, out_w).astype(jnp.bfloat16)
    row_delta = jnp.sum(
        grad_attended.astype(jnp.float32).reshape(attended_wide.shape) * attended_wide, axis=-1
    )
    row_delta = jnp.transpose(row_delta, (1, 2, 0)).reshape(groups, 1, width)
    grad_grouped = jnp.pad(by_group(grad_attended), ((0, 0), (0, 0), (head_size, 0)))

    def pieces_of(terms):
        return terms.reshape(split_count * cycle_size, -1, terms.shape[-1])

    sum_out, sum_gate, sum_up, sum_down, grad_query_acc, grad_pair_all = scatter(
        [pieces_of(t) for t in (terms_out, terms_gate, terms_up, terms_down)],
        REST_ROUTES,
        True,
        3,
        "scatter_rest_retrace",
        Work(
            groups,
            retrace_body,
            [pair_all, query_grouped, grad_grouped, logsum, row_delta],
            [
                jax.ShapeDtypeStruct(query_grouped.shape, jnp.float32),
                jax.ShapeDtypeStruct(pair_all.shape, jnp.bfloat16),
            ],
        ),
    )
    (grad_pair_own,) = scatter(
        [grad_pair_all.reshape(cycle_size, groups * row_count, 2 * head_size)],
        (ONLY_Y,),
        False,
        2,
        "scatter_pairs",
    )
    grad_pair_own = jnp.transpose(
        grad_pair_own.reshape(groups, row_count, 2 * head_size), (1, 0, 2)
    )
    grad_query_rows = jnp.transpose(
        grad_query_acc[..., :head_size].reshape(groups, repeat_count, row_count, head_size),
        (2, 0, 1, 3),
    ).reshape(row_count, HEADS, head_size)
    grad_query = (
        unrotate(grad_query_rows, cosine, sine_table)
        .reshape(row_count, HEADS * head_size)
        .astype(jnp.bfloat16)
    )
    grad_keys = (
        unrotate(grad_pair_own[..., :head_size], cosine, sine_table)
        .reshape(row_count, kv_width)
        .astype(jnp.bfloat16)
    )
    grad_values = grad_pair_own[..., head_size:].astype(jnp.bfloat16).reshape(row_count, kv_width)

    def shaped(values, wide, pad):
        pieces = values.reshape(row_count, cycle_size, wide)
        return jnp.pad(pieces, ((0, 0), (0, 0), (0, pad - wide)))

    grad_raw = jnp.concatenate(
        [
            shaped(grad_query, wide_q, pad_q),
            shaped(grad_keys, wide_k, pad_k),
            shaped(grad_values, wide_v, pad_v),
        ],
        axis=-1,
    ).reshape(row_count, -1)
    grad_norm1 = backward_dot(grad_raw, first)
    normed_first, pull_first = jax.vjp(normed, resid1, gain_first)
    grad_part1, term_gain1 = pull_first(grad_norm1)
    grad_input = (
        (grad_resid2 + grad_part1).astype(jnp.bfloat16).reshape(seq_count, block_len, model_width)
    )
    gain_terms = jnp.concatenate(
        [term_gain1.reshape(cycle_size, -1), term_gain2.reshape(cycle_size, -1)], axis=-1
    ).astype(jnp.bfloat16)
    terms_first = weight_terms(grad_raw, normal1, split_count)
    terms_first = terms_first.reshape(split_count, cycle_size, -1, part_width)
    terms_first = terms_first.at[:, :, pad_q + wide_k, : 2 * gain_size].set(gain_terms[None])

    terms_first = terms_first.reshape(split_count * cycle_size, -1, part_width)
    sum_first = jnp.concatenate(
        scatter([terms_first[:, :half], terms_first[:, half:]], (YX, XY), True, 5, "scatter_first")
    )
    start_k, start_v = pad_q, pad_q + pad_k
    gain_sums = sum_first[pad_q + wide_k]
    return (
        output.reshape(seq_count, block_len, model_width),
        grad_input,
        sum_first[:wide_q].T,
        sum_first[start_k : start_k + wide_k].T,
        sum_first[start_v : start_v + wide_v].T,
        sum_out[:wide_o].T,
        sum_gate[:wide_g].T,
        sum_up[:wide_u].T,
        sum_down[:wide_d].T,
        gain_sums[:gain_size],
        gain_sums[gain_size : 2 * gain_size],
    )


def solution(mesh):
    rows, weight, gain = P("fsdp", "ctx", None), P("fsdp", "ctx"), P("ctx")
    return jax.shard_map(
        local,
        mesh=mesh,
        in_specs=(rows, rows) + (weight,) * 7 + (gain, gain),
        out_specs=(rows, rows) + (weight,) * 7 + (gain, gain),
        check_vma=False,
    )
```

```python
import functools

import jax
import jax.numpy as jnp
from jax import lax
from jax.experimental import pallas as pl
from jax.experimental.pallas import tpu as pltpu
from jax.sharding import PartitionSpec as P

HEADS = 15
KV_HEADS = 5
HEAD = 64

EPSILON = 1e-05
ROPE_THETA = 100000.0
MESH = pl.DeviceIdType.MESH
VMEM_LIMIT = 67_000_000


def tables(positions, head_size):
    half_size = head_size // 2
    frequency = ROPE_THETA ** (-jnp.arange(half_size, dtype=jnp.float32) * 2.0 / head_size)
    angles = positions.astype(jnp.float32)[:, None] * frequency[None, :]
    return (jnp.cos(angles), jnp.sin(angles))


def rotate(values, cosine, sine_table):
    half_size = values.shape[-1] // 2
    first_half = values[..., :half_size]
    second = values[..., half_size:]
    cosine = cosine[:, None, :]
    sine_table = sine_table[:, None, :]
    return jnp.concatenate(
        [first_half * cosine - second * sine_table, second * cosine + first_half * sine_table],
        axis=-1,
    )


def unrotate(values, cosine, sine_table):
    return rotate(values, cosine, -sine_table)


class Place:
    def __init__(self, depth, use_x):
        self.depth = depth
        self.use_x = use_x
        self.f = lax.axis_index("fsdp")
        self.ctx = lax.axis_index("ctx")
        self.c = self.ctx % 2
        self.y = (self.ctx // 2) % 2
        self.z = self.ctx // 4
        self.has_up = self.z < depth - 1
        self.has_down = self.z > 0

    def device(self, way):
        if way == "c":
            return (self.f, self.ctx + 1 - 2 * self.c)
        if way == "y":
            return (self.f, self.ctx + 2 - 4 * self.y)
        if way == "x":
            return (1 - self.f, self.ctx)
        return (self.f, self.ctx + (4 if way == "up" else -4))

    def piece(self, route, rel_p, rel_q, z):
        rel = {route[1]: rel_q}
        if route[0] is not None:
            rel[route[0]] = rel_p
        y0 = 1 - self.y if rel.get("y", 0) else self.y
        pid = z * 2 + y0
        if self.use_x:
            x0 = 1 - self.f if rel.get("x", 0) else self.f
            pid = pid + x0 * 2 * self.depth
        return pid

    def barrier(self):
        sem = pltpu.get_barrier_semaphore()
        ways = ["c", "y"] + (["x"] if self.use_x else [])
        for way in ways:
            pl.semaphore_signal(sem, inc=1, device_id=self.device(way), device_id_type=MESH)

        @pl.when(self.has_up)
        def _():
            pl.semaphore_signal(sem, inc=1, device_id=self.device("up"), device_id_type=MESH)

        @pl.when(self.has_down)
        def _():
            pl.semaphore_signal(sem, inc=1, device_id=self.device("down"), device_id_type=MESH)

        peers = len(ways) + self.has_up.astype(jnp.int32) + self.has_down.astype(jnp.int32)
        pl.semaphore_wait(sem, peers)


def both_sides(place, distance, body):
    high = place.z + distance
    low = place.z - distance

    @pl.when((distance >= 0) & (high < place.depth))
    def _():
        body(high, True)

    @pl.when((distance >= 1) & (low >= 0))
    def _():
        body(low, False)


class Chunk:
    def __init__(self, array, start, rows, route):
        self.array, self.start, self.rows, self.route = array, start, rows, route
        self.span = pl.ds(start, rows)


def cut(array, rows, parts, routes):
    size = padded(-(-rows // parts))
    starts = range(0, rows, size)
    return [
        Chunk(array, start, min(size, rows - start), routes[i % len(routes)])
        for i, start in enumerate(starts)
    ]


def gather_kernel(depth, use_x, chunks, work, *refs):
    total, count = chunks[-1].array + 1, len(chunks)
    routes = [chunk.route for chunk in chunks]
    ins, work_ins, refs = refs[:total], refs[total : total + work.ins], refs[total + work.ins :]
    outs, work_outs, refs = refs[:total], refs[total : total + work.outs], refs[total + work.outs :]
    recv, send_z, send_p, send_q, send_c, local_sem = refs
    place = Place(depth, use_x)
    place.barrier()

    def landing(k, slot):
        return outs[chunks[k].array].at[slot, chunks[k].span]

    def copy(k, pid, send_sem, way, src=None):
        slot = pid * 2 + place.c
        return pltpu.make_async_remote_copy(
            src_ref=landing(k, slot) if src is None else src,
            dst_ref=landing(k, slot),
            send_sem=send_sem,
            recv_sem=recv.at[k, slot],
            device_id=place.device(way),
            device_id_type=MESH,
        )

    def forward_z(k, z0, up, src=None):
        pid = place.piece(routes[k], 0, 0, z0)
        return copy(k, pid, send_z.at[k, 0 if up else 1, z0], "up" if up else "down", src)

    def forward_p(k, z0, src=None):
        return copy(k, place.piece(routes[k], 0, 0, z0), send_p.at[k, z0], routes[k][0], src)

    def forward_q(k, rel_p, z0, src=None):
        pid = place.piece(routes[k], rel_p, 0, z0)
        return copy(k, pid, send_q.at[k, rel_p, z0], routes[k][1], src)

    def forward_c(k, pid, src=None):
        return copy(k, pid, send_c.at[k, pid], "c", src)

    def arrived(k, pid):
        copy(k, pid, send_c.at[k, pid], "c").wait_recv()

    own = []
    for k in range(count):
        pid = place.piece(routes[k], 0, 0, place.z)
        src = ins[chunks[k].array].at[chunks[k].span]

        @pl.when(place.has_up)
        def _():
            forward_z(k, place.z, True, src).start()

        @pl.when(place.has_down)
        def _():
            forward_z(k, place.z, False, src).start()

        if routes[k][0] is not None:
            forward_p(k, place.z, src).start()
        forward_q(k, 0, place.z, src).start()
        forward_c(k, pid, src).start()
        mine = pltpu.make_async_copy(src, landing(k, pid * 2 + place.c), local_sem.at[k])
        mine.start()
        own.append(mine)

    def step(d, carry):
        def from_z(z0, above):
            for k in range(count):
                pid = place.piece(routes[k], 0, 0, z0)
                arrived(k, pid)
                if above:

                    @pl.when(place.has_down)
                    def _():
                        forward_z(k, z0, False).start()

                else:

                    @pl.when(place.has_up)
                    def _():
                        forward_z(k, z0, True).start()

                if routes[k][0] is not None:
                    forward_p(k, z0).start()
                forward_q(k, 0, z0).start()
                forward_c(k, pid).start()

        def from_p(z0, above):
            for k in range(count):
                if routes[k][0] is not None:
                    pid = place.piece(routes[k], 1, 0, z0)
                    arrived(k, pid)
                    forward_q(k, 1, z0).start()
                    forward_c(k, pid).start()

        def from_q(rel_p, z0, above):
            for k in range(count):
                if routes[k][0] is not None or not rel_p:
                    pid = place.piece(routes[k], rel_p, 1, z0)
                    arrived(k, pid)
                    forward_c(k, pid).start()

        @pl.when((d >= 1) & (d < depth))
        def _():
            both_sides(place, d, from_z)

        both_sides(place, d - 1, from_p)
        both_sides(place, d - 1, functools.partial(from_q, 0))
        both_sides(place, d - 2, functools.partial(from_q, 1))

        if work.count:

            @pl.when(d - 1 < work.count)
            def _():
                work.body(d - 1, place.ctx, *work_ins, *work_outs)

        return carry

    lax.fori_loop(1, depth + 2, step, 0)
    for item in range(depth + 1, work.count):
        work.body(item, place.ctx, *work_ins, *work_outs)

    def finish(z0, carry):
        for k in range(count):

            @pl.when(place.has_up & (z0 <= place.z))
            def _():
                forward_z(k, z0, True).wait_send()

            @pl.when(place.has_down & (z0 >= place.z))
            def _():
                forward_z(k, z0, False).wait_send()

            if routes[k][0] is not None:
                forward_p(k, z0).wait_send()
                forward_q(k, 1, z0).wait_send()
            forward_q(k, 0, z0).wait_send()
        return carry

    lax.fori_loop(0, depth, finish, 0)

    def finish_partner(pid, carry):
        for k in range(count):
            forward_c(k, pid).wait_send()
            slot = pid * 2 + 1 - place.c
            pltpu.make_async_remote_copy(
                src_ref=landing(k, slot),
                dst_ref=landing(k, slot),
                send_sem=send_c.at[k, pid],
                recv_sem=recv.at[k, slot],
                device_id=place.device("c"),
                device_id_type=MESH,
            ).wait_recv()
        return carry

    lax.fori_loop(0, (4 if use_x else 2) * depth, finish_partner, 0)
    for mine in own:
        mine.wait()


class Work:
    def __init__(self, count=0, body=None, arrays=(), shapes=()):
        self.count, self.body, self.arrays, self.shapes = count, body, arrays, list(shapes)
        self.ins, self.outs = len(arrays), len(self.shapes)


def gather(arrays, chunks, use_x, collective_id, name, work=Work()):
    depth = lax.axis_size("ctx") // 4
    pieces = (4 if use_x else 2) * depth
    total, count = len(arrays), len(chunks)
    dma = pltpu.SemaphoreType.DMA
    return pl.pallas_call(
        functools.partial(gather_kernel, depth, use_x, chunks, work),
        out_shape=[jax.ShapeDtypeStruct((2 * pieces, *a.shape), a.dtype) for a in arrays]
        + work.shapes,
        in_specs=[pl.BlockSpec(memory_space=pltpu.VMEM)] * (total + work.ins),
        out_specs=[pl.BlockSpec(memory_space=pl.ANY)] * total
        + [pl.BlockSpec(memory_space=pltpu.VMEM)] * work.outs,
        scratch_shapes=[
            dma((count, 2 * pieces)),
            dma((count, 2, depth)),
            dma((count, depth)),
            dma((count, 2, depth)),
            dma((count, pieces)),
            dma((count,)),
        ],
        compiler_params=pltpu.CompilerParams(
            collective_id=collective_id, has_side_effects=True, vmem_limit_bytes=VMEM_LIMIT
        ),
        name=name,
    )(*arrays, *work.arrays)


def add_up(dst, sources, rows):
    block = 32 if rows % 32 == 0 else 16

    def body(i, carry):
        span = pl.ds(pl.multiple_of(i * block, block), block)
        total = sources[0][span, :].astype(jnp.float32)
        for source in sources[1:]:
            total = total + source[span, :].astype(jnp.float32)
        dst[span, :] = total.astype(dst.dtype)
        return carry

    lax.fori_loop(0, rows // block, body, 0)


def scatter_kernel(depth, use_x, chunks, work, *refs):
    total, count = chunks[-1].array + 1, len(chunks)
    routes = [chunk.route for chunk in chunks]
    ins, work_ins, refs = refs[:total], refs[total : total + work.ins], refs[total + work.ins :]
    outs, work_outs, refs = refs[:total], refs[total : total + work.outs], refs[total + work.outs :]
    whole = [refs[i * total : (1 + i) * total] for i in range(5)]
    load_sem, c_send, c_recv, q_send, q_recv, p_send, p_recv, z_send, z_recv = refs[5 * total :]

    class View:
        def __init__(self, ref, span):
            self.ref, self.span = ref, span

        @property
        def at(self):
            return self

        def __getitem__(self, index):
            index = index if isinstance(index, tuple) else (index,)
            return self.ref.at[(*index, self.span)]

    own, part, land_q, land_p, land_z = (
        [View(group[chunk.array], chunk.span) for chunk in chunks] for group in whole
    )
    sums = [outs[chunk.array].at[chunk.span] for chunk in chunks]
    place = Place(depth, use_x)
    pieces = (4 if use_x else 2) * depth
    rows = [chunk.rows for chunk in chunks]

    def load(k):
        return pltpu.make_async_copy(ins[k].at[:, place.c], whole[0][k], load_sem.at[k])

    for k in range(total):
        load(k).start()
    place.barrier()

    def remote(src, dst, send_sem, recv_sem, way):
        return pltpu.make_async_remote_copy(
            src_ref=src,
            dst_ref=dst,
            send_sem=send_sem,
            recv_sem=recv_sem,
            device_id=place.device(way),
            device_id_type=MESH,
        )

    def send_c(k, pid):
        return remote(
            ins[chunks[k].array].at[pid, 1 - place.c, chunks[k].span], part[k].at[pid], c_send.at[k, pid], c_recv.at[k, pid], "c"
        )

    def send_q(k, rel_p, z0):
        pid = place.piece(routes[k], rel_p, 1, z0)
        return remote(
            own[k].at[pid],
            land_q[k].at[rel_p, z0],
            q_send.at[k, rel_p, z0],
            q_recv.at[k, rel_p, z0],
            routes[k][1],
        )

    def send_p(k, z0):
        pid = place.piece(routes[k], 1, 0, z0)
        return remote(
            own[k].at[pid], land_p[k].at[z0], p_send.at[k, z0], p_recv.at[k, z0], routes[k][0]
        )

    def send_z(k, z0, up):
        pid = place.piece(routes[k], 0, 0, z0)
        if up:
            target = z0
        else:
            target = jnp.where(z0 == place.z - 1, depth, z0)
        return remote(
            own[k].at[pid],
            land_z[k].at[target],
            z_send.at[k, z0],
            z_recv.at[k, target],
            "up" if up else "down",
        )

    def wait_z(k, index):
        pltpu.make_async_copy(land_z[k].at[index], land_z[k].at[index], z_recv.at[k, index]).wait()

    def first(s, carry):
        def body(z0, above):
            for k in range(count):
                for rel_q in (1, 0):
                    for rel_p in (1, 0) if routes[k][0] is not None else (0,):
                        send_c(k, place.piece(routes[k], rel_p, rel_q, z0)).start()

        both_sides(place, depth - 1 - s, body)
        return carry

    lax.fori_loop(0, depth, first, 0)
    for k in range(total):
        load(k).wait()

    def step(s, carry):
        def leaf(z0, above):
            for k in range(count):
                for rel_p in (1, 0) if routes[k][0] is not None else (0,):
                    pid = place.piece(routes[k], rel_p, 1, z0)
                    send_c(k, pid).wait_recv()
                    add_up(own[k].at[pid], [own[k].at[pid], part[k].at[pid]], rows[k])
                    send_q(k, rel_p, z0).start()

        def middle(z0, above):
            for k in range(count):
                if routes[k][0] is not None:
                    pid = place.piece(routes[k], 1, 0, z0)
                    send_c(k, pid).wait_recv()
                    send_q(k, 1, z0).wait_recv()
                    add_up(
                        own[k].at[pid],
                        [own[k].at[pid], part[k].at[pid], land_q[k].at[1, z0]],
                        rows[k],
                    )
                    send_p(k, z0).start()

        def sources_of(k, z0):
            pid = place.piece(routes[k], 0, 0, z0)
            send_c(k, pid).wait_recv()
            send_q(k, 0, z0).wait_recv()
            sources = [own[k].at[pid], part[k].at[pid], land_q[k].at[0, z0]]
            if routes[k][0] is not None:
                send_p(k, z0).wait_recv()
                sources.append(land_p[k].at[z0])
            return pid, sources

        def along(z0, above):
            for k in range(count):
                pid, sources = sources_of(k, z0)
                child = place.has_down if above else place.has_up

                @pl.when(child)
                def _():
                    wait_z(k, z0)
                    add_up(own[k].at[pid], sources + [land_z[k].at[z0]], rows[k])

                @pl.when(jnp.logical_not(child))
                def _():
                    add_up(own[k].at[pid], sources, rows[k])

                send_z(k, z0, above).start()

        both_sides(place, depth - 1 - s, leaf)

        if work.count:

            @pl.when(s < work.count)
            def _():
                work.body(s, place.ctx, *work_ins, *work_outs)

        @pl.when(s < depth + 1)
        def _():
            both_sides(place, depth - s, middle)

        @pl.when(depth + 1 - s >= 1)
        def _():
            both_sides(place, depth + 1 - s, along)

        @pl.when(s == depth + 1)
        def _():
            for k in range(count):
                _, sources = sources_of(k, place.z)
                add_up(sums[k], sources, rows[k])

                @pl.when(place.has_down)
                def _():
                    wait_z(k, place.z)
                    add_up(sums[k], [sums[k], land_z[k].at[place.z]], rows[k])

                @pl.when(place.has_up)
                def _():
                    wait_z(k, depth)
                    add_up(sums[k], [sums[k], land_z[k].at[depth]], rows[k])

        return carry

    lax.fori_loop(0, depth + 2, step, 0)
    for item in range(depth + 2, work.count):
        work.body(item, place.ctx, *work_ins, *work_outs)

    def finish(z0, carry):
        for k in range(count):
            send_q(k, 0, z0).wait_send()
            if routes[k][0] is not None:
                send_q(k, 1, z0).wait_send()
                send_p(k, z0).wait_send()

            @pl.when(z0 > place.z)
            def _():
                send_z(k, z0, True).wait_send()

            @pl.when(z0 < place.z)
            def _():
                send_z(k, z0, False).wait_send()

        return carry

    lax.fori_loop(0, depth, finish, 0)

    def finish_partner(pid, carry):
        for k in range(count):
            send_c(k, pid).wait_send()
        return carry

    lax.fori_loop(0, pieces, finish_partner, 0)


def scatter(arrays, chunks, use_x, collective_id, name, work=Work()):
    depth = lax.axis_size("ctx") // 4
    pieces = (4 if use_x else 2) * depth
    total, count = len(arrays), len(chunks)
    dma = pltpu.SemaphoreType.DMA
    shapes = [a.shape[1:] for a in arrays]
    pairs = [a.reshape(pieces, 2, *s) for a, s in zip(arrays, shapes)]
    bf16 = jnp.bfloat16
    return pl.pallas_call(
        functools.partial(scatter_kernel, depth, use_x, chunks, work),
        out_shape=[jax.ShapeDtypeStruct(s, jnp.float32) for s in shapes] + work.shapes,
        in_specs=[pl.BlockSpec(memory_space=pl.ANY)] * total
        + [pl.BlockSpec(memory_space=pltpu.VMEM)] * work.ins,
        out_specs=[pl.BlockSpec(memory_space=pltpu.VMEM)] * (total + work.outs),
        scratch_shapes=[pltpu.VMEM((pieces, *s), bf16) for s in shapes]
        + [pltpu.VMEM((pieces, *s), bf16) for s in shapes]
        + [pltpu.VMEM((2, depth, *s), bf16) for s in shapes]
        + [pltpu.VMEM((depth, *s), bf16) for s in shapes]
        + [pltpu.VMEM((depth + 1, *s), bf16) for s in shapes]
        + [
            dma((total,)),
            dma((count, pieces)),
            dma((count, pieces)),
            dma((count, 2, depth)),
            dma((count, 2, depth)),
            dma((count, depth)),
            dma((count, depth)),
            dma((count, depth)),
            dma((count, depth + 1)),
        ],
        compiler_params=pltpu.CompilerParams(
            collective_id=collective_id, has_side_effects=True, vmem_limit_bytes=VMEM_LIMIT
        ),
        name=name,
    )(*pairs, *work.arrays)


def padded(rows, multiple=16):
    return -(-rows // multiple) * multiple


def pad_rows(rows, total):
    return jnp.pad(rows, ((0, total - rows.shape[0]), (0, 0)))


XY, YX, ONLY_Y = ("x", "y"), ("y", "x"), (None, "y")
def halves(values, split_count):
    return values.reshape(values.shape[0], split_count, values.shape[1] // split_count)


def forward_dot(values, weights):
    split_count = weights.shape[0]
    part = values.shape[1] // split_count
    total = None
    for i in range(split_count):
        term = lax.dot_general(
            values[:, i * part : (i + 1) * part],
            weights[i],
            (((1,), (1,)), ((), ())),
            preferred_element_type=jnp.float32,
        )
        total = term if total is None else total + term
    return total


def backward_dot(grads, weights):
    return jnp.concatenate(
        [
            jnp.dot(grads, weights[i], preferred_element_type=jnp.float32)
            for i in range(weights.shape[0])
        ],
        axis=-1,
    )


def terms_kernel(grads, values, out):
    for i in range(values.shape[0]):
        out[i] = lax.dot_general(
            grads[...], values[i], (((0,), (0,)), ((), ())), preferred_element_type=jnp.float32
        ).astype(out.dtype)


def weight_terms(grads, values, split_count):
    rows, width = grads.shape
    values = jnp.transpose(halves(values, split_count), (1, 0, 2))
    block = next((b for b in (512, 256, 128) if width % b == 0), width)
    part = values.shape[2]
    return pl.pallas_call(
        terms_kernel,
        out_shape=jax.ShapeDtypeStruct((split_count, width, part), jnp.bfloat16),
        grid=(width // block,),
        in_specs=[
            pl.BlockSpec((rows, block), lambda i: (0, i)),
            pl.BlockSpec(values.shape, lambda i: (0, 0, 0)),
        ],
        out_specs=pl.BlockSpec((split_count, block, part), lambda i: (0, i, 0)),
        compiler_params=pltpu.CompilerParams(vmem_limit_bytes=VMEM_LIMIT),
        cost_estimate=pl.CostEstimate(
            flops=2 * rows * width * part * split_count,
            bytes_accessed=2 * width * part * split_count,
            transcendentals=0,
        ),
        name="weight_terms",
    )(grads, values)


PIECES_PER_BLOCK = 4


def block_scores(step, ctx, kv_ref, group, query):
    _, _, block_len, width = kv_ref.shape
    span = pl.ds(step * PIECES_PER_BLOCK, PIECES_PER_BLOCK)
    kv = kv_ref[span, group].reshape(PIECES_PER_BLOCK * block_len, width)
    scores = (
        lax.dot_general(kv, query, (((1,), (1,)), ((), ())), preferred_element_type=jnp.float32)
        * 0.125
    )
    key_pos = step * kv.shape[0] + lax.broadcasted_iota(jnp.int32, scores.shape, 0)
    query_pos = ctx * block_len + lax.rem(
        lax.broadcasted_iota(jnp.int32, scores.shape, 1), block_len
    )
    return kv, scores, key_pos <= query_pos


def attend_body(group, ctx, kv_ref, query_ref, out_ref, logsum_ref):
    query = query_ref[group]
    rows, width = query.shape

    def body(step, carry):
        peak, total, acc = carry
        kv, scores, allowed = block_scores(step, ctx, kv_ref, group, query)
        scores = jnp.where(allowed, scores, -jnp.inf)
        new_peak = jnp.maximum(peak, jnp.max(scores, axis=0, keepdims=True))
        terms = jnp.exp(scores - new_peak)
        shrink = jnp.exp(peak - new_peak)
        total = total * shrink + jnp.sum(terms, axis=0, keepdims=True)
        acc = acc * shrink + lax.dot_general(
            kv,
            terms.astype(jnp.bfloat16),
            (((0,), (0,)), ((), ())),
            preferred_element_type=jnp.float32,
        )
        return new_peak, total, acc

    peak, total, acc = lax.fori_loop(
        0,
        ctx // PIECES_PER_BLOCK + 1,
        body,
        (
            jnp.full((1, rows), -jnp.inf, jnp.float32),
            jnp.zeros((1, rows), jnp.float32),
            jnp.zeros((width, rows), jnp.float32),
        ),
    )
    out_ref[group] = acc / total
    logsum_ref[group] = peak + jnp.log(total)


def retrace_body(group, ctx, kv_ref, query_ref, grad_ref, logsum_ref, delta_ref, dq_ref, dkv_ref):
    query, grad = query_ref[group], grad_ref[group]
    logsum, delta = logsum_ref[group], delta_ref[group]
    blocks, _, block_len, width = kv_ref.shape
    needed = ctx // PIECES_PER_BLOCK + 1

    def body(step, dq):
        kv, scores, allowed = block_scores(step, ctx, kv_ref, group, query)
        probs = jnp.where(allowed, jnp.exp(scores - logsum), 0.0)
        grad_probs = lax.dot_general(
            kv, grad, (((1,), (1,)), ((), ())), preferred_element_type=jnp.float32
        )
        grad_scores = (probs * (grad_probs - delta) * 0.125).astype(jnp.bfloat16)
        dkv = jnp.dot(
            probs.astype(jnp.bfloat16), grad, preferred_element_type=jnp.float32
        ) + jnp.dot(grad_scores, query, preferred_element_type=jnp.float32)
        span = pl.ds(step * PIECES_PER_BLOCK, PIECES_PER_BLOCK)
        dkv_ref[span, group] = dkv.astype(jnp.bfloat16).reshape(PIECES_PER_BLOCK, block_len, width)
        return dq + lax.dot_general(
            grad_scores, kv, (((0,), (0,)), ((), ())), preferred_element_type=jnp.float32
        )

    dq_ref[group] = lax.fori_loop(0, needed, body, jnp.zeros(query.shape, jnp.float32))

    def clear(step, carry):
        span = pl.ds(step * PIECES_PER_BLOCK, PIECES_PER_BLOCK)
        dkv_ref[span, group] = jnp.zeros((PIECES_PER_BLOCK, block_len, width), jnp.bfloat16)
        return carry

    lax.fori_loop(needed, blocks // PIECES_PER_BLOCK, clear, 0)


def wait_all(copies):
    for copy in copies:
        copy.wait()


def turned(left, right):
    return lax.dot_general(left, right, (((1,), (1,)), ((), ())), preferred_element_type=jnp.float32)


def plain(left, right):
    return jnp.dot(left, right, preferred_element_type=jnp.float32)


def mlp_kernel(
    real_width,
    attended_ref, resid_ref, grad_ref, gain_ref, out_hbm, gate_hbm, up_hbm, down_hbm,
    output_ref, grad_resid_ref, grad_attended_ref, term_gain_ref,
    terms_out_hbm, terms_gate_hbm, terms_up_hbm, terms_down_hbm,
    out_w, gate_w, up_w, down_w, terms_out, terms_gate, terms_up, terms_down,
    resid2_ref, normal_ref, gate_ref, up_ref, hidden_ref, grad_gate_ref, grad_up_ref, branch_ref,
    load_sem, store_sem,
):
    splits, _, part = gate_w.shape
    span = down_w.shape[2]
    width = out_w.shape[1]
    loads = [
        pltpu.make_async_copy(src, dst, load_sem.at[i])
        for i, (src, dst) in enumerate(
            ((out_hbm, out_w), (gate_hbm, gate_w), (up_hbm, up_w), (down_hbm, down_w))
        )
    ]
    for load in loads:
        load.start()

    def slice_of(i, size=part):
        return slice(i * size, (i + 1) * size)

    loads[0].wait()
    resid2 = resid_ref[...]
    for i in range(splits):
        resid2 = resid2 + turned(attended_ref[:, slice_of(i)], out_w[i])
    scale = lax.rsqrt(jnp.sum(resid2 * resid2, axis=-1, keepdims=True) / real_width + EPSILON)
    resid2_ref[...] = resid2
    normal_ref[...] = (resid2 * scale * gain_ref[...]).astype(jnp.bfloat16)
    loads[1].wait()
    loads[2].wait()
    block = 256 if span % 256 == 0 else 128
    steps = span // block

    def lanes(i, step):
        return pl.ds(pl.multiple_of(i * span + step * block, block), block)

    def forward(index, carry):
        cols = pl.ds(pl.multiple_of(index * block, block), block)
        gate = up = None
        for i in range(splits):
            normal = normal_ref[:, slice_of(i)]
            gate_term = turned(normal, gate_w[i, cols, :])
            up_term = turned(normal, up_w[i, cols, :])
            gate = gate_term if gate is None else gate + gate_term
            up = up_term if up is None else up + up_term
        gate_ref[:, cols] = gate
        up_ref[:, cols] = up
        hidden_ref[:, cols] = (gate * jax.nn.sigmoid(gate) * up).astype(jnp.bfloat16)
        return carry

    lax.fori_loop(0, splits * steps, forward, 0)
    loads[3].wait()
    total = resid2_ref[...]
    for i in range(splits):
        total = total + turned(hidden_ref[:, slice_of(i, span)], down_w[i])
    output_ref[...] = total.astype(jnp.bfloat16)

    for i in range(splits):

        def backward(step, carry):
            inner = pl.ds(pl.multiple_of(step * block, block), block)
            cols = lanes(i, step)
            grad_hidden = plain(grad_ref[...], down_w[i, :, inner])
            gate, up = gate_ref[:, cols], up_ref[:, cols]
            sigma = jax.nn.sigmoid(gate)
            grad_up_ref[:, cols] = (grad_hidden * gate * sigma).astype(jnp.bfloat16)
            grad_gate_ref[:, cols] = (
                grad_hidden * up * sigma * (1.0 + gate * (1.0 - sigma))
            ).astype(jnp.bfloat16)
            return carry

        lax.fori_loop(0, steps, backward, 0)

    def terms(rows, left_ref, right_ref, size, target):
        rows_block = 256 if rows % 256 == 0 else 128

        def body(step, carry):
            cols = pl.ds(pl.multiple_of(step * rows_block, rows_block), rows_block)
            left = left_ref[:, cols]
            for i in range(splits):
                target[i, cols, :] = lax.dot_general(
                    left,
                    right_ref[:, slice_of(i, size)],
                    (((0,), (0,)), ((), ())),
                    preferred_element_type=jnp.float32,
                ).astype(jnp.bfloat16)
            return carry

        lax.fori_loop(0, rows // rows_block, body, 0)

    stores = [
        pltpu.make_async_copy(src, dst, store_sem.at[i])
        for i, (src, dst) in enumerate(
            (
                (terms_down, terms_down_hbm),
                (terms_gate, terms_gate_hbm),
                (terms_up, terms_up_hbm),
                (terms_out, terms_out_hbm),
            )
        )
    ]
    terms(width, grad_ref, hidden_ref, span, terms_down)
    stores[0].start()
    terms(splits * span, grad_gate_ref, normal_ref, part, terms_gate)
    stores[1].start()
    terms(splits * span, grad_up_ref, normal_ref, part, terms_up)
    stores[2].start()

    resid2 = resid2_ref[...]
    scale = lax.rsqrt(jnp.sum(resid2 * resid2, axis=-1, keepdims=True) / real_width + EPSILON)
    pulls, inner_sum = [], 0.0
    for i in range(splits):
        pull = plain(grad_gate_ref[...], gate_w[i]) + plain(grad_up_ref[...], up_w[i])
        resid_part = resid2_ref[:, slice_of(i)]
        term_gain_ref[:, slice_of(i)] = jnp.sum(pull * resid_part * scale, axis=0, keepdims=True)
        pull = pull * gain_ref[:, slice_of(i)]
        inner_sum = inner_sum + jnp.sum(pull * resid_part, axis=-1, keepdims=True)
        pulls.append(pull)
    shift = scale * scale * scale * inner_sum / real_width
    for i in range(splits):
        grad_resid = (
            grad_ref[:, slice_of(i)].astype(jnp.float32)
            + pulls[i] * scale
            - resid2_ref[:, slice_of(i)] * shift
        )
        grad_resid_ref[:, slice_of(i)] = grad_resid
        branch_ref[:, slice_of(i)] = grad_resid.astype(jnp.bfloat16)
    for i in range(splits):
        grad_attended_ref[:, slice_of(i)] = plain(branch_ref[...], out_w[i]).astype(jnp.bfloat16)
    terms(width, branch_ref, attended_ref, part, terms_out)
    stores[3].start()
    wait_all(stores)


def mlp(attended, resid1, grad_rows, gain, out_w, gate_w, up_w, down_w, real_width):
    rows, width = resid1.shape
    hidden_width = gate_w.shape[1]
    f32, bf16 = jnp.float32, jnp.bfloat16
    weights = [out_w, gate_w, up_w, down_w]
    vmem, anywhere = pl.BlockSpec(memory_space=pltpu.VMEM), pl.BlockSpec(memory_space=pl.ANY)
    kept = [pltpu.VMEM(w.shape, bf16) for w in weights]
    return pl.pallas_call(
        functools.partial(mlp_kernel, real_width),
        out_shape=[
            jax.ShapeDtypeStruct((rows, width), bf16),
            jax.ShapeDtypeStruct((rows, width), f32),
            jax.ShapeDtypeStruct(attended.shape, bf16),
            jax.ShapeDtypeStruct((1, width), f32),
        ]
        + [jax.ShapeDtypeStruct(w.shape, bf16) for w in weights],
        in_specs=[vmem] * 4 + [anywhere] * 4,
        out_specs=[vmem] * 4 + [anywhere] * 4,
        scratch_shapes=kept
        + kept
        + [
            pltpu.VMEM((rows, width), f32),
            pltpu.VMEM((rows, width), bf16),
            pltpu.VMEM((rows, hidden_width), f32),
            pltpu.VMEM((rows, hidden_width), f32),
            pltpu.VMEM((rows, hidden_width), bf16),
            pltpu.VMEM((rows, hidden_width), bf16),
            pltpu.VMEM((rows, hidden_width), bf16),
            pltpu.VMEM((rows, width), bf16),
            pltpu.SemaphoreType.DMA((4,)),
            pltpu.SemaphoreType.DMA((4,)),
        ],
        compiler_params=pltpu.CompilerParams(vmem_limit_bytes=VMEM_LIMIT),
        name="mlp",
    )(attended, resid1, grad_rows, gain, *weights)


def local(
    inputs, grad_output, w_query, w_key, w_value, w_out, w_gate, w_up, w_down, gain_attn, gain_mlp
):
    seq_count, block_len, model_width = inputs.shape
    row_count = seq_count * block_len
    split_count = lax.axis_size("fsdp")
    cycle_size = lax.axis_size("ctx")
    cycle_index = lax.axis_index("ctx")
    groups = KV_HEADS
    head_size = HEAD
    repeat_count = HEADS // KV_HEADS
    kv_width = groups * head_size
    positions = cycle_index * block_len + jnp.arange(block_len, dtype=jnp.int32)
    cosine, sine_table = tables(positions, head_size)
    cosine = jnp.tile(cosine, (seq_count, 1))
    sine_table = jnp.tile(sine_table, (seq_count, 1))
    wide_q, wide_k, wide_v = w_query.shape[1], w_key.shape[1], w_value.shape[1]
    wide_o, wide_g = w_out.shape[1], w_gate.shape[1]
    pad_q, pad_k, pad_v = padded(wide_q), padded(wide_k + 1), padded(wide_v)
    pad_o, pad_g = padded(wide_o), padded(wide_g)
    part_width = w_query.shape[0]
    wide_part = part_width // wide_o * pad_o
    gain_size = gain_attn.shape[0]

    def spread(weight, wide, pad):
        pieces = weight.reshape(-1, wide, weight.shape[1])
        pieces = jnp.pad(pieces, ((0, 0), (0, pad - wide), (0, 0)))
        return pieces.reshape(-1, weight.shape[1]).T

    def gathered_spread(total, wide, pad):
        pieces = total.T.reshape(-1, pad, total.shape[0])
        return pieces[:, :wide].reshape(-1, total.shape[0])

    def open_up(values, wide, start):
        pieces = values.reshape(values.shape[0], cycle_size, -1)
        return pieces[:, :, start : start + wide].reshape(values.shape[0], cycle_size * wide)

    def close_up(values):
        pieces = values.reshape(row_count, cycle_size, wide_o)
        return jnp.pad(pieces, ((0, 0), (0, 0), (0, pad_o - wide_o))).reshape(row_count, -1)

    def model(weight):
        return spread(weight, wide_o, pad_o)

    gain_row = jnp.pad(
        jnp.concatenate([jnp.pad(g, (0, pad_o - gain_size)) for g in (gain_attn, gain_mlp)]),
        (0, wide_part - 2 * pad_o),
    )[None, :]
    first_piece = jnp.concatenate(
        [
            pad_rows(model(w_query), pad_q),
            pad_rows(jnp.concatenate([model(w_key), gain_row], axis=0), pad_k),
            pad_rows(model(w_value), pad_v),
        ],
        axis=0,
    )
    first_chunks = cut(0, first_piece.shape[0], 4, (YX, XY))
    (first,) = gather([first_piece], first_chunks, True, 0, "gather_first")
    gain_rows = first[:cycle_size, pad_q + wide_k, : 2 * pad_o]
    gain_first = gain_rows[:, :pad_o].reshape(1, -1).astype(jnp.float32)
    gain_second = gain_rows[:, pad_o:].reshape(1, -1).astype(jnp.float32)
    first = first.reshape(split_count, -1, wide_part)

    resid1 = close_up(inputs.reshape(row_count, model_width)).astype(jnp.float32)
    scale1 = lax.rsqrt(jnp.sum(resid1 * resid1, axis=-1, keepdims=True) / model_width + EPSILON)
    normal1 = (resid1 * scale1 * gain_first).astype(jnp.bfloat16)
    raw = forward_dot(normal1, first)
    query_raw = open_up(raw, wide_q, 0).reshape(row_count, HEADS, head_size)
    query_rot = rotate(query_raw, cosine, sine_table).astype(jnp.bfloat16)
    key_raw = open_up(raw, wide_k, pad_q).reshape(row_count, groups, head_size)
    key_rows = rotate(key_raw, cosine, sine_table).astype(jnp.bfloat16)
    value_rows = open_up(raw, wide_v, pad_q + pad_k).astype(jnp.bfloat16)
    value_rows = value_rows.reshape(row_count, groups, head_size)
    pair_rows = jnp.transpose(jnp.concatenate([key_rows, value_rows], axis=-1), (1, 0, 2))
    pair_chunks = cut(0, groups * row_count, 2, (ONLY_Y,))
    (pair_all,) = gather(
        [pair_rows.reshape(groups * row_count, 2 * head_size)],
        pair_chunks,
        False,
        1,
        "gather_pairs",
    )
    pair_all = pair_all.reshape(cycle_size, groups, row_count, 2 * head_size)

    def by_group(values):
        values = values.reshape(row_count, groups, repeat_count, head_size)
        return jnp.transpose(values, (1, 2, 0, 3)).reshape(groups, repeat_count * row_count, head_size)

    query_grouped = jnp.pad(by_group(query_rot), ((0, 0), (0, 0), (0, head_size)))
    width = repeat_count * row_count
    out_piece = jnp.pad(w_out.T, ((0, pad_o - wide_o), (0, wide_part - part_width)))
    rest_chunks = (
        cut(0, pad_o, 2, (XY, YX))
        + cut(1, pad_g, 1, (XY,))
        + cut(2, pad_g, 1, (YX,))
        + cut(3, pad_o, 2, (XY, YX))
    )
    out_w, gate_w, up_w, down_w, attended_turned, logsum = gather(
        [
            out_piece,
            pad_rows(model(w_gate), pad_g),
            pad_rows(model(w_up), pad_g),
            pad_rows(spread(w_down, wide_g, pad_g), pad_o),
        ],
        rest_chunks,
        True,
        4,
        "gather_rest_attend",
        Work(
            groups,
            attend_body,
            [pair_all, query_grouped],
            [
                jax.ShapeDtypeStruct((groups, 2 * head_size, width), jnp.float32),
                jax.ShapeDtypeStruct((groups, 1, width), jnp.float32),
            ],
        ),
    )
    out_w, gate_w, up_w, down_w = (
        w.reshape(split_count, -1, w.shape[-1]) for w in (out_w, gate_w, up_w, down_w)
    )
    attended_wide = jnp.transpose(
        attended_turned[:, head_size:].reshape(groups, head_size, repeat_count, row_count),
        (3, 0, 2, 1),
    )
    attended = jnp.pad(
        attended_wide.astype(jnp.bfloat16).reshape(row_count, split_count, part_width),
        ((0, 0), (0, 0), (0, wide_part - part_width)),
    ).reshape(row_count, -1)
    grad_rows = close_up(grad_output.reshape(row_count, model_width))
    output, grad_resid2, grad_attended, term_gain2, terms_out, terms_gate, terms_up, terms_down = mlp(
        attended, resid1, grad_rows, gain_second, out_w, gate_w, up_w, down_w, model_width
    )
    grad_attended = grad_attended.reshape(row_count, split_count, wide_part)[..., :part_width]
    grad_attended = grad_attended.reshape(row_count, -1)
    row_delta = jnp.sum(
        grad_attended.astype(jnp.float32).reshape(attended_wide.shape) * attended_wide, axis=-1
    )
    row_delta = jnp.transpose(row_delta, (1, 2, 0)).reshape(groups, 1, width)
    grad_grouped = jnp.pad(by_group(grad_attended), ((0, 0), (0, 0), (head_size, 0)))

    def pieces_of(terms):
        return terms.reshape(split_count * cycle_size, -1, terms.shape[-1])

    sum_out, sum_gate, sum_up, sum_down, grad_query_acc, grad_pair_all = scatter(
        [pieces_of(t) for t in (terms_out, terms_gate, terms_up, terms_down)],
        rest_chunks,
        True,
        3,
        "scatter_rest_retrace",
        Work(
            groups,
            retrace_body,
            [pair_all, query_grouped, grad_grouped, logsum, row_delta],
            [
                jax.ShapeDtypeStruct(query_grouped.shape, jnp.float32),
                jax.ShapeDtypeStruct(pair_all.shape, jnp.bfloat16),
            ],
        ),
    )
    (grad_pair_own,) = scatter(
        [grad_pair_all.reshape(cycle_size, groups * row_count, 2 * head_size)],
        pair_chunks,
        False,
        2,
        "scatter_pairs",
    )
    grad_pair_own = jnp.transpose(
        grad_pair_own.reshape(groups, row_count, 2 * head_size), (1, 0, 2)
    )
    grad_query_rows = jnp.transpose(
        grad_query_acc[..., :head_size].reshape(groups, repeat_count, row_count, head_size),
        (2, 0, 1, 3),
    ).reshape(row_count, HEADS, head_size)
    grad_query = (
        unrotate(grad_query_rows, cosine, sine_table)
        .reshape(row_count, HEADS * head_size)
        .astype(jnp.bfloat16)
    )
    grad_keys = (
        unrotate(grad_pair_own[..., :head_size], cosine, sine_table)
        .reshape(row_count, kv_width)
        .astype(jnp.bfloat16)
    )
    grad_values = grad_pair_own[..., head_size:].astype(jnp.bfloat16).reshape(row_count, kv_width)

    def shaped(values, wide, pad):
        pieces = values.reshape(row_count, cycle_size, wide)
        return jnp.pad(pieces, ((0, 0), (0, 0), (0, pad - wide)))

    grad_raw = jnp.concatenate(
        [
            shaped(grad_query, wide_q, pad_q),
            shaped(grad_keys, wide_k, pad_k),
            shaped(grad_values, wide_v, pad_v),
        ],
        axis=-1,
    ).reshape(row_count, -1)
    grad_norm1 = backward_dot(grad_raw, first)
    term_gain1 = jnp.sum(grad_norm1 * resid1 * scale1, axis=0)
    pull = grad_norm1 * gain_first
    shift = scale1**3 * jnp.sum(pull * resid1, axis=-1, keepdims=True) / model_width
    grad_input = (grad_resid2 + pull * scale1 - resid1 * shift).astype(jnp.bfloat16)
    gain_terms = jnp.concatenate(
        [term_gain1.reshape(cycle_size, pad_o), term_gain2.reshape(cycle_size, pad_o)], axis=-1
    ).astype(jnp.bfloat16)
    terms_first = weight_terms(grad_raw, normal1, split_count)
    terms_first = terms_first.reshape(split_count, cycle_size, -1, wide_part)
    terms_first = terms_first.at[:, :, pad_q + wide_k, : 2 * pad_o].set(gain_terms[None])
    terms_first = terms_first.reshape(split_count * cycle_size, -1, wide_part)
    (sum_first,) = scatter([terms_first], first_chunks, True, 5, "scatter_first")
    start_k, start_v = pad_q, pad_q + pad_k
    gain_sums = sum_first[pad_q + wide_k]

    def model_sum(total):
        return gathered_spread(total, wide_o, pad_o)

    def rows_of(values):
        return open_up(values, wide_o, 0).reshape(seq_count, block_len, model_width)

    return (
        rows_of(output),
        rows_of(grad_input),
        model_sum(sum_first[:wide_q]),
        model_sum(sum_first[start_k : start_k + wide_k]),
        model_sum(sum_first[start_v : start_v + wide_v]),
        sum_out[:wide_o, :part_width].T,
        model_sum(sum_gate[:wide_g]),
        model_sum(sum_up[:wide_g]),
        gathered_spread(sum_down[:wide_o], wide_g, pad_g),
        gain_sums[:gain_size],
        gain_sums[pad_o : pad_o + gain_size],
    )


def solution(mesh):
    rows, weight, gain = P("fsdp", "ctx", None), P("fsdp", "ctx"), P("ctx")
    return jax.shard_map(
        local,
        mesh=mesh,
        in_specs=(rows, rows) + (weight,) * 7 + (gain, gain),
        out_specs=(rows, rows) + (weight,) * 7 + (gain, gain),
        check_vma=False,
    )
```

```python
import functools

import jax
import jax.numpy as jnp
from jax import lax
from jax.experimental import pallas as pl
from jax.experimental.pallas import tpu as pltpu
from jax.sharding import PartitionSpec as P

HEADS = 15
KV_HEADS = 5
HEAD = 64

EPSILON = 1e-05
ROPE_THETA = 100000.0
MESH = pl.DeviceIdType.MESH
VMEM_LIMIT = 67_000_000


def tables(positions, head_size):
    half_size = head_size // 2
    frequency = ROPE_THETA ** (-jnp.arange(half_size, dtype=jnp.float32) * 2.0 / head_size)
    angles = positions.astype(jnp.float32)[:, None] * frequency[None, :]
    return (jnp.cos(angles), jnp.sin(angles))


def rotate(values, cosine, sine_table):
    half_size = values.shape[-1] // 2
    first_half = values[..., :half_size]
    second = values[..., half_size:]
    cosine = cosine[:, None, :]
    sine_table = sine_table[:, None, :]
    return jnp.concatenate(
        [first_half * cosine - second * sine_table, second * cosine + first_half * sine_table],
        axis=-1,
    )


def unrotate(values, cosine, sine_table):
    return rotate(values, cosine, -sine_table)


class Place:
    def __init__(self, depth, use_x):
        self.depth = depth
        self.use_x = use_x
        self.f = lax.axis_index("fsdp")
        self.ctx = lax.axis_index("ctx")
        self.c = self.ctx % 2
        self.y = (self.ctx // 2) % 2
        self.z = self.ctx // 4
        self.has_up = self.z < depth - 1
        self.has_down = self.z > 0

    def device(self, way):
        if way == "c":
            return (self.f, self.ctx + 1 - 2 * self.c)
        if way == "y":
            return (self.f, self.ctx + 2 - 4 * self.y)
        if way == "x":
            return (1 - self.f, self.ctx)
        return (self.f, self.ctx + (4 if way == "up" else -4))

    def piece(self, route, rel_p, rel_q, z):
        rel = {route[1]: rel_q}
        if route[0] is not None:
            rel[route[0]] = rel_p
        y0 = 1 - self.y if rel.get("y", 0) else self.y
        pid = z * 2 + y0
        if self.use_x:
            x0 = 1 - self.f if rel.get("x", 0) else self.f
            pid = pid + x0 * 2 * self.depth
        return pid

    def barrier(self):
        sem = pltpu.get_barrier_semaphore()
        ways = ["c", "y"] + (["x"] if self.use_x else [])
        for way in ways:
            pl.semaphore_signal(sem, inc=1, device_id=self.device(way), device_id_type=MESH)

        @pl.when(self.has_up)
        def _():
            pl.semaphore_signal(sem, inc=1, device_id=self.device("up"), device_id_type=MESH)

        @pl.when(self.has_down)
        def _():
            pl.semaphore_signal(sem, inc=1, device_id=self.device("down"), device_id_type=MESH)

        peers = len(ways) + self.has_up.astype(jnp.int32) + self.has_down.astype(jnp.int32)
        pl.semaphore_wait(sem, peers)


def both_sides(place, distance, body):
    high = place.z + distance
    low = place.z - distance

    @pl.when((distance >= 0) & (high < place.depth))
    def _():
        body(high, True)

    @pl.when((distance >= 1) & (low >= 0))
    def _():
        body(low, False)


class Chunk:
    def __init__(self, array, start, rows, route):
        self.array, self.start, self.rows, self.route = array, start, rows, route[:2]
        self.late = len(route) > 2
        self.span = pl.ds(start, rows)


def cut(array, rows, parts, routes):
    size = padded(-(-rows // parts))
    starts = range(0, rows, size)
    return [
        Chunk(array, start, min(size, rows - start), routes[i % len(routes)])
        for i, start in enumerate(starts)
    ]


def gather_kernel(depth, use_x, chunks, work, *refs):
    total, count = 1 + max(chunk.array for chunk in chunks), len(chunks)
    routes = [chunk.route for chunk in chunks]
    early = [k for k in range(count) if not chunks[k].late]
    late = [k for k in range(count) if chunks[k].late]
    ins, work_ins, refs = refs[:total], refs[total : total + work.ins], refs[total + work.ins :]
    outs, work_outs, refs = refs[:total], refs[total : total + work.outs], refs[total + work.outs :]
    recv, send_z, send_p, send_q, send_c, local_sem, send_l = refs
    place = Place(depth, use_x)
    place.barrier()

    def landing(k, slot):
        return outs[chunks[k].array].at[slot, chunks[k].span]

    def copy(k, pid, send_sem, way, src=None):
        slot = pid * 2 + place.c
        return pltpu.make_async_remote_copy(
            src_ref=landing(k, slot) if src is None else src,
            dst_ref=landing(k, slot),
            send_sem=send_sem,
            recv_sem=recv.at[k, slot],
            device_id=place.device(way),
            device_id_type=MESH,
        )

    def forward_late(k, rel_p, rel_q, z0, up, src=None):
        pid = place.piece(routes[k], rel_p, rel_q, z0)
        sem = send_l.at[late.index(k), 2 * rel_p + rel_q, 0 if up else 1, z0]
        return copy(k, pid, sem, "up" if up else "down", src)

    def both_late(k, rel_p, rel_q):
        @pl.when(place.has_up)
        def _():
            forward_late(k, rel_p, rel_q, place.z, True).start()

        @pl.when(place.has_down)
        def _():
            forward_late(k, rel_p, rel_q, place.z, False).start()

    def forward_z(k, z0, up, src=None):
        if chunks[k].late:
            return forward_late(k, 0, 0, z0, up, src)
        pid = place.piece(routes[k], 0, 0, z0)
        return copy(k, pid, send_z.at[k, 0 if up else 1, z0], "up" if up else "down", src)

    def forward_p(k, z0, src=None):
        return copy(k, place.piece(routes[k], 0, 0, z0), send_p.at[k, z0], routes[k][0], src)

    def forward_q(k, rel_p, z0, src=None):
        pid = place.piece(routes[k], rel_p, 0, z0)
        return copy(k, pid, send_q.at[k, rel_p, z0], routes[k][1], src)

    def forward_c(k, pid, src=None):
        return copy(k, pid, send_c.at[k, pid], "c", src)

    def arrived(k, pid):
        copy(k, pid, send_c.at[k, pid], "c").wait_recv()

    own = []
    for k in range(count):
        pid = place.piece(routes[k], 0, 0, place.z)
        src = ins[chunks[k].array].at[chunks[k].span]

        @pl.when(place.has_up)
        def _():
            forward_z(k, place.z, True, src).start()

        @pl.when(place.has_down)
        def _():
            forward_z(k, place.z, False, src).start()

        if routes[k][0] is not None:
            forward_p(k, place.z, src).start()
        forward_q(k, 0, place.z, src).start()
        forward_c(k, pid, src).start()
        mine = pltpu.make_async_copy(src, landing(k, pid * 2 + place.c), local_sem.at[k])
        mine.start()
        own.append(mine)

    for k in late:
        pid = place.piece(routes[k], 1, 0, place.z)
        arrived(k, pid)
        forward_q(k, 1, place.z).start()
        both_late(k, 1, 0)
        forward_c(k, pid).start()
    for k in late:
        for rel_p in (0, 1):
            pid = place.piece(routes[k], rel_p, 1, place.z)
            arrived(k, pid)
            both_late(k, rel_p, 1)
            forward_c(k, pid).start()

    def step(d, carry):
        def from_z(z0, above):
            for k in late:
                for rel_p, rel_q in ((0, 0), (1, 0), (0, 1), (1, 1)):
                    pid = place.piece(routes[k], rel_p, rel_q, z0)
                    arrived(k, pid)

                    @pl.when(place.has_down if above else place.has_up)
                    def _():
                        forward_late(k, rel_p, rel_q, z0, not above).start()

                    forward_c(k, pid).start()
            for k in early:
                pid = place.piece(routes[k], 0, 0, z0)
                arrived(k, pid)
                if above:

                    @pl.when(place.has_down)
                    def _():
                        forward_z(k, z0, False).start()

                else:

                    @pl.when(place.has_up)
                    def _():
                        forward_z(k, z0, True).start()

                if routes[k][0] is not None:
                    forward_p(k, z0).start()
                forward_q(k, 0, z0).start()
                forward_c(k, pid).start()

        def from_p(z0, above):
            for k in early:
                if routes[k][0] is not None:
                    pid = place.piece(routes[k], 1, 0, z0)
                    arrived(k, pid)
                    forward_q(k, 1, z0).start()
                    forward_c(k, pid).start()

        def from_q(rel_p, z0, above):
            for k in early:
                if routes[k][0] is not None or not rel_p:
                    pid = place.piece(routes[k], rel_p, 1, z0)
                    arrived(k, pid)
                    forward_c(k, pid).start()

        @pl.when((d >= 1) & (d < depth))
        def _():
            both_sides(place, d, from_z)

        both_sides(place, d - 1, from_p)
        both_sides(place, d - 1, functools.partial(from_q, 0))
        both_sides(place, d - 2, functools.partial(from_q, 1))

        if work.count:

            @pl.when(d - 1 < work.count)
            def _():
                work.body(d - 1, place.ctx, *work_ins, *work_outs)

        return carry

    lax.fori_loop(1, depth + 2, step, 0)
    for item in range(depth + 1, work.count):
        work.body(item, place.ctx, *work_ins, *work_outs)

    def finish(z0, carry):
        for k in late:
            for rel_p, rel_q in ((0, 0), (1, 0), (0, 1), (1, 1)):

                @pl.when(place.has_up & (z0 <= place.z))
                def _():
                    forward_late(k, rel_p, rel_q, z0, True).wait_send()

                @pl.when(place.has_down & (z0 >= place.z))
                def _():
                    forward_late(k, rel_p, rel_q, z0, False).wait_send()

            @pl.when(z0 == place.z)
            def _():
                forward_p(k, z0).wait_send()
                forward_q(k, 0, z0).wait_send()
                forward_q(k, 1, z0).wait_send()

        for k in early:

            @pl.when(place.has_up & (z0 <= place.z))
            def _():
                forward_z(k, z0, True).wait_send()

            @pl.when(place.has_down & (z0 >= place.z))
            def _():
                forward_z(k, z0, False).wait_send()

            if routes[k][0] is not None:
                forward_p(k, z0).wait_send()
                forward_q(k, 1, z0).wait_send()
            forward_q(k, 0, z0).wait_send()
        return carry

    lax.fori_loop(0, depth, finish, 0)

    def finish_partner(pid, carry):
        for k in range(count):
            forward_c(k, pid).wait_send()
            slot = pid * 2 + 1 - place.c
            pltpu.make_async_remote_copy(
                src_ref=landing(k, slot),
                dst_ref=landing(k, slot),
                send_sem=send_c.at[k, pid],
                recv_sem=recv.at[k, slot],
                device_id=place.device("c"),
                device_id_type=MESH,
            ).wait_recv()
        return carry

    lax.fori_loop(0, (4 if use_x else 2) * depth, finish_partner, 0)
    for mine in own:
        mine.wait()


class Work:
    def __init__(self, count=0, body=None, arrays=(), shapes=()):
        self.count, self.body, self.arrays, self.shapes = count, body, arrays, list(shapes)
        self.ins, self.outs = len(arrays), len(self.shapes)


def gather(arrays, chunks, use_x, collective_id, name, work=Work()):
    depth = lax.axis_size("ctx") // 4
    pieces = (4 if use_x else 2) * depth
    total, count = len(arrays), len(chunks)
    dma = pltpu.SemaphoreType.DMA
    return pl.pallas_call(
        functools.partial(gather_kernel, depth, use_x, chunks, work),
        out_shape=[jax.ShapeDtypeStruct((2 * pieces, *a.shape), a.dtype) for a in arrays]
        + work.shapes,
        in_specs=[pl.BlockSpec(memory_space=pltpu.VMEM)] * (total + work.ins),
        out_specs=[pl.BlockSpec(memory_space=pl.ANY)] * total
        + [pl.BlockSpec(memory_space=pltpu.VMEM)] * work.outs,
        scratch_shapes=[
            dma((count, 2 * pieces)),
            dma((count, 2, depth)),
            dma((count, depth)),
            dma((count, 2, depth)),
            dma((count, pieces)),
            dma((count,)),
            dma((max(1, sum(chunk.late for chunk in chunks)), 4, 2, depth)),
        ],
        compiler_params=pltpu.CompilerParams(
            collective_id=collective_id, has_side_effects=True, vmem_limit_bytes=VMEM_LIMIT
        ),
        name=name,
    )(*arrays, *work.arrays)


def add_up(dst, sources, rows):
    block = 32 if rows % 32 == 0 else 16

    def body(i, carry):
        span = pl.ds(pl.multiple_of(i * block, block), block)
        total = sources[0][span, :].astype(jnp.float32)
        for source in sources[1:]:
            total = total + source[span, :].astype(jnp.float32)
        dst[span, :] = total.astype(dst.dtype)
        return carry

    lax.fori_loop(0, rows // block, body, 0)


def scatter_kernel(depth, use_x, chunks, work, *refs):
    total, count = 1 + max(chunk.array for chunk in chunks), len(chunks)
    routes = [chunk.route for chunk in chunks]
    early = [k for k in range(count) if not chunks[k].late]
    late = [k for k in range(count) if chunks[k].late]
    ins, work_ins, refs = refs[:total], refs[total : total + work.ins], refs[total + work.ins :]
    outs, work_outs, refs = refs[:total], refs[total : total + work.outs], refs[total + work.outs :]
    whole = [refs[i * total : (1 + i) * total] for i in range(5)]
    land_l, refs = refs[5 * total : 5 * total + len(late)], refs[5 * total + len(late) :]
    load_sem, c_send, c_recv, q_send, q_recv, p_send, p_recv, z_send, z_recv, l_send, l_recv = refs

    class View:
        def __init__(self, ref, span):
            self.ref, self.span = ref, span

        @property
        def at(self):
            return self

        def __getitem__(self, index):
            index = index if isinstance(index, tuple) else (index,)
            return self.ref.at[(*index, self.span)]

    own, part, land_q, land_p, land_z = (
        [View(group[chunk.array], chunk.span) for chunk in chunks] for group in whole
    )
    sums = [outs[chunk.array].at[chunk.span] for chunk in chunks]
    place = Place(depth, use_x)
    pieces = (4 if use_x else 2) * depth
    rows = [chunk.rows for chunk in chunks]

    def load(k):
        return pltpu.make_async_copy(ins[k].at[:, place.c], whole[0][k], load_sem.at[k])

    for k in range(total):
        load(k).start()
    place.barrier()

    def remote(src, dst, send_sem, recv_sem, way):
        return pltpu.make_async_remote_copy(
            src_ref=src,
            dst_ref=dst,
            send_sem=send_sem,
            recv_sem=recv_sem,
            device_id=place.device(way),
            device_id_type=MESH,
        )

    def send_c(k, pid):
        return remote(
            ins[chunks[k].array].at[pid, 1 - place.c, chunks[k].span], part[k].at[pid], c_send.at[k, pid], c_recv.at[k, pid], "c"
        )

    def send_q(k, rel_p, z0):
        pid = place.piece(routes[k], rel_p, 1, z0)
        return remote(
            own[k].at[pid],
            land_q[k].at[rel_p, z0],
            q_send.at[k, rel_p, z0],
            q_recv.at[k, rel_p, z0],
            routes[k][1],
        )

    def send_p(k, z0):
        pid = place.piece(routes[k], 1, 0, z0)
        return remote(
            own[k].at[pid], land_p[k].at[z0], p_send.at[k, z0], p_recv.at[k, z0], routes[k][0]
        )

    def send_z(k, z0, up):
        pid = place.piece(routes[k], 0, 0, z0)
        if up:
            target = z0
        else:
            target = jnp.where(z0 == place.z - 1, depth, z0)
        return remote(
            own[k].at[pid],
            land_z[k].at[target],
            z_send.at[k, z0],
            z_recv.at[k, target],
            "up" if up else "down",
        )

    def send_late(k, rel_p, rel_q, z0, up):
        target = z0 if up else jnp.where(z0 == place.z - 1, depth, z0)
        i, rel = late.index(k), 2 * rel_p + rel_q
        return remote(
            own[k].at[place.piece(routes[k], rel_p, rel_q, z0)],
            land_l[i].at[rel, target],
            l_send.at[i, rel, z0],
            l_recv.at[i, rel, target],
            "up" if up else "down",
        )

    def late_child(k, rel_p, rel_q, index):
        i, rel = late.index(k), 2 * rel_p + rel_q
        child = land_l[i].at[rel, index]
        pltpu.make_async_copy(child, child, l_recv.at[i, rel, index]).wait()
        return child

    def add_children(k, rel_p, rel_q, total_ref):
        @pl.when(place.has_down)
        def _():
            add_up(total_ref, [total_ref, late_child(k, rel_p, rel_q, place.z)], rows[k])

        @pl.when(place.has_up)
        def _():
            add_up(total_ref, [total_ref, late_child(k, rel_p, rel_q, depth)], rows[k])

    def late_along(z0, above):
        for k in late:
            for rel_p, rel_q in ((1, 1), (0, 1), (1, 0), (0, 0)):
                pid = place.piece(routes[k], rel_p, rel_q, z0)
                send_c(k, pid).wait_recv()
                sources = [own[k].at[pid], part[k].at[pid]]
                child = place.has_down if above else place.has_up

                @pl.when(child)
                def _():
                    add_up(own[k].at[pid], sources + [late_child(k, rel_p, rel_q, z0)], rows[k])

                @pl.when(jnp.logical_not(child))
                def _():
                    add_up(own[k].at[pid], sources, rows[k])

                send_late(k, rel_p, rel_q, z0, above).start()

    def late_here(k, rel_p, rel_q, target, extra):
        pid = place.piece(routes[k], rel_p, rel_q, place.z)
        send_c(k, pid).wait_recv()
        target = own[k].at[pid] if target is None else target
        add_up(target, [own[k].at[pid], part[k].at[pid]] + extra, rows[k])
        add_children(k, rel_p, rel_q, target)

    def wait_z(k, index):
        pltpu.make_async_copy(land_z[k].at[index], land_z[k].at[index], z_recv.at[k, index]).wait()

    def first(s, carry):
        def body(z0, above):
            for k in range(count):
                for rel_q in (1, 0):
                    for rel_p in (1, 0) if routes[k][0] is not None else (0,):
                        send_c(k, place.piece(routes[k], rel_p, rel_q, z0)).start()

        both_sides(place, depth - 1 - s, body)
        return carry

    lax.fori_loop(0, depth, first, 0)
    for k in range(total):
        load(k).wait()

    def step(s, carry):
        def leaf(z0, above):
            for k in early:
                for rel_p in (1, 0) if routes[k][0] is not None else (0,):
                    pid = place.piece(routes[k], rel_p, 1, z0)
                    send_c(k, pid).wait_recv()
                    add_up(own[k].at[pid], [own[k].at[pid], part[k].at[pid]], rows[k])
                    send_q(k, rel_p, z0).start()

        def middle(z0, above):
            for k in early:
                if routes[k][0] is not None:
                    pid = place.piece(routes[k], 1, 0, z0)
                    send_c(k, pid).wait_recv()
                    send_q(k, 1, z0).wait_recv()
                    add_up(
                        own[k].at[pid],
                        [own[k].at[pid], part[k].at[pid], land_q[k].at[1, z0]],
                        rows[k],
                    )
                    send_p(k, z0).start()

        def sources_of(k, z0):
            pid = place.piece(routes[k], 0, 0, z0)
            send_c(k, pid).wait_recv()
            send_q(k, 0, z0).wait_recv()
            sources = [own[k].at[pid], part[k].at[pid], land_q[k].at[0, z0]]
            if routes[k][0] is not None:
                send_p(k, z0).wait_recv()
                sources.append(land_p[k].at[z0])
            return pid, sources

        def along(z0, above):
            for k in early:
                pid, sources = sources_of(k, z0)
                child = place.has_down if above else place.has_up

                @pl.when(child)
                def _():
                    wait_z(k, z0)
                    add_up(own[k].at[pid], sources + [land_z[k].at[z0]], rows[k])

                @pl.when(jnp.logical_not(child))
                def _():
                    add_up(own[k].at[pid], sources, rows[k])

                send_z(k, z0, above).start()

        if late:

            @pl.when(s < depth - 1)
            def _():
                both_sides(place, depth - 1 - s, late_along)

            @pl.when(s == depth - 1)
            def _():
                for k in late:
                    for rel_p in (1, 0):
                        late_here(k, rel_p, 1, None, [])
                        send_q(k, rel_p, place.z).start()

            @pl.when(s == depth)
            def _():
                for k in late:
                    send_q(k, 1, place.z).wait_recv()
                    late_here(k, 1, 0, None, [land_q[k].at[1, place.z]])
                    send_p(k, place.z).start()

        both_sides(place, depth - 1 - s, leaf)

        if work.count:

            @pl.when(s < work.count)
            def _():
                work.body(s, place.ctx, *work_ins, *work_outs)

        @pl.when(s < depth + 1)
        def _():
            both_sides(place, depth - s, middle)

        @pl.when(depth + 1 - s >= 1)
        def _():
            both_sides(place, depth + 1 - s, along)

        @pl.when(s == depth + 1)
        def _():
            for k in late:
                send_q(k, 0, place.z).wait_recv()
                send_p(k, place.z).wait_recv()
                extra = [land_q[k].at[0, place.z], land_p[k].at[place.z]]
                late_here(k, 0, 0, sums[k], extra)
            for k in early:
                _, sources = sources_of(k, place.z)
                add_up(sums[k], sources, rows[k])

                @pl.when(place.has_down)
                def _():
                    wait_z(k, place.z)
                    add_up(sums[k], [sums[k], land_z[k].at[place.z]], rows[k])

                @pl.when(place.has_up)
                def _():
                    wait_z(k, depth)
                    add_up(sums[k], [sums[k], land_z[k].at[depth]], rows[k])

        return carry

    lax.fori_loop(0, depth + 2, step, 0)
    for item in range(depth + 2, work.count):
        work.body(item, place.ctx, *work_ins, *work_outs)

    def finish(z0, carry):
        for k in late:
            for rel_p, rel_q in ((1, 1), (0, 1), (1, 0), (0, 0)):

                @pl.when(z0 > place.z)
                def _():
                    send_late(k, rel_p, rel_q, z0, True).wait_send()

                @pl.when(z0 < place.z)
                def _():
                    send_late(k, rel_p, rel_q, z0, False).wait_send()

            @pl.when(z0 == place.z)
            def _():
                send_p(k, z0).wait_send()
                send_q(k, 0, z0).wait_send()
                send_q(k, 1, z0).wait_send()

        for k in early:
            send_q(k, 0, z0).wait_send()
            if routes[k][0] is not None:
                send_q(k, 1, z0).wait_send()
                send_p(k, z0).wait_send()

            @pl.when(z0 > place.z)
            def _():
                send_z(k, z0, True).wait_send()

            @pl.when(z0 < place.z)
            def _():
                send_z(k, z0, False).wait_send()

        return carry

    lax.fori_loop(0, depth, finish, 0)

    def finish_partner(pid, carry):
        for k in range(count):
            send_c(k, pid).wait_send()
        return carry

    lax.fori_loop(0, pieces, finish_partner, 0)


def scatter(arrays, chunks, use_x, collective_id, name, work=Work()):
    depth = lax.axis_size("ctx") // 4
    pieces = (4 if use_x else 2) * depth
    total, count = len(arrays), len(chunks)
    dma = pltpu.SemaphoreType.DMA
    shapes = [a.shape[1:] for a in arrays]
    pairs = [a.reshape(pieces, 2, *s) for a, s in zip(arrays, shapes)]
    bf16 = jnp.bfloat16
    late = [chunk for chunk in chunks if chunk.late]
    return pl.pallas_call(
        functools.partial(scatter_kernel, depth, use_x, chunks, work),
        out_shape=[jax.ShapeDtypeStruct(s, jnp.float32) for s in shapes] + work.shapes,
        in_specs=[pl.BlockSpec(memory_space=pl.ANY)] * total
        + [pl.BlockSpec(memory_space=pltpu.VMEM)] * work.ins,
        out_specs=[pl.BlockSpec(memory_space=pltpu.VMEM)] * (total + work.outs),
        scratch_shapes=[pltpu.VMEM((pieces, *s), bf16) for s in shapes]
        + [pltpu.VMEM((pieces, *s), bf16) for s in shapes]
        + [pltpu.VMEM((2, depth, *s), bf16) for s in shapes]
        + [pltpu.VMEM((depth, *s), bf16) for s in shapes]
        + [pltpu.VMEM((depth + 1, *s), bf16) for s in shapes]
        + [pltpu.VMEM((4, depth + 1, c.rows, *shapes[c.array][1:]), bf16) for c in late]
        + [
            dma((total,)),
            dma((count, pieces)),
            dma((count, pieces)),
            dma((count, 2, depth)),
            dma((count, 2, depth)),
            dma((count, depth)),
            dma((count, depth)),
            dma((count, depth)),
            dma((count, depth + 1)),
            dma((max(1, len(late)), 4, depth)),
            dma((max(1, len(late)), 4, depth + 1)),
        ],
        compiler_params=pltpu.CompilerParams(
            collective_id=collective_id, has_side_effects=True, vmem_limit_bytes=VMEM_LIMIT
        ),
        name=name,
    )(*pairs, *work.arrays)


def padded(rows, multiple=16):
    return -(-rows // multiple) * multiple


def pad_rows(rows, total):
    return jnp.pad(rows, ((0, total - rows.shape[0]), (0, 0)))


XY, YX, ONLY_Y = ("x", "y"), ("y", "x"), (None, "y")
XYZ, YXZ = ("x", "y", "z"), ("y", "x", "z")
def halves(values, split_count):
    return values.reshape(values.shape[0], split_count, values.shape[1] // split_count)


def forward_dot(values, weights):
    split_count = weights.shape[0]
    part = values.shape[1] // split_count
    total = None
    for i in range(split_count):
        term = lax.dot_general(
            values[:, i * part : (i + 1) * part],
            weights[i],
            (((1,), (1,)), ((), ())),
            preferred_element_type=jnp.float32,
        )
        total = term if total is None else total + term
    return total


def backward_dot(grads, weights):
    return jnp.concatenate(
        [
            jnp.dot(grads, weights[i], preferred_element_type=jnp.float32)
            for i in range(weights.shape[0])
        ],
        axis=-1,
    )


def terms_kernel(grads, values, out):
    for i in range(values.shape[0]):
        out[i] = lax.dot_general(
            grads[...], values[i], (((0,), (0,)), ((), ())), preferred_element_type=jnp.float32
        ).astype(out.dtype)


def weight_terms(grads, values, split_count):
    rows, width = grads.shape
    values = jnp.transpose(halves(values, split_count), (1, 0, 2))
    block = next((b for b in (512, 256, 128) if width % b == 0), width)
    part = values.shape[2]
    return pl.pallas_call(
        terms_kernel,
        out_shape=jax.ShapeDtypeStruct((split_count, width, part), jnp.bfloat16),
        grid=(width // block,),
        in_specs=[
            pl.BlockSpec((rows, block), lambda i: (0, i)),
            pl.BlockSpec(values.shape, lambda i: (0, 0, 0)),
        ],
        out_specs=pl.BlockSpec((split_count, block, part), lambda i: (0, i, 0)),
        compiler_params=pltpu.CompilerParams(vmem_limit_bytes=VMEM_LIMIT),
        cost_estimate=pl.CostEstimate(
            flops=2 * rows * width * part * split_count,
            bytes_accessed=2 * width * part * split_count,
            transcendentals=0,
        ),
        name="weight_terms",
    )(grads, values)


PIECES_PER_BLOCK = 4


def block_scores(step, ctx, kv_ref, group, query):
    _, _, block_len, width = kv_ref.shape
    span = pl.ds(step * PIECES_PER_BLOCK, PIECES_PER_BLOCK)
    kv = kv_ref[span, group].reshape(PIECES_PER_BLOCK * block_len, width)
    scores = (
        lax.dot_general(kv, query, (((1,), (1,)), ((), ())), preferred_element_type=jnp.float32)
        * 0.125
    )
    key_pos = step * kv.shape[0] + lax.broadcasted_iota(jnp.int32, scores.shape, 0)
    query_pos = ctx * block_len + lax.rem(
        lax.broadcasted_iota(jnp.int32, scores.shape, 1), block_len
    )
    return kv, scores, key_pos <= query_pos


def attend_body(group, ctx, kv_ref, query_ref, out_ref, logsum_ref):
    query = query_ref[group]
    rows, width = query.shape

    def body(step, carry):
        peak, total, acc = carry
        kv, scores, allowed = block_scores(step, ctx, kv_ref, group, query)
        scores = jnp.where(allowed, scores, -jnp.inf)
        new_peak = jnp.maximum(peak, jnp.max(scores, axis=0, keepdims=True))
        terms = jnp.exp(scores - new_peak)
        shrink = jnp.exp(peak - new_peak)
        total = total * shrink + jnp.sum(terms, axis=0, keepdims=True)
        acc = acc * shrink + lax.dot_general(
            kv,
            terms.astype(jnp.bfloat16),
            (((0,), (0,)), ((), ())),
            preferred_element_type=jnp.float32,
        )
        return new_peak, total, acc

    peak, total, acc = lax.fori_loop(
        0,
        ctx // PIECES_PER_BLOCK + 1,
        body,
        (
            jnp.full((1, rows), -jnp.inf, jnp.float32),
            jnp.zeros((1, rows), jnp.float32),
            jnp.zeros((width, rows), jnp.float32),
        ),
    )
    out_ref[group] = acc / total
    logsum_ref[group] = peak + jnp.log(total)


def retrace_body(group, ctx, kv_ref, query_ref, grad_ref, logsum_ref, delta_ref, dq_ref, dkv_ref):
    query, grad = query_ref[group], grad_ref[group]
    logsum, delta = logsum_ref[group], delta_ref[group]
    blocks, _, block_len, width = kv_ref.shape
    needed = ctx // PIECES_PER_BLOCK + 1

    def body(step, dq):
        kv, scores, allowed = block_scores(step, ctx, kv_ref, group, query)
        probs = jnp.where(allowed, jnp.exp(scores - logsum), 0.0)
        grad_probs = lax.dot_general(
            kv, grad, (((1,), (1,)), ((), ())), preferred_element_type=jnp.float32
        )
        grad_scores = (probs * (grad_probs - delta) * 0.125).astype(jnp.bfloat16)
        dkv = jnp.dot(
            probs.astype(jnp.bfloat16), grad, preferred_element_type=jnp.float32
        ) + jnp.dot(grad_scores, query, preferred_element_type=jnp.float32)
        span = pl.ds(step * PIECES_PER_BLOCK, PIECES_PER_BLOCK)
        dkv_ref[span, group] = dkv.astype(jnp.bfloat16).reshape(PIECES_PER_BLOCK, block_len, width)
        return dq + lax.dot_general(
            grad_scores, kv, (((0,), (0,)), ((), ())), preferred_element_type=jnp.float32
        )

    dq_ref[group] = lax.fori_loop(0, needed, body, jnp.zeros(query.shape, jnp.float32))

    def clear(step, carry):
        span = pl.ds(step * PIECES_PER_BLOCK, PIECES_PER_BLOCK)
        dkv_ref[span, group] = jnp.zeros((PIECES_PER_BLOCK, block_len, width), jnp.bfloat16)
        return carry

    lax.fori_loop(needed, blocks // PIECES_PER_BLOCK, clear, 0)


def one_hot(rows, columns, wide, pad):
    row = lax.broadcasted_iota(jnp.int32, (rows, columns), 0)
    column = lax.broadcasted_iota(jnp.int32, (rows, columns), 1)
    place = column // pad * wide + column % pad
    chosen = (row == place) & (column % pad < wide)
    return jnp.where(chosen, 1.0, 0.0).astype(jnp.bfloat16)


def pieces_kernel(plans, *refs):
    ins, outs = refs[: len(plans)], refs[len(plans) :]
    for (target, start, wide, pad), weight in zip(plans, ins):
        rows, columns = weight.shape
        end = padded(columns)
        lanes = outs[target].shape[1]
        turn = one_hot(end, columns, columns, columns)
        piece = turned(turn, weight[...]).astype(jnp.bfloat16)
        if wide != pad or lanes != rows:
            piece = plain(piece, one_hot(rows, lanes, wide, pad)).astype(jnp.bfloat16)
        outs[target][start : start + end, :] = piece


def make_pieces(weights, plans, shapes):
    vmem = pl.BlockSpec(memory_space=pltpu.VMEM)
    return pl.pallas_call(
        functools.partial(pieces_kernel, plans),
        out_shape=[jax.ShapeDtypeStruct(shape, jnp.bfloat16) for shape in shapes],
        in_specs=[vmem] * len(weights),
        out_specs=[vmem] * len(shapes),
        compiler_params=pltpu.CompilerParams(vmem_limit_bytes=VMEM_LIMIT),
        name="make_pieces",
    )(*weights)


def wait_all(copies):
    for copy in copies:
        copy.wait()


def turned(left, right):
    return lax.dot_general(left, right, (((1,), (1,)), ((), ())), preferred_element_type=jnp.float32)


def plain(left, right):
    return jnp.dot(left, right, preferred_element_type=jnp.float32)


def mlp_kernel(
    real_width,
    attended_ref, resid_ref, grad_ref, gain_ref, out_hbm, gate_hbm, up_hbm, down_hbm,
    output_ref, grad_resid_ref, grad_attended_ref, term_gain_ref,
    terms_out_hbm, terms_gate_hbm, terms_up_hbm, terms_down_hbm,
    out_w, gate_w, up_w, down_w, terms_out, terms_gate, terms_up, terms_down,
    resid2_ref, normal_ref, gate_ref, up_ref, hidden_ref, grad_gate_ref, grad_up_ref, branch_ref,
    load_sem, store_sem,
):
    splits, _, part = gate_w.shape
    span = down_w.shape[2]
    width = out_w.shape[1]
    loads = [
        pltpu.make_async_copy(src, dst, load_sem.at[i])
        for i, (src, dst) in enumerate(
            ((out_hbm, out_w), (gate_hbm, gate_w), (up_hbm, up_w), (down_hbm, down_w))
        )
    ]
    for load in loads:
        load.start()

    def slice_of(i, size=part):
        return slice(i * size, (i + 1) * size)

    loads[0].wait()
    resid2 = resid_ref[...]
    for i in range(splits):
        resid2 = resid2 + turned(attended_ref[:, slice_of(i)], out_w[i])
    scale = lax.rsqrt(jnp.sum(resid2 * resid2, axis=-1, keepdims=True) / real_width + EPSILON)
    resid2_ref[...] = resid2
    normal_ref[...] = (resid2 * scale * gain_ref[...]).astype(jnp.bfloat16)
    loads[1].wait()
    loads[2].wait()
    block = 256 if span % 256 == 0 else 128
    steps = span // block

    def lanes(i, step):
        return pl.ds(pl.multiple_of(i * span + step * block, block), block)

    def forward(index, carry):
        cols = pl.ds(pl.multiple_of(index * block, block), block)
        gate = up = None
        for i in range(splits):
            normal = normal_ref[:, slice_of(i)]
            gate_term = turned(normal, gate_w[i, cols, :])
            up_term = turned(normal, up_w[i, cols, :])
            gate = gate_term if gate is None else gate + gate_term
            up = up_term if up is None else up + up_term
        gate_ref[:, cols] = gate
        up_ref[:, cols] = up
        hidden_ref[:, cols] = (gate * jax.nn.sigmoid(gate) * up).astype(jnp.bfloat16)
        return carry

    lax.fori_loop(0, splits * steps, forward, 0)
    loads[3].wait()
    total = resid2_ref[...]
    for i in range(splits):
        total = total + turned(hidden_ref[:, slice_of(i, span)], down_w[i])
    output_ref[...] = total.astype(jnp.bfloat16)

    for i in range(splits):

        def backward(step, carry):
            inner = pl.ds(pl.multiple_of(step * block, block), block)
            cols = lanes(i, step)
            grad_hidden = plain(grad_ref[...], down_w[i, :, inner])
            gate, up = gate_ref[:, cols], up_ref[:, cols]
            sigma = jax.nn.sigmoid(gate)
            grad_up_ref[:, cols] = (grad_hidden * gate * sigma).astype(jnp.bfloat16)
            grad_gate_ref[:, cols] = (
                grad_hidden * up * sigma * (1.0 + gate * (1.0 - sigma))
            ).astype(jnp.bfloat16)
            return carry

        lax.fori_loop(0, steps, backward, 0)

    def terms(rows, left_ref, right_ref, size, target):
        rows_block = 256 if rows % 256 == 0 else 128

        def body(step, carry):
            cols = pl.ds(pl.multiple_of(step * rows_block, rows_block), rows_block)
            left = left_ref[:, cols]
            for i in range(splits):
                target[i, cols, :] = lax.dot_general(
                    left,
                    right_ref[:, slice_of(i, size)],
                    (((0,), (0,)), ((), ())),
                    preferred_element_type=jnp.float32,
                ).astype(jnp.bfloat16)
            return carry

        lax.fori_loop(0, rows // rows_block, body, 0)

    stores = [
        pltpu.make_async_copy(src, dst, store_sem.at[i])
        for i, (src, dst) in enumerate(
            (
                (terms_down, terms_down_hbm),
                (terms_gate, terms_gate_hbm),
                (terms_up, terms_up_hbm),
                (terms_out, terms_out_hbm),
            )
        )
    ]
    terms(width, grad_ref, hidden_ref, span, terms_down)
    stores[0].start()
    terms(splits * span, grad_gate_ref, normal_ref, part, terms_gate)
    stores[1].start()
    terms(splits * span, grad_up_ref, normal_ref, part, terms_up)
    stores[2].start()

    resid2 = resid2_ref[...]
    scale = lax.rsqrt(jnp.sum(resid2 * resid2, axis=-1, keepdims=True) / real_width + EPSILON)
    pulls, inner_sum = [], 0.0
    for i in range(splits):
        pull = plain(grad_gate_ref[...], gate_w[i]) + plain(grad_up_ref[...], up_w[i])
        resid_part = resid2_ref[:, slice_of(i)]
        term_gain_ref[:, slice_of(i)] = jnp.sum(pull * resid_part * scale, axis=0, keepdims=True)
        pull = pull * gain_ref[:, slice_of(i)]
        inner_sum = inner_sum + jnp.sum(pull * resid_part, axis=-1, keepdims=True)
        pulls.append(pull)
    shift = scale * scale * scale * inner_sum / real_width
    for i in range(splits):
        grad_resid = (
            grad_ref[:, slice_of(i)].astype(jnp.float32)
            + pulls[i] * scale
            - resid2_ref[:, slice_of(i)] * shift
        )
        grad_resid_ref[:, slice_of(i)] = grad_resid
        branch_ref[:, slice_of(i)] = grad_resid.astype(jnp.bfloat16)
    for i in range(splits):
        grad_attended_ref[:, slice_of(i)] = plain(branch_ref[...], out_w[i]).astype(jnp.bfloat16)
    terms(width, branch_ref, attended_ref, part, terms_out)
    stores[3].start()
    wait_all(stores)


def mlp(attended, resid1, grad_rows, gain, out_w, gate_w, up_w, down_w, real_width):
    rows, width = resid1.shape
    hidden_width = gate_w.shape[1]
    f32, bf16 = jnp.float32, jnp.bfloat16
    weights = [out_w, gate_w, up_w, down_w]
    vmem, anywhere = pl.BlockSpec(memory_space=pltpu.VMEM), pl.BlockSpec(memory_space=pl.ANY)
    kept = [pltpu.VMEM(w.shape, bf16) for w in weights]
    return pl.pallas_call(
        functools.partial(mlp_kernel, real_width),
        out_shape=[
            jax.ShapeDtypeStruct((rows, width), bf16),
            jax.ShapeDtypeStruct((rows, width), f32),
            jax.ShapeDtypeStruct(attended.shape, bf16),
            jax.ShapeDtypeStruct((1, width), f32),
        ]
        + [jax.ShapeDtypeStruct(w.shape, bf16) for w in weights],
        in_specs=[vmem] * 4 + [anywhere] * 4,
        out_specs=[vmem] * 4 + [anywhere] * 4,
        scratch_shapes=kept
        + kept
        + [
            pltpu.VMEM((rows, width), f32),
            pltpu.VMEM((rows, width), bf16),
            pltpu.VMEM((rows, hidden_width), f32),
            pltpu.VMEM((rows, hidden_width), f32),
            pltpu.VMEM((rows, hidden_width), bf16),
            pltpu.VMEM((rows, hidden_width), bf16),
            pltpu.VMEM((rows, hidden_width), bf16),
            pltpu.VMEM((rows, width), bf16),
            pltpu.SemaphoreType.DMA((4,)),
            pltpu.SemaphoreType.DMA((4,)),
        ],
        compiler_params=pltpu.CompilerParams(vmem_limit_bytes=VMEM_LIMIT),
        name="mlp",
    )(attended, resid1, grad_rows, gain, *weights)


def local(
    inputs, grad_output, w_query, w_key, w_value, w_out, w_gate, w_up, w_down, gain_attn, gain_mlp
):
    seq_count, block_len, model_width = inputs.shape
    row_count = seq_count * block_len
    split_count = lax.axis_size("fsdp")
    cycle_size = lax.axis_size("ctx")
    cycle_index = lax.axis_index("ctx")
    groups = KV_HEADS
    head_size = HEAD
    repeat_count = HEADS // KV_HEADS
    kv_width = groups * head_size
    positions = cycle_index * block_len + jnp.arange(block_len, dtype=jnp.int32)
    cosine, sine_table = tables(positions, head_size)
    cosine = jnp.tile(cosine, (seq_count, 1))
    sine_table = jnp.tile(sine_table, (seq_count, 1))
    wide_q, wide_k, wide_v = w_query.shape[1], w_key.shape[1], w_value.shape[1]
    wide_o, wide_g = w_out.shape[1], w_gate.shape[1]
    pad_q, pad_k, pad_v = padded(wide_q), padded(wide_k), padded(wide_v)
    pad_o, pad_g = padded(wide_o), padded(wide_g)
    part_width = w_query.shape[0]
    wide_part = part_width // wide_o * pad_o
    gain_size = gain_attn.shape[0]

    def gathered_spread(total, wide, pad):
        pieces = total.T.reshape(-1, pad, total.shape[0])
        return pieces[:, :wide].reshape(-1, total.shape[0])

    def open_up(values, wide, start):
        pieces = values.reshape(values.shape[0], cycle_size, -1)
        return pieces[:, :, start : start + wide].reshape(values.shape[0], cycle_size * wide)

    def close_up(values):
        pieces = values.reshape(row_count, cycle_size, wide_o)
        return jnp.pad(pieces, ((0, 0), (0, 0), (0, pad_o - wide_o))).reshape(row_count, -1)

    gain_row = jnp.concatenate([jnp.pad(g, (0, pad_o - gain_size)) for g in (gain_attn, gain_mlp)])
    gain_piece = jnp.pad(gain_row[None, :], ((0, padded(1) - 1), (0, 0)))
    hidden_part = w_down.shape[0] // wide_g * pad_g
    first_rows = pad_q + pad_k + pad_v
    first_piece, out_piece, gate_piece, up_piece, down_piece = make_pieces(
        [w_query, w_key, w_value, w_out, w_gate, w_up, w_down],
        (
            (0, 0, wide_o, pad_o),
            (0, pad_q, wide_o, pad_o),
            (0, pad_q + pad_k, wide_o, pad_o),
            (1, 0, part_width, wide_part),
            (2, 0, wide_o, pad_o),
            (3, 0, wide_o, pad_o),
            (4, 0, wide_g, pad_g),
        ),
        [
            (first_rows, wide_part),
            (pad_o, wide_part),
            (pad_g, wide_part),
            (pad_g, wide_part),
            (pad_o, hidden_part),
        ],
    )
    first_chunks = cut(0, first_rows, 4, (YX, XY)) + cut(1, padded(1), 1, (XY,))
    first, gains = gather([first_piece, gain_piece], first_chunks, True, 0, "gather_first")
    gain_rows = gains[:cycle_size, 0]
    gain_first = gain_rows[:, :pad_o].reshape(1, -1).astype(jnp.float32)
    gain_second = gain_rows[:, pad_o:].reshape(1, -1).astype(jnp.float32)
    first = first.reshape(split_count, -1, wide_part)

    resid1 = close_up(inputs.reshape(row_count, model_width)).astype(jnp.float32)
    scale1 = lax.rsqrt(jnp.sum(resid1 * resid1, axis=-1, keepdims=True) / model_width + EPSILON)
    normal1 = (resid1 * scale1 * gain_first).astype(jnp.bfloat16)
    raw = forward_dot(normal1, first)
    query_raw = open_up(raw, wide_q, 0).reshape(row_count, HEADS, head_size)
    query_rot = rotate(query_raw, cosine, sine_table).astype(jnp.bfloat16)
    key_raw = open_up(raw, wide_k, pad_q).reshape(row_count, groups, head_size)
    key_rows = rotate(key_raw, cosine, sine_table).astype(jnp.bfloat16)
    value_rows = open_up(raw, wide_v, pad_q + pad_k).astype(jnp.bfloat16)
    value_rows = value_rows.reshape(row_count, groups, head_size)
    pair_rows = jnp.transpose(jnp.concatenate([key_rows, value_rows], axis=-1), (1, 0, 2))
    pair_chunks = cut(0, groups * row_count, 2, (ONLY_Y,))
    (pair_all,) = gather(
        [pair_rows.reshape(groups * row_count, 2 * head_size)],
        pair_chunks,
        False,
        1,
        "gather_pairs",
    )
    pair_all = pair_all.reshape(cycle_size, groups, row_count, 2 * head_size)

    def by_group(values):
        values = values.reshape(row_count, groups, repeat_count, head_size)
        return jnp.transpose(values, (1, 2, 0, 3)).reshape(groups, repeat_count * row_count, head_size)

    query_grouped = jnp.pad(by_group(query_rot), ((0, 0), (0, 0), (0, head_size)))
    width = repeat_count * row_count
    late_rows = padded(pad_g // 8)
    main_rows = pad_g - late_rows
    rest_chunks = (
        cut(0, pad_o, 2, (XYZ, YXZ))
        + [Chunk(1, main_rows, late_rows, XYZ), Chunk(2, main_rows, late_rows, YXZ)]
        + [Chunk(1, 0, main_rows, XY), Chunk(2, 0, main_rows, YX)]
        + cut(3, pad_o, 2, (XY, YX))
    )
    out_w, gate_w, up_w, down_w, attended_turned, logsum = gather(
        [out_piece, gate_piece, up_piece, down_piece],
        rest_chunks,
        True,
        4,
        "gather_rest_attend",
        Work(
            groups,
            attend_body,
            [pair_all, query_grouped],
            [
                jax.ShapeDtypeStruct((groups, 2 * head_size, width), jnp.float32),
                jax.ShapeDtypeStruct((groups, 1, width), jnp.float32),
            ],
        ),
    )
    out_w, gate_w, up_w, down_w = (
        w.reshape(split_count, -1, w.shape[-1]) for w in (out_w, gate_w, up_w, down_w)
    )
    attended_wide = jnp.transpose(
        attended_turned[:, head_size:].reshape(groups, head_size, repeat_count, row_count),
        (3, 0, 2, 1),
    )
    attended = jnp.pad(
        attended_wide.astype(jnp.bfloat16).reshape(row_count, split_count, part_width),
        ((0, 0), (0, 0), (0, wide_part - part_width)),
    ).reshape(row_count, -1)
    grad_rows = close_up(grad_output.reshape(row_count, model_width))
    output, grad_resid2, grad_attended, term_gain2, terms_out, terms_gate, terms_up, terms_down = mlp(
        attended, resid1, grad_rows, gain_second, out_w, gate_w, up_w, down_w, model_width
    )
    grad_attended = grad_attended.reshape(row_count, split_count, wide_part)[..., :part_width]
    grad_attended = grad_attended.reshape(row_count, -1)
    row_delta = jnp.sum(
        grad_attended.astype(jnp.float32).reshape(attended_wide.shape) * attended_wide, axis=-1
    )
    row_delta = jnp.transpose(row_delta, (1, 2, 0)).reshape(groups, 1, width)
    grad_grouped = jnp.pad(by_group(grad_attended), ((0, 0), (0, 0), (head_size, 0)))

    def pieces_of(terms):
        return terms.reshape(split_count * cycle_size, -1, terms.shape[-1])

    sum_out, sum_gate, sum_up, sum_down, grad_query_acc, grad_pair_all = scatter(
        [pieces_of(t) for t in (terms_out, terms_gate, terms_up, terms_down)],
        rest_chunks,
        True,
        3,
        "scatter_rest_retrace",
        Work(
            groups,
            retrace_body,
            [pair_all, query_grouped, grad_grouped, logsum, row_delta],
            [
                jax.ShapeDtypeStruct(query_grouped.shape, jnp.float32),
                jax.ShapeDtypeStruct(pair_all.shape, jnp.bfloat16),
            ],
        ),
    )
    (grad_pair_own,) = scatter(
        [grad_pair_all.reshape(cycle_size, groups * row_count, 2 * head_size)],
        pair_chunks,
        False,
        2,
        "scatter_pairs",
    )
    grad_pair_own = jnp.transpose(
        grad_pair_own.reshape(groups, row_count, 2 * head_size), (1, 0, 2)
    )
    grad_query_rows = jnp.transpose(
        grad_query_acc[..., :head_size].reshape(groups, repeat_count, row_count, head_size),
        (2, 0, 1, 3),
    ).reshape(row_count, HEADS, head_size)
    grad_query = (
        unrotate(grad_query_rows, cosine, sine_table)
        .reshape(row_count, HEADS * head_size)
        .astype(jnp.bfloat16)
    )
    grad_keys = (
        unrotate(grad_pair_own[..., :head_size], cosine, sine_table)
        .reshape(row_count, kv_width)
        .astype(jnp.bfloat16)
    )
    grad_values = grad_pair_own[..., head_size:].astype(jnp.bfloat16).reshape(row_count, kv_width)

    def shaped(values, wide, pad):
        pieces = values.reshape(row_count, cycle_size, wide)
        return jnp.pad(pieces, ((0, 0), (0, 0), (0, pad - wide)))

    grad_raw = jnp.concatenate(
        [
            shaped(grad_query, wide_q, pad_q),
            shaped(grad_keys, wide_k, pad_k),
            shaped(grad_values, wide_v, pad_v),
        ],
        axis=-1,
    ).reshape(row_count, -1)
    grad_norm1 = backward_dot(grad_raw, first)
    term_gain1 = jnp.sum(grad_norm1 * resid1 * scale1, axis=0)
    pull = grad_norm1 * gain_first
    shift = scale1**3 * jnp.sum(pull * resid1, axis=-1, keepdims=True) / model_width
    grad_input = (grad_resid2 + pull * scale1 - resid1 * shift).astype(jnp.bfloat16)
    gain_terms = jnp.concatenate(
        [term_gain1.reshape(cycle_size, pad_o), term_gain2.reshape(cycle_size, pad_o)], axis=-1
    ).astype(jnp.bfloat16)
    terms_first = weight_terms(grad_raw, normal1, split_count)
    gain_terms = jnp.pad(gain_terms[:, None, :], ((0, 0), (0, padded(1) - 1), (0, 0)))
    gain_terms = jnp.tile(gain_terms, (split_count, 1, 1))
    sum_first, gain_sums = scatter(
        [pieces_of(terms_first), gain_terms], first_chunks, True, 5, "scatter_first"
    )
    gain_sums = gain_sums[0]
    start_k, start_v = pad_q, pad_q + pad_k

    def model_sum(total):
        return gathered_spread(total, wide_o, pad_o)

    def rows_of(values):
        return open_up(values, wide_o, 0).reshape(seq_count, block_len, model_width)

    return (
        rows_of(output),
        rows_of(grad_input),
        model_sum(sum_first[:wide_q]),
        model_sum(sum_first[start_k : start_k + wide_k]),
        model_sum(sum_first[start_v : start_v + wide_v]),
        sum_out[:wide_o, :part_width].T,
        model_sum(sum_gate[:wide_g]),
        model_sum(sum_up[:wide_g]),
        gathered_spread(sum_down[:wide_o], wide_g, pad_g),
        gain_sums[:gain_size],
        gain_sums[pad_o : pad_o + gain_size],
    )


def solution(mesh):
    rows, weight, gain = P("fsdp", "ctx", None), P("fsdp", "ctx"), P("ctx")
    return jax.shard_map(
        local,
        mesh=mesh,
        in_specs=(rows, rows) + (weight,) * 7 + (gain, gain),
        out_specs=(rows, rows) + (weight,) * 7 + (gain, gain),
        check_vma=False,
    )
```

```python
import functools

import jax
import jax.numpy as jnp
from jax import lax
from jax.experimental import pallas as pl
from jax.experimental.pallas import tpu as pltpu
from jax.sharding import PartitionSpec as P

HEADS = 15
KV_HEADS = 5
HEAD = 64

EPSILON = 1e-05
ROPE_THETA = 100000.0
MESH = pl.DeviceIdType.MESH
VMEM_LIMIT = 67_000_000


def tables(positions, head_size):
    half_size = head_size // 2
    frequency = ROPE_THETA ** (-jnp.arange(half_size, dtype=jnp.float32) * 2.0 / head_size)
    angles = positions.astype(jnp.float32)[:, None] * frequency[None, :]
    return (jnp.cos(angles), jnp.sin(angles))


def rotate(values, cosine, sine_table):
    half_size = values.shape[-1] // 2
    first_half = values[..., :half_size]
    second = values[..., half_size:]
    cosine = cosine[:, None, :]
    sine_table = sine_table[:, None, :]
    return jnp.concatenate(
        [first_half * cosine - second * sine_table, second * cosine + first_half * sine_table],
        axis=-1,
    )


def unrotate(values, cosine, sine_table):
    return rotate(values, cosine, -sine_table)


class Place:
    def __init__(self, depth, use_x):
        self.depth = depth
        self.use_x = use_x
        self.f = lax.axis_index("fsdp")
        self.ctx = lax.axis_index("ctx")
        self.c = self.ctx % 2
        self.y = (self.ctx // 2) % 2
        self.z = self.ctx // 4
        self.has_up = self.z < depth - 1
        self.has_down = self.z > 0

    def device(self, way):
        if way == "c":
            return (self.f, self.ctx + 1 - 2 * self.c)
        if way == "y":
            return (self.f, self.ctx + 2 - 4 * self.y)
        if way == "x":
            return (1 - self.f, self.ctx)
        return (self.f, self.ctx + (4 if way == "up" else -4))

    def piece(self, route, rel_p, rel_q, z):
        rel = {route[1]: rel_q}
        if route[0] is not None:
            rel[route[0]] = rel_p
        y0 = 1 - self.y if rel.get("y", 0) else self.y
        pid = z * 2 + y0
        if self.use_x:
            x0 = 1 - self.f if rel.get("x", 0) else self.f
            pid = pid + x0 * 2 * self.depth
        return pid

    def barrier(self):
        sem = pltpu.get_barrier_semaphore()
        ways = ["c", "y"] + (["x"] if self.use_x else [])
        for way in ways:
            pl.semaphore_signal(sem, inc=1, device_id=self.device(way), device_id_type=MESH)

        @pl.when(self.has_up)
        def _():
            pl.semaphore_signal(sem, inc=1, device_id=self.device("up"), device_id_type=MESH)

        @pl.when(self.has_down)
        def _():
            pl.semaphore_signal(sem, inc=1, device_id=self.device("down"), device_id_type=MESH)

        peers = len(ways) + self.has_up.astype(jnp.int32) + self.has_down.astype(jnp.int32)
        pl.semaphore_wait(sem, peers)


def both_sides(place, distance, body):
    high = place.z + distance
    low = place.z - distance

    @pl.when((distance >= 0) & (high < place.depth))
    def _():
        body(high, True)

    @pl.when((distance >= 1) & (low >= 0))
    def _():
        body(low, False)


class Chunk:
    def __init__(self, array, start, rows, route):
        self.array, self.start, self.rows, self.route = array, start, rows, route
        self.span = pl.ds(start, rows)


def cut(array, rows, parts, routes):
    size = padded(-(-rows // parts))
    starts = range(0, rows, size)
    return [
        Chunk(array, start, min(size, rows - start), routes[i % len(routes)])
        for i, start in enumerate(starts)
    ]


def gather_kernel(depth, use_x, chunks, work, *refs):
    total, count = chunks[-1].array + 1, len(chunks)
    routes = [chunk.route for chunk in chunks]
    ins, work_ins, refs = refs[:total], refs[total : total + work.ins], refs[total + work.ins :]
    outs, work_outs, refs = refs[:total], refs[total : total + work.outs], refs[total + work.outs :]
    recv, send_z, send_p, send_q, send_c, local_sem = refs
    place = Place(depth, use_x)
    place.barrier()

    def landing(k, slot):
        return outs[chunks[k].array].at[slot, chunks[k].span]

    def copy(k, pid, send_sem, way, src=None):
        slot = pid * 2 + place.c
        return pltpu.make_async_remote_copy(
            src_ref=landing(k, slot) if src is None else src,
            dst_ref=landing(k, slot),
            send_sem=send_sem,
            recv_sem=recv.at[k, slot],
            device_id=place.device(way),
            device_id_type=MESH,
        )

    def forward_z(k, z0, up, src=None):
        pid = place.piece(routes[k], 0, 0, z0)
        return copy(k, pid, send_z.at[k, 0 if up else 1, z0], "up" if up else "down", src)

    def forward_p(k, z0, src=None):
        return copy(k, place.piece(routes[k], 0, 0, z0), send_p.at[k, z0], routes[k][0], src)

    def forward_q(k, rel_p, z0, src=None):
        pid = place.piece(routes[k], rel_p, 0, z0)
        return copy(k, pid, send_q.at[k, rel_p, z0], routes[k][1], src)

    def forward_c(k, pid, src=None):
        return copy(k, pid, send_c.at[k, pid], "c", src)

    def arrived(k, pid):
        copy(k, pid, send_c.at[k, pid], "c").wait_recv()

    own = []
    for k in range(count):
        pid = place.piece(routes[k], 0, 0, place.z)
        src = ins[chunks[k].array].at[chunks[k].span]

        @pl.when(place.has_up)
        def _():
            forward_z(k, place.z, True, src).start()

        @pl.when(place.has_down)
        def _():
            forward_z(k, place.z, False, src).start()

        if routes[k][0] is not None:
            forward_p(k, place.z, src).start()
        forward_q(k, 0, place.z, src).start()
        forward_c(k, pid, src).start()
        mine = pltpu.make_async_copy(src, landing(k, pid * 2 + place.c), local_sem.at[k])
        mine.start()
        own.append(mine)

    def step(d, carry):
        def from_z(z0, above):
            for k in range(count):
                pid = place.piece(routes[k], 0, 0, z0)
                arrived(k, pid)
                if above:

                    @pl.when(place.has_down)
                    def _():
                        forward_z(k, z0, False).start()

                else:

                    @pl.when(place.has_up)
                    def _():
                        forward_z(k, z0, True).start()

                if routes[k][0] is not None:
                    forward_p(k, z0).start()
                forward_q(k, 0, z0).start()
                forward_c(k, pid).start()

        def from_p(z0, above):
            for k in range(count):
                if routes[k][0] is not None:
                    pid = place.piece(routes[k], 1, 0, z0)
                    arrived(k, pid)
                    forward_q(k, 1, z0).start()
                    forward_c(k, pid).start()

        def from_q(rel_p, z0, above):
            for k in range(count):
                if routes[k][0] is not None or not rel_p:
                    pid = place.piece(routes[k], rel_p, 1, z0)
                    arrived(k, pid)
                    forward_c(k, pid).start()

        @pl.when((d >= 1) & (d < depth))
        def _():
            both_sides(place, d, from_z)

        both_sides(place, d - 1, from_p)
        both_sides(place, d - 1, functools.partial(from_q, 0))
        both_sides(place, d - 2, functools.partial(from_q, 1))

        if work.count:

            @pl.when(d - 1 < work.count)
            def _():
                work.body(d - 1, place.ctx, *work_ins, *work_outs)

        return carry

    lax.fori_loop(1, depth + 2, step, 0)
    for item in range(depth + 1, work.count):
        work.body(item, place.ctx, *work_ins, *work_outs)

    def finish(z0, carry):
        for k in range(count):

            @pl.when(place.has_up & (z0 <= place.z))
            def _():
                forward_z(k, z0, True).wait_send()

            @pl.when(place.has_down & (z0 >= place.z))
            def _():
                forward_z(k, z0, False).wait_send()

            if routes[k][0] is not None:
                forward_p(k, z0).wait_send()
                forward_q(k, 1, z0).wait_send()
            forward_q(k, 0, z0).wait_send()
        return carry

    lax.fori_loop(0, depth, finish, 0)

    def finish_partner(pid, carry):
        for k in range(count):
            forward_c(k, pid).wait_send()
            slot = pid * 2 + 1 - place.c
            pltpu.make_async_remote_copy(
                src_ref=landing(k, slot),
                dst_ref=landing(k, slot),
                send_sem=send_c.at[k, pid],
                recv_sem=recv.at[k, slot],
                device_id=place.device("c"),
                device_id_type=MESH,
            ).wait_recv()
        return carry

    lax.fori_loop(0, (4 if use_x else 2) * depth, finish_partner, 0)
    for mine in own:
        mine.wait()


class Work:
    def __init__(self, count=0, body=None, arrays=(), shapes=()):
        self.count, self.body, self.arrays, self.shapes = count, body, arrays, list(shapes)
        self.ins, self.outs = len(arrays), len(self.shapes)


def gather(arrays, chunks, use_x, collective_id, name, work=Work()):
    depth = lax.axis_size("ctx") // 4
    pieces = (4 if use_x else 2) * depth
    total, count = len(arrays), len(chunks)
    dma = pltpu.SemaphoreType.DMA
    return pl.pallas_call(
        functools.partial(gather_kernel, depth, use_x, chunks, work),
        out_shape=[jax.ShapeDtypeStruct((2 * pieces, *a.shape), a.dtype) for a in arrays]
        + work.shapes,
        in_specs=[pl.BlockSpec(memory_space=pltpu.VMEM)] * (total + work.ins),
        out_specs=[pl.BlockSpec(memory_space=pl.ANY)] * total
        + [pl.BlockSpec(memory_space=pltpu.VMEM)] * work.outs,
        scratch_shapes=[
            dma((count, 2 * pieces)),
            dma((count, 2, depth)),
            dma((count, depth)),
            dma((count, 2, depth)),
            dma((count, pieces)),
            dma((count,)),
        ],
        compiler_params=pltpu.CompilerParams(
            collective_id=collective_id, has_side_effects=True, vmem_limit_bytes=VMEM_LIMIT
        ),
        name=name,
    )(*arrays, *work.arrays)


def add_up(dst, sources, rows):
    block = max(b for b in range(16, 81, 16) if rows % b == 0)

    def body(i, carry):
        span = pl.ds(pl.multiple_of(i * block, block), block)
        total = sources[0][span, :].astype(jnp.float32)
        for source in sources[1:]:
            total = total + source[span, :].astype(jnp.float32)
        dst[span, :] = total.astype(dst.dtype)
        return carry

    lax.fori_loop(0, rows // block, body, 0)


def scatter_kernel(depth, use_x, chunks, work, *refs):
    total, count = chunks[-1].array + 1, len(chunks)
    routes = [chunk.route for chunk in chunks]
    ins, work_ins, refs = refs[:total], refs[total : total + work.ins], refs[total + work.ins :]
    outs, work_outs, refs = refs[:total], refs[total : total + work.outs], refs[total + work.outs :]
    whole = [refs[i * total : (1 + i) * total] for i in range(5)]
    load_sem, c_send, c_recv, q_send, q_recv, p_send, p_recv, z_send, z_recv = refs[5 * total :]

    class View:
        def __init__(self, ref, span):
            self.ref, self.span = ref, span

        @property
        def at(self):
            return self

        def __getitem__(self, index):
            index = index if isinstance(index, tuple) else (index,)
            return self.ref.at[(*index, self.span)]

    own, part, land_q, land_p, land_z = (
        [View(group[chunk.array], chunk.span) for chunk in chunks] for group in whole
    )
    sums = [outs[chunk.array].at[chunk.span] for chunk in chunks]
    place = Place(depth, use_x)
    pieces = (4 if use_x else 2) * depth
    rows = [chunk.rows for chunk in chunks]

    def load(k):
        return pltpu.make_async_copy(ins[k].at[:, place.c], whole[0][k], load_sem.at[k])

    for k in range(total):
        load(k).start()
    place.barrier()

    def remote(src, dst, send_sem, recv_sem, way):
        return pltpu.make_async_remote_copy(
            src_ref=src,
            dst_ref=dst,
            send_sem=send_sem,
            recv_sem=recv_sem,
            device_id=place.device(way),
            device_id_type=MESH,
        )

    def send_c(k, pid):
        return remote(
            ins[chunks[k].array].at[pid, 1 - place.c, chunks[k].span], part[k].at[pid], c_send.at[k, pid], c_recv.at[k, pid], "c"
        )

    def send_q(k, rel_p, z0):
        pid = place.piece(routes[k], rel_p, 1, z0)
        return remote(
            own[k].at[pid],
            land_q[k].at[rel_p, z0],
            q_send.at[k, rel_p, z0],
            q_recv.at[k, rel_p, z0],
            routes[k][1],
        )

    def send_p(k, z0):
        pid = place.piece(routes[k], 1, 0, z0)
        return remote(
            own[k].at[pid], land_p[k].at[z0], p_send.at[k, z0], p_recv.at[k, z0], routes[k][0]
        )

    def send_z(k, z0, up):
        pid = place.piece(routes[k], 0, 0, z0)
        if up:
            target = z0
        else:
            target = jnp.where(z0 == place.z - 1, depth, z0)
        return remote(
            own[k].at[pid],
            land_z[k].at[target],
            z_send.at[k, z0],
            z_recv.at[k, target],
            "up" if up else "down",
        )

    def wait_z(k, index):
        pltpu.make_async_copy(land_z[k].at[index], land_z[k].at[index], z_recv.at[k, index]).wait()

    def first(s, carry):
        def body(z0, above):
            for k in range(count):
                for rel_q in (1, 0):
                    for rel_p in (1, 0) if routes[k][0] is not None else (0,):
                        send_c(k, place.piece(routes[k], rel_p, rel_q, z0)).start()

        both_sides(place, depth - 1 - s, body)
        return carry

    lax.fori_loop(0, depth, first, 0)
    for k in range(total):
        load(k).wait()

    def step(s, carry):
        def leaf(z0, above):
            for k in range(count):
                for rel_p in (1, 0) if routes[k][0] is not None else (0,):
                    pid = place.piece(routes[k], rel_p, 1, z0)
                    send_c(k, pid).wait_recv()
                    add_up(own[k].at[pid], [own[k].at[pid], part[k].at[pid]], rows[k])
                    send_q(k, rel_p, z0).start()

        def middle(z0, above):
            for k in range(count):
                if routes[k][0] is not None:
                    pid = place.piece(routes[k], 1, 0, z0)
                    send_c(k, pid).wait_recv()
                    send_q(k, 1, z0).wait_recv()
                    add_up(
                        own[k].at[pid],
                        [own[k].at[pid], part[k].at[pid], land_q[k].at[1, z0]],
                        rows[k],
                    )
                    send_p(k, z0).start()

        def sources_of(k, z0):
            pid = place.piece(routes[k], 0, 0, z0)
            send_c(k, pid).wait_recv()
            send_q(k, 0, z0).wait_recv()
            sources = [own[k].at[pid], part[k].at[pid], land_q[k].at[0, z0]]
            if routes[k][0] is not None:
                send_p(k, z0).wait_recv()
                sources.append(land_p[k].at[z0])
            return pid, sources

        def along(z0, above):
            for k in range(count):
                pid, sources = sources_of(k, z0)
                child = place.has_down if above else place.has_up

                @pl.when(child)
                def _():
                    wait_z(k, z0)
                    add_up(own[k].at[pid], sources + [land_z[k].at[z0]], rows[k])

                @pl.when(jnp.logical_not(child))
                def _():
                    add_up(own[k].at[pid], sources, rows[k])

                send_z(k, z0, above).start()

        both_sides(place, depth - 1 - s, leaf)

        if work.count:

            @pl.when(s < work.count)
            def _():
                work.body(s, place.ctx, *work_ins, *work_outs)

        @pl.when(s < depth + 1)
        def _():
            both_sides(place, depth - s, middle)

        @pl.when(depth + 1 - s >= 1)
        def _():
            both_sides(place, depth + 1 - s, along)

        @pl.when(s == depth + 1)
        def _():
            for k in range(count):
                _, sources = sources_of(k, place.z)
                add_up(sums[k], sources, rows[k])

                @pl.when(place.has_down)
                def _():
                    wait_z(k, place.z)
                    add_up(sums[k], [sums[k], land_z[k].at[place.z]], rows[k])

                @pl.when(place.has_up)
                def _():
                    wait_z(k, depth)
                    add_up(sums[k], [sums[k], land_z[k].at[depth]], rows[k])

        return carry

    lax.fori_loop(0, depth + 2, step, 0)
    for item in range(depth + 2, work.count):
        work.body(item, place.ctx, *work_ins, *work_outs)

    def finish(z0, carry):
        for k in range(count):
            send_q(k, 0, z0).wait_send()
            if routes[k][0] is not None:
                send_q(k, 1, z0).wait_send()
                send_p(k, z0).wait_send()

            @pl.when(z0 > place.z)
            def _():
                send_z(k, z0, True).wait_send()

            @pl.when(z0 < place.z)
            def _():
                send_z(k, z0, False).wait_send()

        return carry

    lax.fori_loop(0, depth, finish, 0)

    def finish_partner(pid, carry):
        for k in range(count):
            send_c(k, pid).wait_send()
        return carry

    lax.fori_loop(0, pieces, finish_partner, 0)


def scatter(arrays, chunks, use_x, collective_id, name, work=Work()):
    depth = lax.axis_size("ctx") // 4
    pieces = (4 if use_x else 2) * depth
    total, count = len(arrays), len(chunks)
    dma = pltpu.SemaphoreType.DMA
    shapes = [a.shape[1:] for a in arrays]
    pairs = [a.reshape(pieces, 2, *s) for a, s in zip(arrays, shapes)]
    bf16 = jnp.bfloat16
    return pl.pallas_call(
        functools.partial(scatter_kernel, depth, use_x, chunks, work),
        out_shape=[jax.ShapeDtypeStruct(s, jnp.float32) for s in shapes] + work.shapes,
        in_specs=[pl.BlockSpec(memory_space=pl.ANY)] * total
        + [pl.BlockSpec(memory_space=pltpu.VMEM)] * work.ins,
        out_specs=[pl.BlockSpec(memory_space=pltpu.VMEM)] * (total + work.outs),
        scratch_shapes=[pltpu.VMEM((pieces, *s), bf16) for s in shapes]
        + [pltpu.VMEM((pieces, *s), bf16) for s in shapes]
        + [pltpu.VMEM((2, depth, *s), bf16) for s in shapes]
        + [pltpu.VMEM((depth, *s), bf16) for s in shapes]
        + [pltpu.VMEM((depth + 1, *s), bf16) for s in shapes]
        + [
            dma((total,)),
            dma((count, pieces)),
            dma((count, pieces)),
            dma((count, 2, depth)),
            dma((count, 2, depth)),
            dma((count, depth)),
            dma((count, depth)),
            dma((count, depth)),
            dma((count, depth + 1)),
        ],
        compiler_params=pltpu.CompilerParams(
            collective_id=collective_id, has_side_effects=True, vmem_limit_bytes=VMEM_LIMIT
        ),
        name=name,
    )(*pairs, *work.arrays)


def padded(rows, multiple=16):
    return -(-rows // multiple) * multiple


def pad_rows(rows, total):
    return jnp.pad(rows, ((0, total - rows.shape[0]), (0, 0)))


XY, YX, ONLY_Y = ("x", "y"), ("y", "x"), (None, "y")
def halves(values, split_count):
    return values.reshape(values.shape[0], split_count, values.shape[1] // split_count)


def forward_dot(values, weights):
    split_count = weights.shape[0]
    part = values.shape[1] // split_count
    total = None
    for i in range(split_count):
        term = lax.dot_general(
            values[:, i * part : (i + 1) * part],
            weights[i],
            (((1,), (1,)), ((), ())),
            preferred_element_type=jnp.float32,
        )
        total = term if total is None else total + term
    return total


def backward_dot(grads, weights):
    return jnp.concatenate(
        [
            jnp.dot(grads, weights[i], preferred_element_type=jnp.float32)
            for i in range(weights.shape[0])
        ],
        axis=-1,
    )


def terms_kernel(grads, values, out):
    for i in range(values.shape[0]):
        out[i] = lax.dot_general(
            grads[...], values[i], (((0,), (0,)), ((), ())), preferred_element_type=jnp.float32
        ).astype(out.dtype)


def weight_terms(grads, values, split_count):
    rows, width = grads.shape
    values = jnp.transpose(halves(values, split_count), (1, 0, 2))
    block = next((b for b in (512, 256, 128) if width % b == 0), width)
    part = values.shape[2]
    return pl.pallas_call(
        terms_kernel,
        out_shape=jax.ShapeDtypeStruct((split_count, width, part), jnp.bfloat16),
        grid=(width // block,),
        in_specs=[
            pl.BlockSpec((rows, block), lambda i: (0, i)),
            pl.BlockSpec(values.shape, lambda i: (0, 0, 0)),
        ],
        out_specs=pl.BlockSpec((split_count, block, part), lambda i: (0, i, 0)),
        compiler_params=pltpu.CompilerParams(vmem_limit_bytes=VMEM_LIMIT),
        cost_estimate=pl.CostEstimate(
            flops=2 * rows * width * part * split_count,
            bytes_accessed=2 * width * part * split_count,
            transcendentals=0,
        ),
        name="weight_terms",
    )(grads, values)


PIECES_PER_BLOCK = 4


def block_scores(step, ctx, kv_ref, group, query):
    _, _, block_len, width = kv_ref.shape
    span = pl.ds(step * PIECES_PER_BLOCK, PIECES_PER_BLOCK)
    kv = kv_ref[span, group].reshape(PIECES_PER_BLOCK * block_len, width)
    scores = (
        lax.dot_general(kv, query, (((1,), (1,)), ((), ())), preferred_element_type=jnp.float32)
        * 0.125
    )
    key_pos = step * kv.shape[0] + lax.broadcasted_iota(jnp.int32, scores.shape, 0)
    query_pos = ctx * block_len + lax.rem(
        lax.broadcasted_iota(jnp.int32, scores.shape, 1), block_len
    )
    return kv, scores, key_pos <= query_pos


def attend_body(group, ctx, kv_ref, query_ref, out_ref, logsum_ref):
    query = query_ref[group]
    rows, width = query.shape

    def body(step, carry):
        peak, total, acc = carry
        kv, scores, allowed = block_scores(step, ctx, kv_ref, group, query)
        scores = jnp.where(allowed, scores, -jnp.inf)
        new_peak = jnp.maximum(peak, jnp.max(scores, axis=0, keepdims=True))
        terms = jnp.exp(scores - new_peak)
        shrink = jnp.exp(peak - new_peak)
        total = total * shrink + jnp.sum(terms, axis=0, keepdims=True)
        acc = acc * shrink + lax.dot_general(
            kv,
            terms.astype(jnp.bfloat16),
            (((0,), (0,)), ((), ())),
            preferred_element_type=jnp.float32,
        )
        return new_peak, total, acc

    peak, total, acc = lax.fori_loop(
        0,
        ctx // PIECES_PER_BLOCK + 1,
        body,
        (
            jnp.full((1, rows), -jnp.inf, jnp.float32),
            jnp.zeros((1, rows), jnp.float32),
            jnp.zeros((width, rows), jnp.float32),
        ),
    )
    out_ref[group] = acc / total
    logsum_ref[group] = peak + jnp.log(total)


def retrace_body(group, ctx, kv_ref, query_ref, grad_ref, logsum_ref, delta_ref, dq_ref, dkv_ref):
    query, grad = query_ref[group], grad_ref[group]
    logsum, delta = logsum_ref[group], delta_ref[group]
    blocks, _, block_len, width = kv_ref.shape
    needed = ctx // PIECES_PER_BLOCK + 1

    def body(step, dq):
        kv, scores, allowed = block_scores(step, ctx, kv_ref, group, query)
        probs = jnp.where(allowed, jnp.exp(scores - logsum), 0.0)
        grad_probs = lax.dot_general(
            kv, grad, (((1,), (1,)), ((), ())), preferred_element_type=jnp.float32
        )
        grad_scores = (probs * (grad_probs - delta) * 0.125).astype(jnp.bfloat16)
        dkv = jnp.dot(
            probs.astype(jnp.bfloat16), grad, preferred_element_type=jnp.float32
        ) + jnp.dot(grad_scores, query, preferred_element_type=jnp.float32)
        span = pl.ds(step * PIECES_PER_BLOCK, PIECES_PER_BLOCK)
        dkv_ref[span, group] = dkv.astype(jnp.bfloat16).reshape(PIECES_PER_BLOCK, block_len, width)
        return dq + lax.dot_general(
            grad_scores, kv, (((0,), (0,)), ((), ())), preferred_element_type=jnp.float32
        )

    dq_ref[group] = lax.fori_loop(0, needed, body, jnp.zeros(query.shape, jnp.float32))

    def clear(step, carry):
        span = pl.ds(step * PIECES_PER_BLOCK, PIECES_PER_BLOCK)
        dkv_ref[span, group] = jnp.zeros((PIECES_PER_BLOCK, block_len, width), jnp.bfloat16)
        return carry

    lax.fori_loop(needed, blocks // PIECES_PER_BLOCK, clear, 0)


def one_hot(rows, columns, wide, pad):
    row = lax.broadcasted_iota(jnp.int32, (rows, columns), 0)
    column = lax.broadcasted_iota(jnp.int32, (rows, columns), 1)
    place = column // pad * wide + column % pad
    chosen = (row == place) & (column % pad < wide)
    return jnp.where(chosen, 1.0, 0.0).astype(jnp.bfloat16)


def eye(rows, columns):
    row = lax.broadcasted_iota(jnp.int32, (rows, columns), 0)
    column = lax.broadcasted_iota(jnp.int32, (rows, columns), 1)
    return jnp.where(row == column, 1.0, 0.0).astype(jnp.bfloat16)


def pieces_kernel(plans, *refs):
    ins, outs = refs[: len(plans)], refs[len(plans) :]
    for (target, start, end, wide, pad), weight in zip(plans, ins):
        columns, rows = weight.shape
        lanes = outs[target].shape[1]
        piece = weight[...]
        if end != columns:
            piece = plain(eye(end, columns), piece).astype(jnp.bfloat16)
        if wide != pad or lanes != rows:
            piece = plain(piece, one_hot(rows, lanes, wide, pad)).astype(jnp.bfloat16)
        outs[target][start : start + end, :] = piece


def make_pieces(weights, plans, shapes):
    vmem = pl.BlockSpec(memory_space=pltpu.VMEM)
    return pl.pallas_call(
        functools.partial(pieces_kernel, plans),
        out_shape=[jax.ShapeDtypeStruct(shape, jnp.bfloat16) for shape in shapes],
        in_specs=[vmem] * len(weights),
        out_specs=[vmem] * len(shapes),
        compiler_params=pltpu.CompilerParams(vmem_limit_bytes=VMEM_LIMIT),
        name="make_pieces",
    )(*weights)


def wait_all(copies):
    for copy in copies:
        copy.wait()


def turned(left, right):
    return lax.dot_general(left, right, (((1,), (1,)), ((), ())), preferred_element_type=jnp.float32)


def plain(left, right):
    return jnp.dot(left, right, preferred_element_type=jnp.float32)


def mlp_kernel(
    real_width,
    attended_ref, resid_ref, grad_ref, gain_ref, out_hbm, gate_hbm, up_hbm, down_hbm,
    output_ref, grad_resid_ref, grad_attended_ref, term_gain_ref,
    terms_out_hbm, terms_gate_hbm, terms_up_hbm, terms_down_hbm,
    out_w, gate_w, up_w, down_w, terms_out, terms_gate, terms_up, terms_down,
    resid2_ref, normal_ref, gate_ref, up_ref, hidden_ref, grad_gate_ref, grad_up_ref, branch_ref,
    load_sem, store_sem,
):
    splits, _, part = gate_w.shape
    span = down_w.shape[2]
    width = out_w.shape[1]
    loads = [
        pltpu.make_async_copy(src, dst, load_sem.at[i])
        for i, (src, dst) in enumerate(
            ((out_hbm, out_w), (gate_hbm, gate_w), (up_hbm, up_w), (down_hbm, down_w))
        )
    ]
    for load in loads:
        load.start()

    def slice_of(i, size=part):
        return slice(i * size, (i + 1) * size)

    loads[0].wait()
    resid2 = resid_ref[...]
    for i in range(splits):
        resid2 = resid2 + turned(attended_ref[:, slice_of(i)], out_w[i])
    scale = lax.rsqrt(jnp.sum(resid2 * resid2, axis=-1, keepdims=True) / real_width + EPSILON)
    resid2_ref[...] = resid2
    normal_ref[...] = (resid2 * scale * gain_ref[...]).astype(jnp.bfloat16)
    loads[1].wait()
    loads[2].wait()
    block = 256 if span % 256 == 0 else 128
    steps = span // block

    def lanes(i, step):
        return pl.ds(pl.multiple_of(i * span + step * block, block), block)

    def forward(index, carry):
        cols = pl.ds(pl.multiple_of(index * block, block), block)
        gate = up = None
        for i in range(splits):
            normal = normal_ref[:, slice_of(i)]
            gate_term = turned(normal, gate_w[i, cols, :])
            up_term = turned(normal, up_w[i, cols, :])
            gate = gate_term if gate is None else gate + gate_term
            up = up_term if up is None else up + up_term
        gate_ref[:, cols] = gate
        up_ref[:, cols] = up
        hidden_ref[:, cols] = (gate * jax.nn.sigmoid(gate) * up).astype(jnp.bfloat16)
        return carry

    lax.fori_loop(0, splits * steps, forward, 0)
    loads[3].wait()
    total = resid2_ref[...]
    for i in range(splits):
        total = total + turned(hidden_ref[:, slice_of(i, span)], down_w[i])
    output_ref[...] = total.astype(jnp.bfloat16)

    for i in range(splits):

        def backward(step, carry):
            inner = pl.ds(pl.multiple_of(step * block, block), block)
            cols = lanes(i, step)
            grad_hidden = plain(grad_ref[...], down_w[i, :, inner])
            gate, up = gate_ref[:, cols], up_ref[:, cols]
            sigma = jax.nn.sigmoid(gate)
            grad_up_ref[:, cols] = (grad_hidden * gate * sigma).astype(jnp.bfloat16)
            grad_gate_ref[:, cols] = (
                grad_hidden * up * sigma * (1.0 + gate * (1.0 - sigma))
            ).astype(jnp.bfloat16)
            return carry

        lax.fori_loop(0, steps, backward, 0)

    def terms(rows, left_ref, right_ref, size, target):
        rows_block = 256 if rows % 256 == 0 else 128

        def body(step, carry):
            cols = pl.ds(pl.multiple_of(step * rows_block, rows_block), rows_block)
            left = left_ref[:, cols]
            for i in range(splits):
                target[i, cols, :] = lax.dot_general(
                    left,
                    right_ref[:, slice_of(i, size)],
                    (((0,), (0,)), ((), ())),
                    preferred_element_type=jnp.float32,
                ).astype(jnp.bfloat16)
            return carry

        lax.fori_loop(0, rows // rows_block, body, 0)

    stores = [
        pltpu.make_async_copy(src, dst, store_sem.at[i])
        for i, (src, dst) in enumerate(
            (
                (terms_down, terms_down_hbm),
                (terms_gate, terms_gate_hbm),
                (terms_up, terms_up_hbm),
                (terms_out, terms_out_hbm),
            )
        )
    ]
    terms(width, grad_ref, hidden_ref, span, terms_down)
    stores[0].start()
    terms(splits * span, grad_gate_ref, normal_ref, part, terms_gate)
    stores[1].start()
    terms(splits * span, grad_up_ref, normal_ref, part, terms_up)
    stores[2].start()

    resid2 = resid2_ref[...]
    scale = lax.rsqrt(jnp.sum(resid2 * resid2, axis=-1, keepdims=True) / real_width + EPSILON)
    pulls, inner_sum = [], 0.0
    for i in range(splits):
        pull = plain(grad_gate_ref[...], gate_w[i]) + plain(grad_up_ref[...], up_w[i])
        resid_part = resid2_ref[:, slice_of(i)]
        term_gain_ref[:, slice_of(i)] = jnp.sum(pull * resid_part * scale, axis=0, keepdims=True)
        pull = pull * gain_ref[:, slice_of(i)]
        inner_sum = inner_sum + jnp.sum(pull * resid_part, axis=-1, keepdims=True)
        pulls.append(pull)
    shift = scale * scale * scale * inner_sum / real_width
    for i in range(splits):
        grad_resid = (
            grad_ref[:, slice_of(i)].astype(jnp.float32)
            + pulls[i] * scale
            - resid2_ref[:, slice_of(i)] * shift
        )
        grad_resid_ref[:, slice_of(i)] = grad_resid
        branch_ref[:, slice_of(i)] = grad_resid.astype(jnp.bfloat16)
    for i in range(splits):
        grad_attended_ref[:, slice_of(i)] = plain(branch_ref[...], out_w[i]).astype(jnp.bfloat16)
    terms(width, branch_ref, attended_ref, part, terms_out)
    stores[3].start()
    wait_all(stores)


def mlp(attended, resid1, grad_rows, gain, out_w, gate_w, up_w, down_w, real_width):
    rows, width = resid1.shape
    hidden_width = gate_w.shape[1]
    f32, bf16 = jnp.float32, jnp.bfloat16
    weights = [out_w, gate_w, up_w, down_w]
    vmem, anywhere = pl.BlockSpec(memory_space=pltpu.VMEM), pl.BlockSpec(memory_space=pl.ANY)
    kept = [pltpu.VMEM(w.shape, bf16) for w in weights]
    return pl.pallas_call(
        functools.partial(mlp_kernel, real_width),
        out_shape=[
            jax.ShapeDtypeStruct((rows, width), bf16),
            jax.ShapeDtypeStruct((rows, width), f32),
            jax.ShapeDtypeStruct(attended.shape, bf16),
            jax.ShapeDtypeStruct((1, width), f32),
        ]
        + [jax.ShapeDtypeStruct(w.shape, bf16) for w in weights],
        in_specs=[vmem] * 4 + [anywhere] * 4,
        out_specs=[vmem] * 4 + [anywhere] * 4,
        scratch_shapes=kept
        + kept
        + [
            pltpu.VMEM((rows, width), f32),
            pltpu.VMEM((rows, width), bf16),
            pltpu.VMEM((rows, hidden_width), f32),
            pltpu.VMEM((rows, hidden_width), f32),
            pltpu.VMEM((rows, hidden_width), bf16),
            pltpu.VMEM((rows, hidden_width), bf16),
            pltpu.VMEM((rows, hidden_width), bf16),
            pltpu.VMEM((rows, width), bf16),
            pltpu.SemaphoreType.DMA((4,)),
            pltpu.SemaphoreType.DMA((4,)),
        ],
        compiler_params=pltpu.CompilerParams(vmem_limit_bytes=VMEM_LIMIT),
        name="mlp",
    )(attended, resid1, grad_rows, gain, *weights)


def local(
    inputs, grad_output, w_query, w_key, w_value, w_out, w_gate, w_up, w_down, gain_attn, gain_mlp
):
    seq_count, block_len, model_width = inputs.shape
    row_count = seq_count * block_len
    split_count = lax.axis_size("fsdp")
    cycle_size = lax.axis_size("ctx")
    cycle_index = lax.axis_index("ctx")
    groups = KV_HEADS
    head_size = HEAD
    repeat_count = HEADS // KV_HEADS
    kv_width = groups * head_size
    positions = cycle_index * block_len + jnp.arange(block_len, dtype=jnp.int32)
    cosine, sine_table = tables(positions, head_size)
    cosine = jnp.tile(cosine, (seq_count, 1))
    sine_table = jnp.tile(sine_table, (seq_count, 1))
    wide_q, wide_k, wide_v = w_query.shape[1], w_key.shape[1], w_value.shape[1]
    wide_o, wide_g = w_out.shape[1], w_gate.shape[1]
    pad_q, pad_k, pad_v = padded(wide_q), padded(wide_k + 1), padded(wide_v)
    pad_o, pad_g = padded(wide_o), padded(wide_g)
    part_width = w_query.shape[0]
    wide_part = part_width // wide_o * pad_o
    gain_size = gain_attn.shape[0]

    def gathered_spread(total, wide, pad):
        pieces = total.T.reshape(-1, pad, total.shape[0])
        return pieces[:, :wide].reshape(-1, total.shape[0])

    def open_up(values, wide, start):
        pieces = values.reshape(values.shape[0], cycle_size, -1)
        return pieces[:, :, start : start + wide].reshape(values.shape[0], cycle_size * wide)

    def close_up(values):
        pieces = values.reshape(row_count, cycle_size, wide_o)
        return jnp.pad(pieces, ((0, 0), (0, 0), (0, pad_o - wide_o))).reshape(row_count, -1)

    gain_row = jnp.concatenate([gain_attn, gain_mlp])
    gain_row = jnp.pad(gain_row, (0, part_width - 2 * gain_size))[None, :]
    hidden_part = w_down.shape[0] // wide_g * pad_g
    first_rows = pad_q + pad_k + pad_v
    first_piece, out_piece, gate_piece, up_piece, down_piece = make_pieces(
        [
            w_query.T,
            jnp.concatenate([w_key.T, gain_row], axis=0),
            w_value.T,
            w_out.T,
            w_gate.T,
            w_up.T,
            w_down.T,
        ],
        (
            (0, 0, pad_q, wide_o, pad_o),
            (0, pad_q, pad_k, wide_o, pad_o),
            (0, pad_q + pad_k, pad_v, wide_o, pad_o),
            (1, 0, pad_o, part_width, wide_part),
            (2, 0, pad_g, wide_o, pad_o),
            (3, 0, pad_g, wide_o, pad_o),
            (4, 0, pad_o, wide_g, pad_g),
        ),
        [
            (first_rows, wide_part),
            (pad_o, wide_part),
            (pad_g, wide_part),
            (pad_g, wide_part),
            (pad_o, hidden_part),
        ],
    )
    first_chunks = cut(0, first_rows, 4, (YX, XY))
    (first,) = gather([first_piece], first_chunks, True, 0, "gather_first")
    gain_rows = first[:cycle_size, pad_q + wide_k, : 2 * pad_o]
    gain_first = gain_rows[:, :pad_o].reshape(1, -1).astype(jnp.float32)
    gain_second = gain_rows[:, pad_o:].reshape(1, -1).astype(jnp.float32)
    first = first.reshape(split_count, -1, wide_part)

    resid1 = close_up(inputs.reshape(row_count, model_width)).astype(jnp.float32)
    scale1 = lax.rsqrt(jnp.sum(resid1 * resid1, axis=-1, keepdims=True) / model_width + EPSILON)
    normal1 = (resid1 * scale1 * gain_first).astype(jnp.bfloat16)
    raw = forward_dot(normal1, first)
    query_raw = open_up(raw, wide_q, 0).reshape(row_count, HEADS, head_size)
    query_rot = rotate(query_raw, cosine, sine_table).astype(jnp.bfloat16)
    key_raw = open_up(raw, wide_k, pad_q).reshape(row_count, groups, head_size)
    key_rows = rotate(key_raw, cosine, sine_table).astype(jnp.bfloat16)
    value_rows = open_up(raw, wide_v, pad_q + pad_k).astype(jnp.bfloat16)
    value_rows = value_rows.reshape(row_count, groups, head_size)
    pair_rows = jnp.transpose(jnp.concatenate([key_rows, value_rows], axis=-1), (1, 0, 2))
    pair_chunks = cut(0, groups * row_count, 2, (ONLY_Y,))
    (pair_all,) = gather(
        [pair_rows.reshape(groups * row_count, 2 * head_size)],
        pair_chunks,
        False,
        1,
        "gather_pairs",
    )
    pair_all = pair_all.reshape(cycle_size, groups, row_count, 2 * head_size)

    def by_group(values):
        values = values.reshape(row_count, groups, repeat_count, head_size)
        return jnp.transpose(values, (1, 2, 0, 3)).reshape(groups, repeat_count * row_count, head_size)

    query_grouped = jnp.pad(by_group(query_rot), ((0, 0), (0, 0), (0, head_size)))
    width = repeat_count * row_count
    rest_chunks = (
        cut(0, pad_o, 2, (XY, YX))
        + cut(1, pad_g, 1, (XY,))
        + cut(2, pad_g, 1, (YX,))
        + cut(3, pad_o, 2, (XY, YX))
    )
    out_w, gate_w, up_w, down_w, attended_turned, logsum = gather(
        [out_piece, gate_piece, up_piece, down_piece],
        rest_chunks,
        True,
        4,
        "gather_rest_attend",
        Work(
            groups,
            attend_body,
            [pair_all, query_grouped],
            [
                jax.ShapeDtypeStruct((groups, 2 * head_size, width), jnp.float32),
                jax.ShapeDtypeStruct((groups, 1, width), jnp.float32),
            ],
        ),
    )
    out_w, gate_w, up_w, down_w = (
        w.reshape(split_count, -1, w.shape[-1]) for w in (out_w, gate_w, up_w, down_w)
    )
    attended_wide = jnp.transpose(
        attended_turned[:, head_size:].reshape(groups, head_size, repeat_count, row_count),
        (3, 0, 2, 1),
    )
    attended = jnp.pad(
        attended_wide.astype(jnp.bfloat16).reshape(row_count, split_count, part_width),
        ((0, 0), (0, 0), (0, wide_part - part_width)),
    ).reshape(row_count, -1)
    grad_rows = close_up(grad_output.reshape(row_count, model_width))
    output, grad_resid2, grad_attended, term_gain2, terms_out, terms_gate, terms_up, terms_down = mlp(
        attended, resid1, grad_rows, gain_second, out_w, gate_w, up_w, down_w, model_width
    )
    grad_attended = grad_attended.reshape(row_count, split_count, wide_part)[..., :part_width]
    grad_attended = grad_attended.reshape(row_count, -1)
    row_delta = jnp.sum(
        grad_attended.astype(jnp.float32).reshape(attended_wide.shape) * attended_wide, axis=-1
    )
    row_delta = jnp.transpose(row_delta, (1, 2, 0)).reshape(groups, 1, width)
    grad_grouped = jnp.pad(by_group(grad_attended), ((0, 0), (0, 0), (head_size, 0)))

    def pieces_of(terms):
        return terms.reshape(split_count * cycle_size, -1, terms.shape[-1])

    sum_out, sum_gate, sum_up, sum_down, grad_query_acc, grad_pair_all = scatter(
        [pieces_of(t) for t in (terms_out, terms_gate, terms_up, terms_down)],
        rest_chunks,
        True,
        3,
        "scatter_rest_retrace",
        Work(
            groups,
            retrace_body,
            [pair_all, query_grouped, grad_grouped, logsum, row_delta],
            [
                jax.ShapeDtypeStruct(query_grouped.shape, jnp.float32),
                jax.ShapeDtypeStruct(pair_all.shape, jnp.bfloat16),
            ],
        ),
    )
    (grad_pair_own,) = scatter(
        [grad_pair_all.reshape(cycle_size, groups * row_count, 2 * head_size)],
        pair_chunks,
        False,
        2,
        "scatter_pairs",
    )
    grad_pair_own = jnp.transpose(
        grad_pair_own.reshape(groups, row_count, 2 * head_size), (1, 0, 2)
    )
    grad_query_rows = jnp.transpose(
        grad_query_acc[..., :head_size].reshape(groups, repeat_count, row_count, head_size),
        (2, 0, 1, 3),
    ).reshape(row_count, HEADS, head_size)
    grad_query = (
        unrotate(grad_query_rows, cosine, sine_table)
        .reshape(row_count, HEADS * head_size)
        .astype(jnp.bfloat16)
    )
    grad_keys = (
        unrotate(grad_pair_own[..., :head_size], cosine, sine_table)
        .reshape(row_count, kv_width)
        .astype(jnp.bfloat16)
    )
    grad_values = grad_pair_own[..., head_size:].astype(jnp.bfloat16).reshape(row_count, kv_width)

    def shaped(values, wide, pad):
        pieces = values.reshape(row_count, cycle_size, wide)
        return jnp.pad(pieces, ((0, 0), (0, 0), (0, pad - wide)))

    grad_raw = jnp.concatenate(
        [
            shaped(grad_query, wide_q, pad_q),
            shaped(grad_keys, wide_k, pad_k),
            shaped(grad_values, wide_v, pad_v),
        ],
        axis=-1,
    ).reshape(row_count, -1)
    grad_norm1 = backward_dot(grad_raw, first)
    term_gain1 = jnp.sum(grad_norm1 * resid1 * scale1, axis=0)
    pull = grad_norm1 * gain_first
    shift = scale1**3 * jnp.sum(pull * resid1, axis=-1, keepdims=True) / model_width
    grad_input = (grad_resid2 + pull * scale1 - resid1 * shift).astype(jnp.bfloat16)
    gain_terms = jnp.concatenate(
        [term_gain1.reshape(cycle_size, pad_o), term_gain2.reshape(cycle_size, pad_o)], axis=-1
    ).astype(jnp.bfloat16)
    terms_first = weight_terms(grad_raw, normal1, split_count)
    terms_first = terms_first.reshape(split_count, cycle_size, -1, wide_part)
    terms_first = terms_first.at[:, :, pad_q + wide_k, : 2 * pad_o].set(gain_terms[None])
    terms_first = terms_first.reshape(split_count * cycle_size, -1, wide_part)
    (sum_first,) = scatter([terms_first], first_chunks, True, 5, "scatter_first")
    start_k, start_v = pad_q, pad_q + pad_k
    gain_sums = sum_first[pad_q + wide_k]

    def model_sum(total):
        return gathered_spread(total, wide_o, pad_o)

    def rows_of(values):
        return open_up(values, wide_o, 0).reshape(seq_count, block_len, model_width)

    return (
        rows_of(output),
        rows_of(grad_input),
        model_sum(sum_first[:wide_q]),
        model_sum(sum_first[start_k : start_k + wide_k]),
        model_sum(sum_first[start_v : start_v + wide_v]),
        sum_out[:wide_o, :part_width].T,
        model_sum(sum_gate[:wide_g]),
        model_sum(sum_up[:wide_g]),
        gathered_spread(sum_down[:wide_o], wide_g, pad_g),
        gain_sums[:gain_size],
        gain_sums[pad_o : pad_o + gain_size],
    )


def solution(mesh):
    rows, weight, gain = P("fsdp", "ctx", None), P("fsdp", "ctx"), P("ctx")
    return jax.shard_map(
        local,
        mesh=mesh,
        in_specs=(rows, rows) + (weight,) * 7 + (gain, gain),
        out_specs=(rows, rows) + (weight,) * 7 + (gain, gain),
        check_vma=False,
    )
```
